32 devices in a mesh: tm: 4 (over y, core), height: 8 (over z, x).
Axes of the slice: x: 2, y: 2, z: 4, core: 2. Of those that a mesh axis runs over, the one named last changes fastest.
Arguments:
- latents: bfloat16 [2, 16, 32, 16, 384], P(None, 'tm', 'height'), may hold values from -6 to 6
- conv_in: bfloat16 [3, 3, 3, 384, 192], replicated, may hold values from -0.0625 to 0.0625
- conv_out: bfloat16 [3, 3, 3, 192, 192], replicated, may hold values from -0.078125 to 0.078125
- shortcut: bfloat16 [384, 192], replicated, may hold values from -0.3125 to 0.3125
- norm_gain: float32 [192], replicated, may hold values from 0.1 to 1.9
- video_rows: int32 [2], replicated, may hold values from 8 to 32, as said below
- video_cols: int32 [2], replicated, may hold values from 4 to 16, as said below
Outputs:
- decoded: bfloat16 [2, 16, 64, 32, 192], P(None, 'tm', 'height')
The draws below stay inside these ranges and needn't reach their ends.
Inputs may be any that keep to these rules, and one draw needn't show every extreme that they name: `video_rows`: some video uses all 32 rows in every draw. `video_cols`: some video uses all 16 columns in every draw.
All inputs are finite; a program needn't handle non-finite values.
Results may differ from the reference program's by a relative error of at most 0.0032.
Values may be sent and summed in bfloat16 or wider, within the bound.
A program may use at most 128 MiB of HBM per device.

```python
import jax
import jax.numpy as jnp
from jax import lax

C_IN = 384
C_OUT = 192
VIDEOS = 2
COLS = 16
FRAMES = 16
ROWS = 32


def forced_most(key, salt, most):
    first, second = jax.random.split(jax.random.fold_in(key, salt))
    values = jax.random.randint(first, (VIDEOS,), most // 4, most + 1)
    picked = jax.random.randint(second, (), 0, VIDEOS)
    return jnp.where(jnp.arange(VIDEOS) == picked, most, values).astype(jnp.int32)


def draw_video_rows(key, part):
    return forced_most(key, 11, ROWS)


def draw_video_cols(key, part):
    return forced_most(key, 23, COLS)


def shard_levels(own_key, shape, shards, least, high):
    loudness, own = 1.0, jax.random.fold_in(own_key, 6)
    for dim, parts in shards:
        steps = jnp.exp(jax.random.uniform(jax.random.fold_in(own, dim), (parts,), jnp.float32, least / len(shards), high / len(shards)))
        loudness = loudness * jnp.repeat(steps, shape[dim] // parts).reshape([-1 if axis == dim else 1 for axis in range(len(shape))])
    return loudness


def scatter_about(own_key, shape, deviation, most, cuts=(), held_as=jnp.bfloat16):
    entries = deviation * jax.random.normal(own_key, shape, jnp.float32)
    if cuts:
        entries = entries * shard_levels(own_key, shape, cuts, -0.22, 0.18)
    return jnp.clip(entries, -most, most).astype(held_as)


def setup_inputs(seed: int = 0) -> dict:
    seeds = jax.random.split(jax.random.key(seed), 8)
    return {
        "latents": scatter_about(seeds[0], (VIDEOS, FRAMES, ROWS, COLS, C_IN), 1.0, 6.0, ((1, 4), (2, 8))),
        "conv_in": scatter_about(seeds[1], (3, 3, 3, C_IN, C_OUT), (27 * C_IN) ** -0.5, 0.0625),
        "conv_out": scatter_about(seeds[2], (3, 3, 3, C_OUT, C_OUT), (27 * C_OUT) ** -0.5, 0.078125),
        "shortcut": scatter_about(seeds[3], (C_IN, C_OUT), C_IN ** -0.5, 0.3125),
        "norm_gain": jnp.clip(1.0 + 0.18 * jax.random.normal(seeds[4], (C_OUT,), jnp.float32), 0.1, 1.9),
        "video_rows": draw_video_rows(jax.random.fold_in(seeds[7], 71), 0),
        "video_cols": draw_video_cols(jax.random.fold_in(seeds[7], 71), 0),
    }


def causal_conv(padded, weight):
    videos, frames_in, rows_in, cols_in, chans = padded.shape
    frames_out = frames_in - 2
    rows_out = rows_in - 2
    cols_out = cols_in - 2
    outputs = weight.shape[-1]
    total = jnp.zeros((videos * frames_out * rows_out * cols_out, outputs), jnp.float32)
    for frame_tap in range(3):
        for row_tap in range(3):
            window = padded[:, frame_tap:frame_tap + frames_out, row_tap:row_tap + rows_out]
            stacked = jnp.concatenate([window[:, :, :, col_tap:col_tap + cols_out] for col_tap in range(3)], axis=-1)
            total = total + jnp.dot(stacked.reshape(-1, 3 * chans), weight[frame_tap, row_tap].reshape(3 * chans, outputs), preferred_element_type=jnp.float32)
    return total.reshape(videos, frames_out, rows_out, cols_out, outputs)

def reference(latents, conv_in, conv_out, shortcut, norm_gain, video_rows, video_cols):

    def one_video(packed):
        frames_all, used_rows, used_cols = packed
        row_ids = jnp.arange(ROWS, dtype=jnp.int32)
        col_ids = jnp.arange(COLS, dtype=jnp.int32)
        keep_in = (row_ids[:, None] < used_rows) & (col_ids[None, :] < used_cols)
        masked = jnp.where(keep_in[None, :, :, None], frames_all, jnp.zeros_like(frames_all))
        upsampled = jnp.repeat(jnp.repeat(masked, 2, axis=1), 2, axis=2)
        padded = jnp.pad(upsampled, ((2, 0), (1, 1), (1, 1), (0, 0)))
        hidden = causal_conv(padded[None], conv_in)[0]
        scale = lax.rsqrt(lax.optimization_barrier(jnp.mean(hidden * hidden, axis=-1, keepdims=True)) + 1e-06)
        normed = hidden * scale * norm_gain
        out_rows = jnp.arange(2 * ROWS, dtype=jnp.int32)
        out_cols = jnp.arange(2 * COLS, dtype=jnp.int32)
        keep_out = (out_rows[:, None] < 2 * used_rows) & (out_cols[None, :] < 2 * used_cols)
        gated = jnp.where(keep_out[None, :, :, None], jax.nn.silu(normed), jnp.zeros_like(normed)).astype(jnp.bfloat16)
        gated_pad = jnp.pad(gated, ((2, 0), (1, 1), (1, 1), (0, 0)))
        result = causal_conv(gated_pad[None], conv_out)[0]
        short = jnp.dot(upsampled.reshape(-1, C_IN), shortcut, preferred_element_type=jnp.float32).reshape(result.shape)
        summed = result + short
        return jnp.where(keep_out[None, :, :, None], summed, jnp.zeros_like(summed)).astype(jnp.bfloat16)
    return lax.map(one_video, (latents, video_rows, video_cols))
```

```python
import functools

import jax
import jax.numpy as jnp
from jax import lax
from jax.experimental import pallas as pl
from jax.experimental.pallas import tpu as pltpu
from jax.sharding import PartitionSpec as P

BF = jnp.bfloat16
F32 = jnp.float32
NT = (((1,), (1,)), ((), ()))
PLANES = ((0, 1, 2), (1, 2, 3))


def nt(lhs, rhs):
    return lax.dot_general(lhs, rhs, NT, preferred_element_type=F32)


def section(
    tm,
    height,
    lat,
    w1_hbm,
    w2_hbm,
    ws_hbm,
    gain_hbm,
    rows_hbm,
    cols_hbm,
    out_ref,
    x,
    prev,
    top,
    bot,
    ptop,
    pbot,
    w1,
    w2,
    ws,
    gain_row,
    rows_s,
    cols_s,
    w2t,
    gain_c,
    xm,
    p_own,
    p_prev,
    g_own,
    g_prev,
    g_time,
    short,
    local_sem,
    send_sem,
    recv_sem,
):
    videos, frames, rows, cols, chans = lat.shape
    outs = ws.shape[0]
    taps = 9 * outs
    ext = rows + 2
    lanes = videos * frames * cols
    seg = frames * cols
    ti = lax.axis_index("tm")
    hi = lax.axis_index("height")
    has_up, has_down = hi > 0, hi < height - 1
    has_prev, has_next = ti > 0, ti < tm - 1

    local = [
        pltpu.make_async_copy(src, dst, local_sem.at[k])
        for k, (src, dst) in enumerate(
            (
                (rows_hbm, rows_s),
                (cols_hbm, cols_s),
                (lat, x),
                (gain_hbm, gain_row),
                (w2_hbm, w2),
                (w1_hbm, w1),
                (ws_hbm, ws),
            )
        )
    ]
    for copy in local:
        copy.start()

    def remote(k, src, dst, t, h):
        return pltpu.make_async_remote_copy(
            src_ref=src,
            dst_ref=dst,
            send_sem=send_sem.at[k],
            recv_sem=recv_sem.at[k],
            device_id=(t, h),
            device_id_type=pl.DeviceIdType.MESH,
        )

    half_frames = frames // 2
    sends = (
        (has_next, remote(0, lat.at[:, half_frames:], prev.at[:, half_frames:], ti + 1, hi)),
        (has_down, remote(1, lat.at[:, :, rows - 1], top, ti, hi + 1)),
        (has_up, remote(2, lat.at[:, :, 0], bot, ti, hi - 1)),
        (has_next & has_down, remote(3, lat.at[:, :, rows - 1], ptop, ti + 1, hi + 1)),
        (has_next & has_up, remote(4, lat.at[:, :, 0], pbot, ti + 1, hi - 1)),
        (has_next, remote(5, lat.at[:, :half_frames], prev.at[:, :half_frames], ti + 1, hi)),
    )
    senders = (
        (has_prev, ti - 1, hi),
        (has_up, ti, hi - 1),
        (has_down, ti, hi + 1),
        (has_prev & has_up, ti - 1, hi - 1),
        (has_prev & has_down, ti - 1, hi + 1),
        (has_prev, ti - 1, hi),
    )
    barrier = pltpu.get_barrier_semaphore()
    for there, t, h in senders[:5]:

        @pl.when(there)
        def _():
            pl.semaphore_signal(barrier, inc=1, device_id=(t, h), device_id_type=pl.DeviceIdType.MESH)

    pl.semaphore_wait(barrier, sum(there.astype(jnp.int32) for there, _ in sends[:5]))

    for there, copy in sends:

        @pl.when(there)
        def _():
            copy.start()

    landing = (
        prev.at[:, half_frames:],
        top,
        bot,
        ptop,
        pbot,
        prev.at[:, :half_frames],
    )

    def arrive(k):
        there = senders[k][0]

        @pl.when(there)
        def _():
            sends[k][1].wait_recv()

        @pl.when(jnp.logical_not(there))
        def _():
            landing[k][...] = jnp.zeros(landing[k].shape, BF)

    col_in = lax.broadcasted_iota(jnp.int32, (cols, 1), 0)
    band = hi * rows
    local[0].wait()
    local[1].wait()
    row_limit = [rows_s[v] for v in range(videos)]
    col_limit = [cols_s[v] for v in range(videos)]

    def mask_into(src, at, r, fs, shift):
        for v in range(videos):
            row = band + r - 1
            keep = (col_in < col_limit[v]) & ((row >= 0) & (row < row_limit[v]))
            for f in fs:
                cell = src[v, f] if at is None else src[v, f, at]
                xm[r, v, (f + shift) * cols : (f + shift + 1) * cols] = jnp.where(keep, cell, jnp.zeros_like(cell))

    every = range(frames)
    local[2].wait()
    for r in range(rows):
        mask_into(x, r, r + 1, every, frames)

    local[3].wait()
    gain_c[...] = jnp.broadcast_to(0.5 * gain_row[...], (lanes, outs)).T
    local[4].wait()
    depth = w2.shape[0]
    step = 3 * 128
    for k in range(0, depth, step):
        size = min(step, depth - k)
        w2t[:, k : k + size] = w2[k : k + size].T

    local[5].wait()
    local[6].wait()

    def own_cells(a, r):
        return [xm[r, v, (2 + a) * cols : (2 + a) * cols + seg] for v in range(videos)]

    short[...] = nt(
        ws[...],
        jnp.concatenate([piece for r in range(rows) for piece in own_cells(2, r + 1)], axis=0),
    )

    def conv_in(dst, at, cells):
        rhs = jnp.concatenate([jnp.concatenate(cells(a), axis=0) for a in range(3)], axis=-1)
        third = taps // 3
        for b in range(3):
            lhs = jnp.concatenate([w1[a, b * third : (b + 1) * third] for a in range(3)], axis=-1)
            res = nt(lhs, rhs)
            for n, k in enumerate(at):
                dst[k, b * third : (b + 1) * third] = res[:, n * lanes : (n + 1) * lanes]

    arrive(0)
    for r in range(rows):
        mask_into(prev, r, r + 1, range(half_frames, frames), 0)
    middle = range(1, rows + 1)
    conv_in(p_own, middle, lambda a: [piece for r in middle for piece in own_cells(a, r)])

    arrive(1)
    arrive(2)
    arrive(3)
    arrive(4)
    for src, psrc, r in ((top, ptop, 0), (bot, pbot, ext - 1)):
        mask_into(src, None, r, every, frames)
        mask_into(psrc, None, r, every, 0)
    conv_in(p_own, (0, ext - 1), lambda a: [piece for r in (0, ext - 1) for piece in own_cells(a, r)])

    arrive(5)
    for r in range(rows):
        mask_into(prev, r, r + 1, range(half_frames), 0)
    deep = ext // 2

    def prev_cells(a):
        return [
            xm[half * deep + k, v, a * cols : (a + 2) * cols]
            for k in range(deep)
            for v in range(videos)
            for half in range(2)
        ]

    conv_in(p_prev, range(deep), prev_cells)

    lane = lax.broadcasted_iota(jnp.int32, (1, lanes), 1)
    lane_col = lane % cols
    first_col = lane_col == 0
    last_col = lane_col == cols - 1
    lane_rows, lane_cols = row_limit[0], col_limit[0]
    for v in range(1, videos):
        lane_rows = jnp.where(lane >= v * seg, row_limit[v], lane_rows)
        lane_cols = jnp.where(lane >= v * seg, col_limit[v], lane_cols)
    keep_col = lane_col < lane_cols
    upper = (lane // (seg // 2)) % 2

    def tap(ref, k, b, c):
        at = (b * 3 + c) * outs
        return ref[k, at : at + outs]

    def gate(sums, keep):
        left = jnp.where(first_col, 0.0, pltpu.roll(sums[0], 1, 1))
        right = jnp.where(last_col, 0.0, pltpu.roll(sums[2], lanes - 1, 1))
        planes = []
        for hidden in (left + sums[1] + sums[2], sums[0] + sums[1] + right):
            mean = jnp.sum(hidden * hidden, axis=0, keepdims=True) * (1.0 / outs)
            scale = jnp.where(keep, lax.rsqrt(mean + 1e-06), 0.0)
            normed = hidden * scale * gain_c[...]
            planes.append(normed + normed * jnp.tanh(normed))
        even, odd = planes
        before = jnp.where(first_col, 0.0, pltpu.roll(odd, 1, 1))
        after = jnp.where(last_col, 0.0, pltpu.roll(even, lanes - 1, 1))
        return before, even, odd, after

    for i in range(2 * rows + 2):
        l = (i + 1) // 2
        pick = (l, l, l + 1) if i % 2 == 0 else (l - 1, l, l)
        sums = [sum(tap(p_own, pick[b], b, c) for b in range(3)) for c in range(3)]
        row = band * 2 + i - 1
        keep = keep_col & ((row >= 0) & (row < 2 * lane_rows))
        for at, plane in enumerate(gate(sums, keep)):
            g_own[i, at] = plane.astype(BF)

    quarter = seg // 2
    for k in range(deep):
        for odd_row in range(2):
            sums = []
            for c in range(3):
                own = tap(p_prev, k, 1, c)
                if odd_row:
                    below = tap(p_prev, k + 1, 2, c) if k + 1 < deep else pltpu.roll(tap(p_prev, 0, 2, c), lanes - quarter, 1)
                    sums.append(tap(p_prev, k, 0, c) + own + below)
                else:
                    above = tap(p_prev, k - 1, 0, c) if k else pltpu.roll(tap(p_prev, deep - 1, 0, c), quarter, 1)
                    sums.append(above + own + tap(p_prev, k, 2, c))
            row = 2 * (band + upper * deep + k - 1) + odd_row
            keep = keep_col & ((row >= 0) & (row < 2 * lane_rows))
            for at, plane in enumerate(gate(sums, keep)):
                g_prev[2 * k + odd_row, at] = plane.astype(BF)

    early = lane % seg
    for i in range(2 * rows + 2):
        at_half, at_row = divmod(i + 1, 2 * deep)
        for at in range(4):
            own = g_own[i, at].astype(F32)
            old = g_prev[at_row, at].astype(F32)
            placed = old if at_half == 0 else pltpu.roll(old, lanes - quarter, 1)
            nearer = pltpu.roll(old, lanes - at_half * quarter - cols, 1)
            g_time[0, i, at] = jnp.where(early < 2 * cols, placed, pltpu.roll(own, 2 * cols, 1)).astype(BF)
            g_time[1, i, at] = jnp.where(early < cols, nearer, pltpu.roll(own, cols, 1)).astype(BF)

    cells = 2 * lanes
    place = lax.broadcasted_iota(jnp.int32, (cells, cells), 0)
    taken = lax.broadcasted_iota(jnp.int32, (cells, cells), 1)
    perm = (taken == (place % 2) * lanes + place // 2).astype(BF)

    def plane_of(a, i, at):
        return g_own[i, at] if a == 2 else g_time[a, i, at]

    def finish(l, carry):
        rhs = jnp.concatenate(
            [
                jnp.concatenate(
                    [plane_of(a, 2 * l + s + b, PLANES[p][c]) for s in range(2) for p in range(2)],
                    axis=1,
                )
                for a in range(3)
                for b in range(3)
                for c in range(3)
            ],
            axis=0,
        )
        total = jnp.dot(w2t[...], rhs, preferred_element_type=F32)
        residual = short[:, pl.ds(pl.multiple_of(l * lanes, lanes), lanes)]
        for s in range(2):
            row = 2 * (band + l) + s
            keep = keep_col & (row < 2 * lane_rows)
            pair = jnp.concatenate(
                [
                    jnp.where(keep, total[:, (2 * s + p) * lanes : (2 * s + p + 1) * lanes] + residual, 0.0)
                    for p in range(2)
                ],
                axis=1,
            ).astype(BF)
            mixed = nt(perm, pair).astype(BF)
            out_ref[:, :, 2 * l + s] = mixed.reshape(videos, frames, 2 * cols, outs)
        return carry

    lax.fori_loop(0, rows, finish, 0)

    for there, copy in sends:

        @pl.when(there)
        def _():
            copy.wait_send()


def shards(tm, height, latents, conv_in, conv_out, shortcut, norm_gain, video_rows, video_cols):
    videos, frames, rows, cols, chans = latents.shape
    outs = conv_in.shape[-1]
    ext = rows + 2
    lanes = videos * frames * cols
    taps = 9 * outs
    depth = 27 * outs
    anywhere = pl.BlockSpec(memory_space=pl.ANY)
    return pl.pallas_call(
        functools.partial(section, tm, height),
        out_shape=jax.ShapeDtypeStruct((videos, frames, 2 * rows, 2 * cols, outs), BF),
        in_specs=[anywhere] * 7,
        out_specs=pl.BlockSpec(memory_space=pltpu.VMEM),
        scratch_shapes=[
            pltpu.VMEM((videos, frames, rows, cols, chans), BF),
            pltpu.VMEM((videos, frames, rows, cols, chans), BF),
            pltpu.VMEM((videos, frames, cols, chans), BF),
            pltpu.VMEM((videos, frames, cols, chans), BF),
            pltpu.VMEM((videos, frames, cols, chans), BF),
            pltpu.VMEM((videos, frames, cols, chans), BF),
            pltpu.VMEM((3, taps, chans), BF),
            pltpu.VMEM((depth, outs), BF),
            pltpu.VMEM((outs, chans), BF),
            pltpu.VMEM((1, outs), F32),
            pltpu.SMEM((videos,), jnp.int32),
            pltpu.SMEM((videos,), jnp.int32),
            pltpu.VMEM((outs, depth), BF),
            pltpu.VMEM((outs, lanes), F32),
            pltpu.VMEM((ext, videos, 2 * frames * cols, chans), BF),
            pltpu.VMEM((ext, taps, lanes), F32),
            pltpu.VMEM((ext // 2, taps, lanes), F32),
            pltpu.VMEM((2 * rows + 2, 4, outs, lanes), BF),
            pltpu.VMEM((ext, 4, outs, lanes), BF),
            pltpu.VMEM((2, 2 * rows + 2, 4, outs, lanes), BF),
            pltpu.VMEM((outs, rows * lanes), F32),
            pltpu.SemaphoreType.DMA((7,)),
            pltpu.SemaphoreType.DMA((6,)),
            pltpu.SemaphoreType.DMA((6,)),
        ],
        compiler_params=pltpu.CompilerParams(
            collective_id=0, has_side_effects=True, vmem_limit_bytes=56 << 20
        ),
    )(
        latents,
        jnp.swapaxes(conv_in, 3, 4).reshape(3, taps, chans),
        conv_out.reshape(depth, outs),
        shortcut.T,
        norm_gain.reshape(1, outs),
        video_rows,
        video_cols,
    )


def solution(mesh):
    in_specs = (P(None, "tm", "height", None, None), P(), P(), P(), P(), P(), P())
    out_specs = P(None, "tm", "height", None, None)
    return jax.shard_map(
        functools.partial(shards, mesh.shape["tm"], mesh.shape["height"]),
        mesh=mesh,
        in_specs=in_specs,
        out_specs=out_specs,
        check_vma=False,
    )
```

```python
import functools

import jax
import jax.numpy as jnp
from jax import lax
from jax.experimental import pallas as pl
from jax.experimental.pallas import tpu as pltpu
from jax.sharding import PartitionSpec as P

BF = jnp.bfloat16
F32 = jnp.float32
NT = (((1,), (1,)), ((), ()))
PLANES = ((0, 1, 2), (1, 2, 3))


def nt(lhs, rhs):
    return lax.dot_general(lhs, rhs, NT, preferred_element_type=F32)


def section(
    tm,
    height,
    lat,
    w1_hbm,
    w2_hbm,
    ws_hbm,
    gain_hbm,
    rows_hbm,
    cols_hbm,
    out_ref,
    x,
    prev,
    top,
    bot,
    ptop,
    pbot,
    w1,
    w2,
    ws,
    gain_row,
    rows_s,
    cols_s,
    w2t,
    gain_c,
    xm,
    p_own,
    p_prev,
    g_own,
    g_prev,
    g_time,
    short,
    local_sem,
    send_sem,
    recv_sem,
):
    videos, frames, rows, cols, chans = lat.shape
    outs = ws.shape[0]
    taps = 9 * outs
    ext = rows + 2
    lanes = videos * frames * cols
    seg = frames * cols
    ti = lax.axis_index("tm")
    hi = lax.axis_index("height")
    has_up, has_down = hi > 0, hi < height - 1
    has_prev, has_next = ti > 0, ti < tm - 1

    local = [
        pltpu.make_async_copy(src, dst, local_sem.at[k])
        for k, (src, dst) in enumerate(
            (
                (rows_hbm, rows_s),
                (cols_hbm, cols_s),
                (lat, x),
                (gain_hbm, gain_row),
                (w2_hbm, w2),
                (w1_hbm, w1),
                (ws_hbm, ws),
            )
        )
    ]
    for copy in local:
        copy.start()

    def remote(k, src, dst, t, h):
        return pltpu.make_async_remote_copy(
            src_ref=src,
            dst_ref=dst,
            send_sem=send_sem.at[k],
            recv_sem=recv_sem.at[k],
            device_id=(t, h),
            device_id_type=pl.DeviceIdType.MESH,
        )

    half_frames = frames // 2
    sends = (
        (has_next, remote(0, lat.at[:, half_frames:], prev.at[:, half_frames:], ti + 1, hi)),
        (has_down, remote(1, lat.at[:, :, rows - 1], top, ti, hi + 1)),
        (has_up, remote(2, lat.at[:, :, 0], bot, ti, hi - 1)),
        (has_next & has_down, remote(3, lat.at[:, :, rows - 1], ptop, ti + 1, hi + 1)),
        (has_next & has_up, remote(4, lat.at[:, :, 0], pbot, ti + 1, hi - 1)),
        (has_next, remote(5, lat.at[:, :half_frames], prev.at[:, :half_frames], ti + 1, hi)),
    )
    senders = (
        (has_prev, ti - 1, hi),
        (has_up, ti, hi - 1),
        (has_down, ti, hi + 1),
        (has_prev & has_up, ti - 1, hi - 1),
        (has_prev & has_down, ti - 1, hi + 1),
        (has_prev, ti - 1, hi),
    )
    barrier = pltpu.get_barrier_semaphore()
    for there, t, h in senders[:5]:

        @pl.when(there)
        def _():
            pl.semaphore_signal(barrier, inc=1, device_id=(t, h), device_id_type=pl.DeviceIdType.MESH)

    pl.semaphore_wait(barrier, sum(there.astype(jnp.int32) for there, _ in sends[:5]))

    def start(k):
        @pl.when(sends[k][0])
        def _():
            sends[k][1].start()

    for k in (0, 1, 2, 5):
        start(k)

    landing = (
        prev.at[:, half_frames:],
        top,
        bot,
        ptop,
        pbot,
        prev.at[:, :half_frames],
    )

    def arrive(k):
        there = senders[k][0]

        @pl.when(there)
        def _():
            sends[k][1].wait_recv()

        @pl.when(jnp.logical_not(there))
        def _():
            landing[k][...] = jnp.zeros(landing[k].shape, BF)

    col_in = lax.broadcasted_iota(jnp.int32, (cols, 1), 0)
    band = hi * rows
    local[0].wait()
    local[1].wait()
    row_limit = [rows_s[v] for v in range(videos)]
    col_limit = [cols_s[v] for v in range(videos)]

    def mask_into(src, at, r, fs, shift):
        for v in range(videos):
            row = band + r - 1
            keep = (col_in < col_limit[v]) & ((row >= 0) & (row < row_limit[v]))
            for f in fs:
                cell = src[v, f] if at is None else src[v, f, at]
                xm[r, v, (f + shift) * cols : (f + shift + 1) * cols] = jnp.where(keep, cell, jnp.zeros_like(cell))

    every = range(frames)
    local[2].wait()
    for r in range(rows):
        mask_into(x, r, r + 1, every, frames)

    local[3].wait()
    gain_c[...] = jnp.broadcast_to(0.5 * gain_row[...], (lanes, outs)).T
    local[4].wait()
    depth = w2.shape[0]
    step = 3 * 128
    for k in range(0, depth, step):
        size = min(step, depth - k)
        w2t[:, k : k + size] = w2[k : k + size].T

    local[5].wait()
    local[6].wait()

    def own_cells(a, r):
        return [xm[r, v, (2 + a) * cols : (2 + a) * cols + seg] for v in range(videos)]

    short[...] = nt(
        ws[...],
        jnp.concatenate([piece for r in range(rows) for piece in own_cells(2, r + 1)], axis=0),
    )

    def conv_in(dst, at, cells):
        rhs = jnp.concatenate([jnp.concatenate(cells(a), axis=0) for a in range(3)], axis=-1)
        third = taps // 3
        for b in range(3):
            lhs = jnp.concatenate([w1[a, b * third : (b + 1) * third] for a in range(3)], axis=-1)
            res = nt(lhs, rhs)
            for n, k in enumerate(at):
                dst[k, b * third : (b + 1) * third] = res[:, n * lanes : (n + 1) * lanes]

    lane = lax.broadcasted_iota(jnp.int32, (1, lanes), 1)
    lane_col = lane % cols
    first_col = lane_col == 0
    last_col = lane_col == cols - 1
    lane_rows, lane_cols = row_limit[0], col_limit[0]
    for v in range(1, videos):
        lane_rows = jnp.where(lane >= v * seg, row_limit[v], lane_rows)
        lane_cols = jnp.where(lane >= v * seg, col_limit[v], lane_cols)
    keep_col = lane_col < lane_cols
    upper = (lane // (seg // 2)) % 2
    deep = ext // 2
    quarter = seg // 2
    early = lane % seg

    def tap(ref, k, b, c):
        at = (b * 3 + c) * outs
        return ref[k, at : at + outs]

    def gate(sums, keep):
        left = jnp.where(first_col, 0.0, pltpu.roll(sums[0], 1, 1))
        right = jnp.where(last_col, 0.0, pltpu.roll(sums[2], lanes - 1, 1))
        planes = []
        for hidden in (left + sums[1] + sums[2], sums[0] + sums[1] + right):
            mean = jnp.sum(hidden * hidden, axis=0, keepdims=True) * (1.0 / outs)
            scale = jnp.where(keep, lax.rsqrt(mean + 1e-06), 0.0)
            normed = hidden * scale * gain_c[...]
            planes.append(normed + normed * jnp.tanh(normed))
        even, odd = planes
        before = jnp.where(first_col, 0.0, pltpu.roll(odd, 1, 1))
        after = jnp.where(last_col, 0.0, pltpu.roll(even, lanes - 1, 1))
        return before, even, odd, after

    def gate_own(i):
        l = (i + 1) // 2
        pick = (l, l, l + 1) if i % 2 == 0 else (l - 1, l, l)
        sums = [sum(tap(p_own, pick[b], b, c) for b in range(3)) for c in range(3)]
        row = band * 2 + i - 1
        keep = keep_col & ((row >= 0) & (row < 2 * lane_rows))
        for at, plane in enumerate(gate(sums, keep)):
            g_own[i, at] = plane.astype(BF)

    def gate_prev(k, odd_row):
        sums = []
        for c in range(3):
            own = tap(p_prev, k, 1, c)
            if odd_row:
                below = tap(p_prev, k + 1, 2, c) if k + 1 < deep else pltpu.roll(tap(p_prev, 0, 2, c), lanes - quarter, 1)
                sums.append(tap(p_prev, k, 0, c) + own + below)
            else:
                above = tap(p_prev, k - 1, 0, c) if k else pltpu.roll(tap(p_prev, deep - 1, 0, c), quarter, 1)
                sums.append(above + own + tap(p_prev, k, 2, c))
        row = 2 * (band + upper * deep + k - 1) + odd_row
        keep = keep_col & ((row >= 0) & (row < 2 * lane_rows))
        for at, plane in enumerate(gate(sums, keep)):
            g_prev[2 * k + odd_row, at] = plane.astype(BF)

    def shift_time(i):
        at_half, at_row = divmod(i + 1, 2 * deep)
        for at in range(4):
            own = g_own[i, at]
            old = g_prev[at_row, at]
            placed = old if at_half == 0 else pltpu.roll(old, lanes - quarter, 1)
            nearer = pltpu.roll(old, lanes - at_half * quarter - cols, 1)
            g_time[0, i, at] = jnp.where(early < 2 * cols, placed, pltpu.roll(own, 2 * cols, 1))
            g_time[1, i, at] = jnp.where(early < cols, nearer, pltpu.roll(own, cols, 1))

    def prev_cells(a):
        return [
            xm[half * deep + k, v, a * cols : (a + 2) * cols]
            for k in range(deep)
            for v in range(videos)
            for half in range(2)
        ]

    arrive(0)
    start(3)
    start(4)
    for r in range(rows):
        mask_into(prev, r, r + 1, range(half_frames, frames), 0)
    middle = range(1, rows + 1)
    conv_in(p_own, middle, lambda a: [piece for r in middle for piece in own_cells(a, r)])
    for i in range(2, 2 * rows):
        gate_own(i)

    for k in range(1, 6):
        arrive(k)
    for src, psrc, r in ((top, ptop, 0), (bot, pbot, ext - 1)):
        mask_into(src, None, r, every, frames)
        mask_into(psrc, None, r, every, 0)
    for r in range(rows):
        mask_into(prev, r, r + 1, range(half_frames), 0)
    conv_in(p_prev, range(deep), prev_cells)
    conv_in(p_own, (0, ext - 1), lambda a: [piece for r in (0, ext - 1) for piece in own_cells(a, r)])
    for k in range(deep):
        for odd_row in range(2):
            gate_prev(k, odd_row)
    for i in (0, 1, 2 * rows, 2 * rows + 1):
        gate_own(i)

    cells = 2 * lanes
    place = lax.broadcasted_iota(jnp.int32, (cells, cells), 0)
    taken = lax.broadcasted_iota(jnp.int32, (cells, cells), 1)
    perm = (taken == (place % 2) * lanes + place // 2).astype(BF)

    def plane_of(a, i, at):
        return g_own[i, at] if a == 2 else g_time[a, i, at]

    def finish(l):
        rhs = jnp.concatenate(
            [
                jnp.concatenate(
                    [plane_of(a, 2 * l + s + b, PLANES[p][c]) for s in range(2) for p in range(2)],
                    axis=1,
                )
                for a in range(3)
                for b in range(3)
                for c in range(3)
            ],
            axis=0,
        )
        total = jnp.dot(w2t[...], rhs, preferred_element_type=F32)
        residual = short[:, l * lanes : (l + 1) * lanes]
        for s in range(2):
            row = 2 * (band + l) + s
            keep = keep_col & (row < 2 * lane_rows)
            pair = jnp.concatenate(
                [
                    jnp.where(keep, total[:, (2 * s + p) * lanes : (2 * s + p + 1) * lanes] + residual, 0.0)
                    for p in range(2)
                ],
                axis=1,
            ).astype(BF)
            mixed = nt(perm, pair).astype(BF)
            out_ref[:, :, 2 * l + s] = mixed.reshape(videos, frames, 2 * cols, outs)

    shifted = set()
    for l in (*range(1, rows - 1), 0, rows - 1):
        for i in range(2 * l, 2 * l + 4):
            if i not in shifted:
                shift_time(i)
                shifted.add(i)
        finish(l)

    for there, copy in sends:

        @pl.when(there)
        def _():
            copy.wait_send()


def shards(tm, height, latents, conv_in, conv_out, shortcut, norm_gain, video_rows, video_cols):
    videos, frames, rows, cols, chans = latents.shape
    outs = conv_in.shape[-1]
    ext = rows + 2
    lanes = videos * frames * cols
    taps = 9 * outs
    depth = 27 * outs
    anywhere = pl.BlockSpec(memory_space=pl.ANY)
    return pl.pallas_call(
        functools.partial(section, tm, height),
        out_shape=jax.ShapeDtypeStruct((videos, frames, 2 * rows, 2 * cols, outs), BF),
        in_specs=[anywhere] * 7,
        out_specs=pl.BlockSpec(memory_space=pltpu.VMEM),
        scratch_shapes=[
            pltpu.VMEM((videos, frames, rows, cols, chans), BF),
            pltpu.VMEM((videos, frames, rows, cols, chans), BF),
            pltpu.VMEM((videos, frames, cols, chans), BF),
            pltpu.VMEM((videos, frames, cols, chans), BF),
            pltpu.VMEM((videos, frames, cols, chans), BF),
            pltpu.VMEM((videos, frames, cols, chans), BF),
            pltpu.VMEM((3, taps, chans), BF),
            pltpu.VMEM((depth, outs), BF),
            pltpu.VMEM((outs, chans), BF),
            pltpu.VMEM((1, outs), F32),
            pltpu.SMEM((videos,), jnp.int32),
            pltpu.SMEM((videos,), jnp.int32),
            pltpu.VMEM((outs, depth), BF),
            pltpu.VMEM((outs, lanes), F32),
            pltpu.VMEM((ext, videos, 2 * frames * cols, chans), BF),
            pltpu.VMEM((ext, taps, lanes), F32),
            pltpu.VMEM((ext // 2, taps, lanes), F32),
            pltpu.VMEM((2 * rows + 2, 4, outs, lanes), BF),
            pltpu.VMEM((ext, 4, outs, lanes), BF),
            pltpu.VMEM((2, 2 * rows + 2, 4, outs, lanes), BF),
            pltpu.VMEM((outs, rows * lanes), F32),
            pltpu.SemaphoreType.DMA((7,)),
            pltpu.SemaphoreType.DMA((6,)),
            pltpu.SemaphoreType.DMA((6,)),
        ],
        compiler_params=pltpu.CompilerParams(
            collective_id=0, has_side_effects=True, vmem_limit_bytes=56 << 20
        ),
    )(
        latents,
        jnp.swapaxes(conv_in, 3, 4).reshape(3, taps, chans),
        conv_out.reshape(depth, outs),
        shortcut.T,
        norm_gain.reshape(1, outs),
        video_rows,
        video_cols,
    )


def solution(mesh):
    in_specs = (P(None, "tm", "height", None, None), P(), P(), P(), P(), P(), P())
    out_specs = P(None, "tm", "height", None, None)
    return jax.shard_map(
        functools.partial(shards, mesh.shape["tm"], mesh.shape["height"]),
        mesh=mesh,
        in_specs=in_specs,
        out_specs=out_specs,
        check_vma=False,
    )
```

```python
import functools

import jax
import jax.numpy as jnp
from jax import lax
from jax.experimental import pallas as pl
from jax.experimental.pallas import tpu as pltpu
from jax.sharding import PartitionSpec as P

BF = jnp.bfloat16
F32 = jnp.float32
NT = (((1,), (1,)), ((), ()))
PLANES = ((0, 1, 2), (1, 2, 3))


def nt(lhs, rhs):
    return lax.dot_general(lhs, rhs, NT, preferred_element_type=F32)


def section(
    tm,
    height,
    lat,
    w1_hbm,
    w2_hbm,
    ws_hbm,
    gain_hbm,
    rows_hbm,
    cols_hbm,
    out_ref,
    x,
    prev,
    top,
    bot,
    ptop,
    pbot,
    w1,
    w2,
    ws,
    gain_row,
    rows_s,
    cols_s,
    w2t,
    gain_c,
    xm,
    p_own,
    p_prev,
    g_own,
    g_prev,
    g_time,
    short,
    local_sem,
    send_sem,
    recv_sem,
):
    videos, frames, rows, cols, chans = lat.shape
    outs = ws.shape[0]
    taps = 9 * outs
    ext = rows + 2
    lanes = videos * frames * cols
    seg = frames * cols
    ti = lax.axis_index("tm")
    hi = lax.axis_index("height")
    has_up, has_down = hi > 0, hi < height - 1
    has_prev, has_next = ti > 0, ti < tm - 1

    local = [
        pltpu.make_async_copy(src, dst, local_sem.at[k])
        for k, (src, dst) in enumerate(
            (
                (rows_hbm, rows_s),
                (cols_hbm, cols_s),
                (lat, x),
                (gain_hbm, gain_row),
                (w2_hbm, w2),
                (w1_hbm, w1),
                (ws_hbm, ws),
            )
        )
    ]
    for copy in local:
        copy.start()

    def remote(k, src, dst, t, h):
        return pltpu.make_async_remote_copy(
            src_ref=src,
            dst_ref=dst,
            send_sem=send_sem.at[k],
            recv_sem=recv_sem.at[k],
            device_id=(t, h),
            device_id_type=pl.DeviceIdType.MESH,
        )

    half_frames = frames // 2
    sends = (
        (has_next, remote(0, lat.at[:, half_frames:], prev.at[:, half_frames:], ti + 1, hi)),
        (has_down, remote(1, lat.at[:, :, rows - 1], top, ti, hi + 1)),
        (has_up, remote(2, lat.at[:, :, 0], bot, ti, hi - 1)),
        (has_next & has_down, remote(3, lat.at[:, :, rows - 1], ptop, ti + 1, hi + 1)),
        (has_next & has_up, remote(4, lat.at[:, :, 0], pbot, ti + 1, hi - 1)),
        (has_next, remote(5, lat.at[:, :half_frames], prev.at[:, :half_frames], ti + 1, hi)),
    )
    senders = (
        (has_prev, ti - 1, hi),
        (has_up, ti, hi - 1),
        (has_down, ti, hi + 1),
        (has_prev & has_up, ti - 1, hi - 1),
        (has_prev & has_down, ti - 1, hi + 1),
        (has_prev, ti - 1, hi),
    )
    barrier = pltpu.get_barrier_semaphore()
    for there, t, h in senders[:5]:

        @pl.when(there)
        def _():
            pl.semaphore_signal(barrier, inc=1, device_id=(t, h), device_id_type=pl.DeviceIdType.MESH)

    pl.semaphore_wait(barrier, sum(there.astype(jnp.int32) for there, _ in sends[:5]))

    def start(k):
        @pl.when(sends[k][0])
        def _():
            sends[k][1].start()

    for k in (0, 1, 2, 5):
        start(k)

    landing = (
        prev.at[:, half_frames:],
        top,
        bot,
        ptop,
        pbot,
        prev.at[:, :half_frames],
    )

    def arrive(k):
        there = senders[k][0]

        @pl.when(there)
        def _():
            sends[k][1].wait_recv()

        @pl.when(jnp.logical_not(there))
        def _():
            landing[k][...] = jnp.zeros(landing[k].shape, BF)

    col_in = lax.broadcasted_iota(jnp.int32, (cols, 1), 0)
    band = hi * rows
    local[0].wait()
    local[1].wait()
    row_limit = [rows_s[v] for v in range(videos)]
    col_limit = [cols_s[v] for v in range(videos)]

    def mask_into(src, at, r, fs, shift):
        for v in range(videos):
            row = band + r - 1
            keep = (col_in < col_limit[v]) & ((row >= 0) & (row < row_limit[v]))
            for f in fs:
                cell = src[v, f] if at is None else src[v, f, at]
                xm[r, v, (f + shift) * cols : (f + shift + 1) * cols] = jnp.where(keep, cell, jnp.zeros_like(cell))

    every = range(frames)
    local[2].wait()
    for r in range(rows):
        mask_into(x, r, r + 1, every, frames)

    local[3].wait()
    gain_c[...] = jnp.broadcast_to(0.5 * gain_row[...], (lanes, outs)).T
    local[4].wait()
    depth = w2.shape[0]
    step = 3 * 128
    for k in range(0, depth, step):
        size = min(step, depth - k)
        w2t[:, k : k + size] = w2[k : k + size].T

    local[5].wait()
    local[6].wait()

    def own_cells(a, r):
        return [xm[r, v, (2 + a) * cols : (2 + a) * cols + seg] for v in range(videos)]

    short[...] = nt(
        ws[...],
        jnp.concatenate([piece for r in range(rows) for piece in own_cells(2, r + 1)], axis=0),
    )

    def conv_in(targets, cells):
        rhs = jnp.concatenate([jnp.concatenate(cells(a), axis=0) for a in range(3)], axis=-1)
        third = taps // 3
        for b in range(3):
            lhs = jnp.concatenate([w1[a, b * third : (b + 1) * third] for a in range(3)], axis=-1)
            res = nt(lhs, rhs)
            for n, (dst, k) in enumerate(targets):
                dst[k, b * third : (b + 1) * third] = res[:, n * lanes : (n + 1) * lanes]

    lane = lax.broadcasted_iota(jnp.int32, (1, lanes), 1)
    lane_col = lane % cols
    first_col = lane_col == 0
    last_col = lane_col == cols - 1
    lane_rows, lane_cols = row_limit[0], col_limit[0]
    for v in range(1, videos):
        lane_rows = jnp.where(lane >= v * seg, row_limit[v], lane_rows)
        lane_cols = jnp.where(lane >= v * seg, col_limit[v], lane_cols)
    keep_col = lane_col < lane_cols
    upper = (lane // (seg // 2)) % 2 == 1
    half = rows // 2
    edge = half
    pairs = [(0, 2 * rows + 1), (1, 2 * rows)] + [(i, i + 2 * half) for i in range(2, rows)] + [(rows, rows + 1)]
    spot = {i: (n, side) for n, pair in enumerate(pairs) for side, i in enumerate(pair)}
    quarter = seg // 2
    early = lane % seg

    def tap(ref, k, b, c):
        at = (b * 3 + c) * outs
        return ref[k, at : at + outs]

    def gate(sums, keep):
        left = jnp.where(first_col, 0.0, pltpu.roll(sums[0], 1, 1))
        right = jnp.where(last_col, 0.0, pltpu.roll(sums[2], lanes - 1, 1))
        planes = []
        for hidden in (left + sums[1] + sums[2], sums[0] + sums[1] + right):
            mean = jnp.sum(hidden * hidden, axis=0, keepdims=True) * (1.0 / outs)
            scale = jnp.where(keep, lax.rsqrt(mean + 1e-06), 0.0)
            normed = hidden * scale * gain_c[...]
            planes.append(normed + normed * jnp.tanh(normed))
        even, odd = planes
        before = jnp.where(first_col, 0.0, pltpu.roll(odd, 1, 1))
        after = jnp.where(last_col, 0.0, pltpu.roll(even, lanes - 1, 1))
        return before, even, odd, after

    def gate_own(i):
        l = (i + 1) // 2
        pick = (l, l, l + 1) if i % 2 == 0 else (l - 1, l, l)
        sums = [sum(tap(p_own, pick[b], b, c) for b in range(3)) for c in range(3)]
        row = band * 2 + i - 1
        keep = keep_col & ((row >= 0) & (row < 2 * lane_rows))
        for at, plane in enumerate(gate(sums, keep)):
            g_own[i, at] = plane.astype(BF)

    def prev_tap(r, side, b, c):
        k, lies = (edge, int(r > rows)) if r in (0, ext - 1) else ((r - 1) % half, (r - 1) // half)
        piece = tap(p_prev, k, b, c)
        if lies == side:
            return (k, None), piece
        return (k, lies), pltpu.roll(piece, quarter if lies == 0 else lanes - quarter, 1)

    def gate_prev(n):
        pair = pairs[n]
        sums = []
        for c in range(3):
            terms = []
            for b in range(3):
                sides = []
                for side, i in enumerate(pair):
                    l = (i + 1) // 2
                    r = ((l, l, l + 1) if i % 2 == 0 else (l - 1, l, l))[b]
                    sides.append(prev_tap(r, side, b, c))
                (low_key, low), (high_key, high) = sides
                terms.append(low if low_key == high_key else jnp.where(upper, high, low))
            sums.append(sum(terms))
        row = 2 * band - 1 + jnp.where(upper, pair[1], pair[0])
        keep = keep_col & ((row >= 0) & (row < 2 * lane_rows))
        for at, plane in enumerate(gate(sums, keep)):
            g_prev[n, at] = plane.astype(BF)

    def shift_time(i):
        at_row, at_half = spot[i]
        for at in range(4):
            own = g_own[i, at]
            old = g_prev[at_row, at]
            placed = old if at_half == 0 else pltpu.roll(old, lanes - quarter, 1)
            nearer = pltpu.roll(old, lanes - at_half * quarter - cols, 1)
            g_time[0, i, at] = jnp.where(early < 2 * cols, placed, pltpu.roll(own, 2 * cols, 1))
            g_time[1, i, at] = jnp.where(early < cols, nearer, pltpu.roll(own, cols, 1))

    cells = 2 * lanes
    place = lax.broadcasted_iota(jnp.int32, (cells, cells), 0)
    taken = lax.broadcasted_iota(jnp.int32, (cells, cells), 1)
    perm = (taken == (place % 2) * lanes + place // 2).astype(BF)

    def plane_of(a, i, at):
        return g_own[i, at] if a == 2 else g_time[a, i, at]

    def finish(l):
        rhs = jnp.concatenate(
            [
                jnp.concatenate(
                    [plane_of(a, 2 * l + s + b, PLANES[p][c]) for s in range(2) for p in range(2)],
                    axis=1,
                )
                for a in range(3)
                for b in range(3)
                for c in range(3)
            ],
            axis=0,
        )
        total = jnp.dot(w2t[...], rhs, preferred_element_type=F32)
        residual = short[:, l * lanes : (l + 1) * lanes]
        for s in range(2):
            row = 2 * (band + l) + s
            keep = keep_col & (row < 2 * lane_rows)
            pair = jnp.concatenate(
                [
                    jnp.where(keep, total[:, (2 * s + p) * lanes : (2 * s + p + 1) * lanes] + residual, 0.0)
                    for p in range(2)
                ],
                axis=1,
            ).astype(BF)
            mixed = nt(perm, pair).astype(BF)
            out_ref[:, :, 2 * l + s] = mixed.reshape(videos, frames, 2 * cols, outs)

    def prev_cells(a, k):
        low, high = (0, ext - 1) if k == edge else (k + 1, k + 1 + half)
        return [xm[r, v, a * cols : (a + 2) * cols] for v in range(videos) for r in (low, high)]

    arrive(0)
    start(3)
    start(4)
    for r in range(rows):
        mask_into(prev, r, r + 1, range(half_frames, frames), 0)
    middle = range(1, rows + 1)
    conv_in([(p_own, r) for r in middle], lambda a: [piece for r in middle for piece in own_cells(a, r)])

    arrive(5)
    for r in range(rows):
        mask_into(prev, r, r + 1, range(half_frames), 0)
    conv_in([(p_prev, k) for k in range(half)], lambda a: [piece for k in range(half) for piece in prev_cells(a, k)])
    inner = range(2, 2 * rows)
    for i in inner:
        gate_own(i)
    for n in range(2, len(pairs)):
        gate_prev(n)
    for i in inner:
        shift_time(i)
    for l in range(1, rows - 1):
        finish(l)

    for k in range(1, 5):
        arrive(k)
    for src, psrc, r in ((top, ptop, 0), (bot, pbot, ext - 1)):
        mask_into(src, None, r, every, frames)
        mask_into(psrc, None, r, every, 0)
    conv_in(
        [(p_own, 0), (p_own, ext - 1), (p_prev, edge)],
        lambda a: own_cells(a, 0) + own_cells(a, ext - 1) + prev_cells(a, edge),
    )
    for n in range(2):
        gate_prev(n)
    outer = (0, 1, 2 * rows, 2 * rows + 1)
    for i in outer:
        gate_own(i)
    for i in outer:
        shift_time(i)
    for l in (0, rows - 1):
        finish(l)

    for there, copy in sends:

        @pl.when(there)
        def _():
            copy.wait_send()


def shards(tm, height, latents, conv_in, conv_out, shortcut, norm_gain, video_rows, video_cols):
    videos, frames, rows, cols, chans = latents.shape
    outs = conv_in.shape[-1]
    ext = rows + 2
    lanes = videos * frames * cols
    taps = 9 * outs
    depth = 27 * outs
    anywhere = pl.BlockSpec(memory_space=pl.ANY)
    return pl.pallas_call(
        functools.partial(section, tm, height),
        out_shape=jax.ShapeDtypeStruct((videos, frames, 2 * rows, 2 * cols, outs), BF),
        in_specs=[anywhere] * 7,
        out_specs=pl.BlockSpec(memory_space=pltpu.VMEM),
        scratch_shapes=[
            pltpu.VMEM((videos, frames, rows, cols, chans), BF),
            pltpu.VMEM((videos, frames, rows, cols, chans), BF),
            pltpu.VMEM((videos, frames, cols, chans), BF),
            pltpu.VMEM((videos, frames, cols, chans), BF),
            pltpu.VMEM((videos, frames, cols, chans), BF),
            pltpu.VMEM((videos, frames, cols, chans), BF),
            pltpu.VMEM((3, taps, chans), BF),
            pltpu.VMEM((depth, outs), BF),
            pltpu.VMEM((outs, chans), BF),
            pltpu.VMEM((1, outs), F32),
            pltpu.SMEM((videos,), jnp.int32),
            pltpu.SMEM((videos,), jnp.int32),
            pltpu.VMEM((outs, depth), BF),
            pltpu.VMEM((outs, lanes), F32),
            pltpu.VMEM((ext, videos, 2 * frames * cols, chans), BF),
            pltpu.VMEM((ext, taps, lanes), F32),
            pltpu.VMEM((ext // 2, taps, lanes), F32),
            pltpu.VMEM((2 * rows + 2, 4, outs, lanes), BF),
            pltpu.VMEM((rows + 1, 4, outs, lanes), BF),
            pltpu.VMEM((2, 2 * rows + 2, 4, outs, lanes), BF),
            pltpu.VMEM((outs, rows * lanes), F32),
            pltpu.SemaphoreType.DMA((7,)),
            pltpu.SemaphoreType.DMA((6,)),
            pltpu.SemaphoreType.DMA((6,)),
        ],
        compiler_params=pltpu.CompilerParams(
            collective_id=0, has_side_effects=True, vmem_limit_bytes=56 << 20
        ),
    )(
        latents,
        jnp.swapaxes(conv_in, 3, 4).reshape(3, taps, chans),
        conv_out.reshape(depth, outs),
        shortcut.T,
        norm_gain.reshape(1, outs),
        video_rows,
        video_cols,
    )


def solution(mesh):
    in_specs = (P(None, "tm", "height", None, None), P(), P(), P(), P(), P(), P())
    out_specs = P(None, "tm", "height", None, None)
    return jax.shard_map(
        functools.partial(shards, mesh.shape["tm"], mesh.shape["height"]),
        mesh=mesh,
        in_specs=in_specs,
        out_specs=out_specs,
        check_vma=False,
    )
```

```python
import functools

import jax
import jax.numpy as jnp
from jax import lax
from jax.experimental import pallas as pl
from jax.experimental.pallas import tpu as pltpu
from jax.sharding import PartitionSpec as P

BF = jnp.bfloat16
F32 = jnp.float32
NT = (((1,), (1,)), ((), ()))
PLANES = ((0, 1, 2), (1, 2, 3))


def nt(lhs, rhs):
    return lax.dot_general(lhs, rhs, NT, preferred_element_type=F32)


def section(
    tm,
    height,
    lat,
    w1_hbm,
    w2_hbm,
    ws_hbm,
    gain_hbm,
    rows_hbm,
    cols_hbm,
    out_ref,
    x,
    prev,
    top,
    bot,
    ptop,
    pbot,
    w1,
    w2,
    ws,
    gain_row,
    rows_s,
    cols_s,
    w2t,
    gain_c,
    xm,
    t_own,
    m_own,
    t_prev,
    m_prev,
    g_own,
    g_prev,
    g_time,
    short,
    local_sem,
    send_sem,
    recv_sem,
):
    videos, frames, rows, cols, chans = lat.shape
    outs = ws.shape[0]
    taps = 9 * outs
    ext = rows + 2
    lanes = videos * frames * cols
    seg = frames * cols
    ti = lax.axis_index("tm")
    hi = lax.axis_index("height")
    has_up, has_down = hi > 0, hi < height - 1
    has_prev, has_next = ti > 0, ti < tm - 1

    local = [
        pltpu.make_async_copy(src, dst, local_sem.at[k])
        for k, (src, dst) in enumerate(
            (
                (rows_hbm, rows_s),
                (cols_hbm, cols_s),
                (lat, x),
                (gain_hbm, gain_row),
                (ws_hbm, ws),
                (w1_hbm, w1),
                (w2_hbm, w2),
            )
        )
    ]
    for copy in local:
        copy.start()

    def remote(k, src, dst, t, h):
        return pltpu.make_async_remote_copy(
            src_ref=src,
            dst_ref=dst,
            send_sem=send_sem.at[k],
            recv_sem=recv_sem.at[k],
            device_id=(t, h),
            device_id_type=pl.DeviceIdType.MESH,
        )

    half_frames = frames // 2
    sends = (
        (has_next, remote(0, lat.at[:, half_frames:], prev.at[:, half_frames:], ti + 1, hi)),
        (has_down, remote(1, lat.at[:, :, rows - 1], top, ti, hi + 1)),
        (has_up, remote(2, lat.at[:, :, 0], bot, ti, hi - 1)),
        (has_next & has_down, remote(3, lat.at[:, :, rows - 1], ptop, ti + 1, hi + 1)),
        (has_next & has_up, remote(4, lat.at[:, :, 0], pbot, ti + 1, hi - 1)),
        (has_next, remote(5, lat.at[:, :half_frames], prev.at[:, :half_frames], ti + 1, hi)),
    )
    senders = (
        (has_prev, ti - 1, hi),
        (has_up, ti, hi - 1),
        (has_down, ti, hi + 1),
        (has_prev & has_up, ti - 1, hi - 1),
        (has_prev & has_down, ti - 1, hi + 1),
        (has_prev, ti - 1, hi),
    )
    barrier = pltpu.get_barrier_semaphore()
    for there, t, h in senders[:5]:

        @pl.when(there)
        def _():
            pl.semaphore_signal(barrier, inc=1, device_id=(t, h), device_id_type=pl.DeviceIdType.MESH)

    pl.semaphore_wait(barrier, sum(there.astype(jnp.int32) for there, _ in sends[:5]))

    def start(k):
        @pl.when(sends[k][0])
        def _():
            sends[k][1].start()

    for k in (0, 1, 2):
        start(k)

    landing = (
        prev.at[:, half_frames:],
        top,
        bot,
        ptop,
        pbot,
        prev.at[:, :half_frames],
    )

    def arrive(k):
        there = senders[k][0]

        @pl.when(there)
        def _():
            sends[k][1].wait_recv()

        @pl.when(jnp.logical_not(there))
        def _():
            landing[k][...] = jnp.zeros(landing[k].shape, BF)

    col_in = lax.broadcasted_iota(jnp.int32, (cols, 1), 0)
    band = hi * rows
    local[0].wait()
    local[1].wait()
    row_limit = [rows_s[v] for v in range(videos)]
    col_limit = [cols_s[v] for v in range(videos)]

    def mask_into(src, at, r, fs, shift):
        for v in range(videos):
            row = band + r - 1
            keep = (col_in < col_limit[v]) & ((row >= 0) & (row < row_limit[v]))
            for f in fs:
                cell = src[v, f] if at is None else src[v, f, at]
                xm[r, v, (f + shift) * cols : (f + shift + 1) * cols] = jnp.where(keep, cell, jnp.zeros_like(cell))

    every = range(frames)
    local[2].wait()
    for r in range(rows):
        mask_into(x, r, r + 1, every, frames)

    third = taps // 3

    def own_cells(a, r):
        return [xm[r, v, (2 + a) * cols : (2 + a) * cols + seg] for v in range(videos)]

    def prev_cells(a, r, other):
        return [xm[at, v, a * cols : (a + 2) * cols] for v in range(videos) for at in (r, other)]

    def product(bs, frame_taps, targets, add=False):
        pieces = [(a, b) for a in frame_taps for b in bs]
        lhs = jnp.concatenate([w1[a, b * third : (b + 1) * third] for a, b in pieces], axis=-1)
        rhs = jnp.concatenate(
            [
                jnp.concatenate(
                    [
                        cell
                        for _, _, at in targets
                        for cell in (own_cells if len(at) == 1 else prev_cells)(a, *[r + b // 2 for r in at])
                    ],
                    axis=0,
                )
                for a, b in pieces
            ],
            axis=-1,
        )
        res = nt(lhs, rhs)
        for n, (dst, k, _) in enumerate(targets):
            val = res[:, n * lanes : (n + 1) * lanes]
            dst[k] = dst[k] + val if add else val

    both, mid = (0, 2), (1,)

    lane = lax.broadcasted_iota(jnp.int32, (1, lanes), 1)
    lane_col = lane % cols
    first_col = lane_col == 0
    last_col = lane_col == cols - 1
    lane_rows, lane_cols = row_limit[0], col_limit[0]
    for v in range(1, videos):
        lane_rows = jnp.where(lane >= v * seg, row_limit[v], lane_rows)
        lane_cols = jnp.where(lane >= v * seg, col_limit[v], lane_cols)
    keep_col = lane_col < lane_cols
    upper = (lane // (seg // 2)) % 2 == 1
    pairs = ((0, 9), (1, 8), (2, 6), (3, 7), (4, 5))
    spot = {i: (n, side) for n, pair in enumerate(pairs) for side, i in enumerate(pair)}
    quarter = seg // 2
    early = lane % seg

    def gate(shared, middle, keep):
        s0, s1, s2 = [shared[c * outs : (c + 1) * outs] + middle[c * outs : (c + 1) * outs] for c in range(3)]
        joint = s0 + jnp.where(last_col, 0.0, pltpu.roll(s2, lanes - 1, 1))
        planes = []
        for hidden in (jnp.where(first_col, s2, pltpu.roll(joint, 1, 1)) + s1, joint + s1):
            mean = jnp.sum(hidden * hidden, axis=0, keepdims=True) * (1.0 / outs)
            scale = jnp.where(keep, lax.rsqrt(mean + 1e-06), 0.0)
            normed = hidden * scale * gain_c[...]
            planes.append(normed + normed * jnp.tanh(normed))
        even, odd = planes
        before = jnp.where(first_col, 0.0, pltpu.roll(odd, 1, 1))
        after = jnp.where(last_col, 0.0, pltpu.roll(even, lanes - 1, 1))
        return before, even, odd, after

    def gate_own(i):
        row = band * 2 + i - 1
        keep = keep_col & ((row >= 0) & (row < 2 * lane_rows))
        for at, plane in enumerate(gate(t_own[i // 2], m_own[(i + 1) // 2], keep)):
            g_own[i, at] = plane.astype(BF)

    shared_at = (2, 2, 0, 0, 1)
    middle_at = ((2, 2), (0, 1), (0, 0), (1, 1), (1, 0))

    def gate_prev(n):
        low, high = middle_at[n]
        middle = m_prev[low] if low == high else jnp.where(upper, m_prev[high], m_prev[low])
        row = 2 * band - 1 + jnp.where(upper, pairs[n][1], pairs[n][0])
        keep = keep_col & ((row >= 0) & (row < 2 * lane_rows))
        for at, plane in enumerate(gate(t_prev[shared_at[n]], middle, keep)):
            g_prev[n, at] = plane.astype(BF)

    def shift_time(i):
        at_row, at_half = spot[i]
        for at in range(4):
            own = g_own[i, at]
            old = g_prev[at_row, at]
            placed = old if at_half == 0 else pltpu.roll(old, lanes - quarter, 1)
            nearer = pltpu.roll(old, lanes - at_half * quarter - cols, 1)
            g_time[0, i, at] = jnp.where(early < 2 * cols, placed, pltpu.roll(own, 2 * cols, 1))
            g_time[1, i, at] = jnp.where(early < cols, nearer, pltpu.roll(own, cols, 1))

    cells = 2 * lanes
    place = lax.broadcasted_iota(jnp.int32, (cells, cells), 0)
    taken = lax.broadcasted_iota(jnp.int32, (cells, cells), 1)
    perm = (taken == (place % 2) * lanes + place // 2).astype(BF)

    def plane_of(a, i, at):
        return g_own[i, at] if a == 2 else g_time[a, i, at]

    def finish(l):
        rhs = jnp.concatenate(
            [
                jnp.concatenate(
                    [plane_of(a, 2 * l + s + b, PLANES[p][c]) for s in range(2) for p in range(2)],
                    axis=1,
                )
                for a in range(3)
                for b in range(3)
                for c in range(3)
            ],
            axis=0,
        )
        total = jnp.dot(w2t[...], rhs, preferred_element_type=F32)
        residual = short[:, l * lanes : (l + 1) * lanes]
        for s in range(2):
            row = 2 * (band + l) + s
            keep = keep_col & (row < 2 * lane_rows)
            pair = jnp.concatenate(
                [
                    jnp.where(keep, total[:, (2 * s + p) * lanes : (2 * s + p + 1) * lanes] + residual, 0.0)
                    for p in range(2)
                ],
                axis=1,
            ).astype(BF)
            mixed = nt(perm, pair).astype(BF)
            out_ref[:, :, 2 * l + s] = mixed.reshape(videos, frames, 2 * cols, outs)

    own_shared = [(t_own, l, (l,)) for l in range(1, rows)]
    own_middle = [(m_own, r, (r,)) for r in range(1, rows + 1)]
    local[4].wait()
    local[5].wait()
    product(both, (2,), own_shared)
    product(mid, (2,), own_middle)
    start(5)
    local[3].wait()
    gain_c[...] = jnp.broadcast_to(0.5 * gain_row[...], (lanes, outs)).T
    short[...] = nt(
        ws[...],
        jnp.concatenate([piece for r in range(rows) for piece in own_cells(2, r + 1)], axis=0),
    )
    local[6].wait()
    depth = w2.shape[0]
    step = 3 * 128
    for k in range(0, depth, step):
        size = min(step, depth - k)
        w2t[:, k : k + size] = w2[k : k + size].T

    arrive(0)
    for r in range(rows):
        mask_into(prev, r, r + 1, range(half_frames, frames), 0)
    product(both, (0, 1), own_shared, add=True)
    product(mid, (0, 1), own_middle, add=True)
    start(3)
    start(4)

    arrive(5)
    for r in range(rows):
        mask_into(prev, r, r + 1, range(half_frames), 0)
    product(both, range(3), [(t_prev, 0, (1, 3)), (t_prev, 1, (2, 2))])
    product(mid, range(3), [(m_prev, 0, (1, 3)), (m_prev, 1, (2, 4))])
    inner = range(2, 2 * rows)
    for i in inner:
        gate_own(i)
    for n in range(2, len(pairs)):
        gate_prev(n)
    for i in inner:
        shift_time(i)
    for l in range(1, rows - 1):
        finish(l)

    for k in range(1, 5):
        arrive(k)
    for src, psrc, r in ((top, ptop, 0), (bot, pbot, ext - 1)):
        mask_into(src, None, r, every, frames)
        mask_into(psrc, None, r, every, 0)
    product(both, range(3), [(t_own, 0, (0,)), (t_own, rows, (rows,)), (t_prev, 2, (0, rows))])
    product(mid, range(3), [(m_own, 0, (0,)), (m_own, ext - 1, (ext - 1,)), (m_prev, 2, (0, ext - 1))])
    for n in range(2):
        gate_prev(n)
    outer = (0, 1, 2 * rows, 2 * rows + 1)
    for i in outer:
        gate_own(i)
    for i in outer:
        shift_time(i)
    for l in (0, rows - 1):
        finish(l)

    for there, copy in sends:

        @pl.when(there)
        def _():
            copy.wait_send()


def shards(tm, height, latents, conv_in, conv_out, shortcut, norm_gain, video_rows, video_cols):
    videos, frames, rows, cols, chans = latents.shape
    outs = conv_in.shape[-1]
    ext = rows + 2
    lanes = videos * frames * cols
    taps = 9 * outs
    depth = 27 * outs
    anywhere = pl.BlockSpec(memory_space=pl.ANY)
    return pl.pallas_call(
        functools.partial(section, tm, height),
        out_shape=jax.ShapeDtypeStruct((videos, frames, 2 * rows, 2 * cols, outs), BF),
        in_specs=[anywhere] * 7,
        out_specs=pl.BlockSpec(memory_space=pltpu.VMEM),
        scratch_shapes=[
            pltpu.VMEM((videos, frames, rows, cols, chans), BF),
            pltpu.VMEM((videos, frames, rows, cols, chans), BF),
            pltpu.VMEM((videos, frames, cols, chans), BF),
            pltpu.VMEM((videos, frames, cols, chans), BF),
            pltpu.VMEM((videos, frames, cols, chans), BF),
            pltpu.VMEM((videos, frames, cols, chans), BF),
            pltpu.VMEM((3, taps, chans), BF),
            pltpu.VMEM((depth, outs), BF),
            pltpu.VMEM((outs, chans), BF),
            pltpu.VMEM((1, outs), F32),
            pltpu.SMEM((videos,), jnp.int32),
            pltpu.SMEM((videos,), jnp.int32),
            pltpu.VMEM((outs, depth), BF),
            pltpu.VMEM((outs, lanes), F32),
            pltpu.VMEM((ext, videos, 2 * frames * cols, chans), BF),
            pltpu.VMEM((ext - 1, 3 * outs, lanes), F32),
            pltpu.VMEM((ext, 3 * outs, lanes), F32),
            pltpu.VMEM((3, 3 * outs, lanes), F32),
            pltpu.VMEM((3, 3 * outs, lanes), F32),
            pltpu.VMEM((2 * rows + 2, 4, outs, lanes), BF),
            pltpu.VMEM((rows + 1, 4, outs, lanes), BF),
            pltpu.VMEM((2, 2 * rows + 2, 4, outs, lanes), BF),
            pltpu.VMEM((outs, rows * lanes), F32),
            pltpu.SemaphoreType.DMA((7,)),
            pltpu.SemaphoreType.DMA((6,)),
            pltpu.SemaphoreType.DMA((6,)),
        ],
        compiler_params=pltpu.CompilerParams(
            collective_id=0, has_side_effects=True, vmem_limit_bytes=56 << 20
        ),
    )(
        latents,
        jnp.swapaxes(conv_in, 3, 4).reshape(3, taps, chans),
        conv_out.reshape(depth, outs),
        shortcut.T,
        norm_gain.reshape(1, outs),
        video_rows,
        video_cols,
    )


def solution(mesh):
    in_specs = (P(None, "tm", "height", None, None), P(), P(), P(), P(), P(), P())
    out_specs = P(None, "tm", "height", None, None)
    return jax.shard_map(
        functools.partial(shards, mesh.shape["tm"], mesh.shape["height"]),
        mesh=mesh,
        in_specs=in_specs,
        out_specs=out_specs,
        check_vma=False,
    )
```

```python
import functools

import jax
import jax.numpy as jnp
from jax import lax
from jax.experimental import pallas as pl
from jax.experimental.pallas import tpu as pltpu
from jax.sharding import PartitionSpec as P

BF = jnp.bfloat16
F32 = jnp.float32
NT = (((1,), (1,)), ((), ()))
PLANES = ((0, 1, 2), (1, 2, 3))


def nt(lhs, rhs):
    return lax.dot_general(lhs, rhs, NT, preferred_element_type=F32)


def section(
    tm,
    height,
    lat,
    w1_hbm,
    w2_hbm,
    ws_hbm,
    gain_hbm,
    rows_hbm,
    cols_hbm,
    out_ref,
    x,
    prev,
    top,
    bot,
    ptop,
    pbot,
    w1,
    w2,
    ws,
    gain_row,
    rows_s,
    cols_s,
    w2t,
    gain_c,
    xm,
    t_own,
    m_own,
    t_prev,
    m_prev,
    g_own,
    g_prev,
    g_time,
    short,
    local_sem,
    send_sem,
    recv_sem,
):
    videos, frames, rows, cols, chans = lat.shape
    outs = ws.shape[0]
    taps = 9 * outs
    ext = rows + 2
    lanes = videos * frames * cols
    seg = frames * cols
    ti = lax.axis_index("tm")
    hi = lax.axis_index("height")
    has_up, has_down = hi > 0, hi < height - 1
    has_prev, has_next = ti > 0, ti < tm - 1

    local = [
        pltpu.make_async_copy(src, dst, local_sem.at[k])
        for k, (src, dst) in enumerate(
            (
                (rows_hbm, rows_s),
                (cols_hbm, cols_s),
                (lat, x),
                (gain_hbm, gain_row),
                (ws_hbm, ws),
                (w1_hbm, w1),
                (w2_hbm, w2),
            )
        )
    ]
    for copy in local:
        copy.start()

    def remote(k, src, dst, t, h):
        return pltpu.make_async_remote_copy(
            src_ref=src,
            dst_ref=dst,
            send_sem=send_sem.at[k],
            recv_sem=recv_sem.at[k],
            device_id=(t, h),
            device_id_type=pl.DeviceIdType.MESH,
        )

    half_frames = frames // 2
    sends = (
        (has_next, remote(0, lat.at[:, half_frames:], prev.at[:, half_frames:], ti + 1, hi)),
        (has_down, remote(1, lat.at[:, :, rows - 1], top, ti, hi + 1)),
        (has_up, remote(2, lat.at[:, :, 0], bot, ti, hi - 1)),
        (has_prev & has_down, remote(3, prev.at[:, :, rows - 1], ptop, ti, hi + 1)),
        (has_prev & has_up, remote(4, prev.at[:, :, 0], pbot, ti, hi - 1)),
        (has_next, remote(5, lat.at[:, :half_frames], prev.at[:, :half_frames], ti + 1, hi)),
    )
    senders = (
        (has_prev, ti - 1, hi),
        (has_up, ti, hi - 1),
        (has_down, ti, hi + 1),
        (has_prev & has_up, ti, hi - 1),
        (has_prev & has_down, ti, hi + 1),
        (has_prev, ti - 1, hi),
    )
    barrier = pltpu.get_barrier_semaphore()
    for there, t, h in senders[:3]:

        @pl.when(there)
        def _():
            pl.semaphore_signal(barrier, inc=1, device_id=(t, h), device_id_type=pl.DeviceIdType.MESH)

    pl.semaphore_wait(barrier, sum(there.astype(jnp.int32) for there, _ in sends[:3]))

    def start(k):
        @pl.when(sends[k][0])
        def _():
            sends[k][1].start()

    for k in (0, 1, 2):
        start(k)

    landing = (
        prev.at[:, half_frames:],
        top,
        bot,
        ptop,
        pbot,
        prev.at[:, :half_frames],
    )

    def arrive(k):
        there = senders[k][0]

        @pl.when(there)
        def _():
            sends[k][1].wait_recv()

        @pl.when(jnp.logical_not(there))
        def _():
            landing[k][...] = jnp.zeros(landing[k].shape, BF)

    col_in = lax.broadcasted_iota(jnp.int32, (cols, 1), 0)
    band = hi * rows
    local[0].wait()
    local[1].wait()
    row_limit = [rows_s[v] for v in range(videos)]
    col_limit = [cols_s[v] for v in range(videos)]

    def mask_into(src, at, r, fs, shift):
        for v in range(videos):
            row = band + r - 1
            keep = (col_in < col_limit[v]) & ((row >= 0) & (row < row_limit[v]))
            for f in fs:
                cell = src[v, f] if at is None else src[v, f, at]
                xm[r, v, (f + shift) * cols : (f + shift + 1) * cols] = jnp.where(keep, cell, jnp.zeros_like(cell))

    every = range(frames)
    local[2].wait()
    for r in range(rows):
        mask_into(x, r, r + 1, every, frames)

    third = taps // 3

    def own_cells(a, r):
        return [xm[r, v, (2 + a) * cols : (2 + a) * cols + seg] for v in range(videos)]

    def prev_cells(a, r, other):
        return [xm[at, v, a * cols : (a + 2) * cols] for v in range(videos) for at in (r, other)]

    def product(bs, frame_taps, targets, add=False):
        pieces = [(a, b) for a in frame_taps for b in bs]
        lhs = jnp.concatenate([w1[a, b * third : (b + 1) * third] for a, b in pieces], axis=-1)
        rhs = jnp.concatenate(
            [
                jnp.concatenate(
                    [
                        cell
                        for _, _, at in targets
                        for cell in (own_cells if len(at) == 1 else prev_cells)(a, *[r + b // 2 for r in at])
                    ],
                    axis=0,
                )
                for a, b in pieces
            ],
            axis=-1,
        )
        res = nt(lhs, rhs)
        for n, (dst, k, _) in enumerate(targets):
            val = res[:, n * lanes : (n + 1) * lanes]
            dst[k] = dst[k] + val if add else val

    both, mid = (0, 2), (1,)

    lane = lax.broadcasted_iota(jnp.int32, (1, lanes), 1)
    lane_col = lane % cols
    first_col = lane_col == 0
    last_col = lane_col == cols - 1
    lane_rows, lane_cols = row_limit[0], col_limit[0]
    for v in range(1, videos):
        lane_rows = jnp.where(lane >= v * seg, row_limit[v], lane_rows)
        lane_cols = jnp.where(lane >= v * seg, col_limit[v], lane_cols)
    keep_col = lane_col < lane_cols
    upper = (lane // (seg // 2)) % 2 == 1
    pairs = ((0, 9), (1, 8), (2, 6), (3, 7), (4, 5))
    spot = {i: (n, side) for n, pair in enumerate(pairs) for side, i in enumerate(pair)}
    quarter = seg // 2
    early = lane % seg

    def gate(shared, middle, keep):
        s0, s1, s2 = [shared[c * outs : (c + 1) * outs] + middle[c * outs : (c + 1) * outs] for c in range(3)]
        joint = s0 + jnp.where(last_col, 0.0, pltpu.roll(s2, lanes - 1, 1))
        planes = []
        for hidden in (jnp.where(first_col, s2, pltpu.roll(joint, 1, 1)) + s1, joint + s1):
            mean = jnp.sum(hidden * hidden, axis=0, keepdims=True) * (1.0 / outs)
            scale = jnp.where(keep, lax.rsqrt(mean + 1e-06), 0.0)
            normed = hidden * scale * gain_c[...]
            planes.append(normed + normed * jnp.tanh(normed))
        even, odd = planes
        before = jnp.where(first_col, 0.0, pltpu.roll(odd, 1, 1))
        after = jnp.where(last_col, 0.0, pltpu.roll(even, lanes - 1, 1))
        return before, even, odd, after

    def gate_own(i):
        row = band * 2 + i - 1
        keep = keep_col & ((row >= 0) & (row < 2 * lane_rows))
        for at, plane in enumerate(gate(t_own[i // 2], m_own[(i + 1) // 2], keep)):
            g_own[i, at] = plane.astype(BF)

    shared_at = (2, 2, 0, 0, 1)
    middle_at = ((2, 2), (0, 1), (0, 0), (1, 1), (1, 0))

    def gate_prev(n):
        low, high = middle_at[n]
        middle = m_prev[low] if low == high else jnp.where(upper, m_prev[high], m_prev[low])
        row = 2 * band - 1 + jnp.where(upper, pairs[n][1], pairs[n][0])
        keep = keep_col & ((row >= 0) & (row < 2 * lane_rows))
        for at, plane in enumerate(gate(t_prev[shared_at[n]], middle, keep)):
            g_prev[n, at] = plane.astype(BF)

    def shift_time(i):
        at_row, at_half = spot[i]
        for at in range(4):
            own = g_own[i, at]
            old = g_prev[at_row, at]
            placed = old if at_half == 0 else pltpu.roll(old, lanes - quarter, 1)
            nearer = pltpu.roll(old, lanes - at_half * quarter - cols, 1)
            g_time[0, i, at] = jnp.where(early < 2 * cols, placed, pltpu.roll(own, 2 * cols, 1))
            g_time[1, i, at] = jnp.where(early < cols, nearer, pltpu.roll(own, cols, 1))

    cells = 2 * lanes
    place = lax.broadcasted_iota(jnp.int32, (cells, cells), 0)
    taken = lax.broadcasted_iota(jnp.int32, (cells, cells), 1)
    perm = (taken == (place % 2) * lanes + place // 2).astype(BF)

    def plane_of(a, i, at):
        return g_own[i, at] if a == 2 else g_time[a, i, at]

    def finish(l):
        rhs = jnp.concatenate(
            [
                jnp.concatenate(
                    [plane_of(a, 2 * l + s + b, PLANES[p][c]) for s in range(2) for p in range(2)],
                    axis=1,
                )
                for a in range(3)
                for b in range(3)
                for c in range(3)
            ],
            axis=0,
        )
        total = jnp.dot(w2t[...], rhs, preferred_element_type=F32)
        residual = short[:, l * lanes : (l + 1) * lanes]
        for s in range(2):
            row = 2 * (band + l) + s
            keep = keep_col & (row < 2 * lane_rows)
            pair = jnp.concatenate(
                [
                    jnp.where(keep, total[:, (2 * s + p) * lanes : (2 * s + p + 1) * lanes] + residual, 0.0)
                    for p in range(2)
                ],
                axis=1,
            ).astype(BF)
            mixed = nt(perm, pair).astype(BF)
            out_ref[:, :, 2 * l + s] = mixed.reshape(videos, frames, 2 * cols, outs)

    own_shared = [(t_own, l, (l,)) for l in range(1, rows)]
    own_middle = [(m_own, r, (r,)) for r in range(1, rows + 1)]
    local[4].wait()
    local[5].wait()
    product(both, (2,), own_shared)
    product(mid, (2,), own_middle)
    local[3].wait()
    gain_c[...] = jnp.broadcast_to(0.5 * gain_row[...], (lanes, outs)).T
    short[...] = nt(
        ws[...],
        jnp.concatenate([piece for r in range(rows) for piece in own_cells(2, r + 1)], axis=0),
    )
    local[6].wait()
    depth = w2.shape[0]
    step = 3 * 128
    for k in range(0, depth, step):
        size = min(step, depth - k)
        w2t[:, k : k + size] = w2[k : k + size].T

    arrive(0)
    for r in range(rows):
        mask_into(prev, r, r + 1, range(half_frames, frames), 0)
    product(both, (0, 1), own_shared, add=True)
    start(5)
    product(mid, (0, 1), own_middle, add=True)

    arrive(5)
    start(3)
    start(4)
    for r in range(rows):
        mask_into(prev, r, r + 1, range(half_frames), 0)
    product(both, range(3), [(t_prev, 0, (1, 3)), (t_prev, 1, (2, 2))])
    product(mid, range(3), [(m_prev, 0, (1, 3)), (m_prev, 1, (2, 4))])
    inner = range(2, 2 * rows)
    for i in inner:
        gate_own(i)
    for n in range(2, len(pairs)):
        gate_prev(n)
    for i in inner:
        shift_time(i)
    for l in range(1, rows - 1):
        finish(l)

    for k in range(1, 5):
        arrive(k)
    for src, psrc, r in ((top, ptop, 0), (bot, pbot, ext - 1)):
        mask_into(src, None, r, every, frames)
        mask_into(psrc, None, r, every, 0)
    product(both, range(3), [(t_own, 0, (0,)), (t_own, rows, (rows,)), (t_prev, 2, (0, rows))])
    product(mid, range(3), [(m_own, 0, (0,)), (m_own, ext - 1, (ext - 1,)), (m_prev, 2, (0, ext - 1))])
    for n in range(2):
        gate_prev(n)
    outer = (0, 1, 2 * rows, 2 * rows + 1)
    for i in outer:
        gate_own(i)
    for i in outer:
        shift_time(i)
    for l in (0, rows - 1):
        finish(l)

    for there, copy in sends:

        @pl.when(there)
        def _():
            copy.wait_send()


def shards(tm, height, latents, conv_in, conv_out, shortcut, norm_gain, video_rows, video_cols):
    videos, frames, rows, cols, chans = latents.shape
    outs = conv_in.shape[-1]
    ext = rows + 2
    lanes = videos * frames * cols
    taps = 9 * outs
    depth = 27 * outs
    anywhere = pl.BlockSpec(memory_space=pl.ANY)
    return pl.pallas_call(
        functools.partial(section, tm, height),
        out_shape=jax.ShapeDtypeStruct((videos, frames, 2 * rows, 2 * cols, outs), BF),
        in_specs=[anywhere] * 7,
        out_specs=pl.BlockSpec(memory_space=pltpu.VMEM),
        scratch_shapes=[
            pltpu.VMEM((videos, frames, rows, cols, chans), BF),
            pltpu.VMEM((videos, frames, rows, cols, chans), BF),
            pltpu.VMEM((videos, frames, cols, chans), BF),
            pltpu.VMEM((videos, frames, cols, chans), BF),
            pltpu.VMEM((videos, frames, cols, chans), BF),
            pltpu.VMEM((videos, frames, cols, chans), BF),
            pltpu.VMEM((3, taps, chans), BF),
            pltpu.VMEM((depth, outs), BF),
            pltpu.VMEM((outs, chans), BF),
            pltpu.VMEM((1, outs), F32),
            pltpu.SMEM((videos,), jnp.int32),
            pltpu.SMEM((videos,), jnp.int32),
            pltpu.VMEM((outs, depth), BF),
            pltpu.VMEM((outs, lanes), F32),
            pltpu.VMEM((ext, videos, 2 * frames * cols, chans), BF),
            pltpu.VMEM((ext - 1, 3 * outs, lanes), F32),
            pltpu.VMEM((ext, 3 * outs, lanes), F32),
            pltpu.VMEM((3, 3 * outs, lanes), F32),
            pltpu.VMEM((3, 3 * outs, lanes), F32),
            pltpu.VMEM((2 * rows + 2, 4, outs, lanes), BF),
            pltpu.VMEM((rows + 1, 4, outs, lanes), BF),
            pltpu.VMEM((2, 2 * rows + 2, 4, outs, lanes), BF),
            pltpu.VMEM((outs, rows * lanes), F32),
            pltpu.SemaphoreType.DMA((7,)),
            pltpu.SemaphoreType.DMA((6,)),
            pltpu.SemaphoreType.DMA((6,)),
        ],
        compiler_params=pltpu.CompilerParams(
            collective_id=0, has_side_effects=True, vmem_limit_bytes=56 << 20
        ),
    )(
        latents,
        jnp.swapaxes(conv_in, 3, 4).reshape(3, taps, chans),
        conv_out.reshape(depth, outs),
        shortcut.T,
        norm_gain.reshape(1, outs),
        video_rows,
        video_cols,
    )


def solution(mesh):
    in_specs = (P(None, "tm", "height", None, None), P(), P(), P(), P(), P(), P())
    out_specs = P(None, "tm", "height", None, None)
    return jax.shard_map(
        functools.partial(shards, mesh.shape["tm"], mesh.shape["height"]),
        mesh=mesh,
        in_specs=in_specs,
        out_specs=out_specs,
        check_vma=False,
    )
```

```python
import functools

import jax
import jax.numpy as jnp
from jax import lax
from jax.experimental import pallas as pl
from jax.experimental.pallas import tpu as pltpu
from jax.sharding import PartitionSpec as P

BF = jnp.bfloat16
F32 = jnp.float32
NT = (((1,), (1,)), ((), ()))
PLANES = ((0, 1, 2), (1, 2, 3))


def nt(lhs, rhs):
    return lax.dot_general(lhs, rhs, NT, preferred_element_type=F32)


def section(
    tm,
    height,
    lat,
    w1_hbm,
    w2_hbm,
    ws_hbm,
    gain_hbm,
    rows_hbm,
    cols_hbm,
    out_ref,
    x,
    prev,
    top,
    bot,
    ptop,
    pbot,
    w1,
    w2,
    ws,
    gain_row,
    rows_s,
    cols_s,
    w2t,
    gain_c,
    xm,
    t_own,
    m_own,
    g_own,
    g_pack,
    g_recv,
    g_time,
    totals,
    short,
    local_sem,
    send_sem,
    recv_sem,
):
    videos, frames, rows, cols, chans = lat.shape
    outs = ws.shape[0]
    taps = 9 * outs
    ext = rows + 2
    lanes = videos * frames * cols
    seg = frames * cols
    ti = lax.axis_index("tm")
    hi = lax.axis_index("height")
    has_up, has_down = hi > 0, hi < height - 1
    has_prev, has_next = ti > 0, ti < tm - 1

    local = [
        pltpu.make_async_copy(src, dst, local_sem.at[k])
        for k, (src, dst) in enumerate(
            (
                (rows_hbm, rows_s),
                (cols_hbm, cols_s),
                (lat, x),
                (gain_hbm, gain_row),
                (ws_hbm, ws),
                (w1_hbm.at[2], w1.at[2]),
                (w2_hbm, w2),
                (w1_hbm.at[:2], w1.at[:2]),
            )
        )
    ]
    for copy in local:
        copy.start()

    def remote(k, src, dst, t, h):
        return pltpu.make_async_remote_copy(
            src_ref=src,
            dst_ref=dst,
            send_sem=send_sem.at[k],
            recv_sem=recv_sem.at[k],
            device_id=(t, h),
            device_id_type=pl.DeviceIdType.MESH,
        )

    old = prev.shape[1]
    inner, outer_low, outer_high = pl.ds(2, 2 * rows - 2), pl.ds(0, 2), pl.ds(2 * rows, 2)
    sends = (
        (has_next, remote(0, lat.at[:, frames - old :], prev, ti + 1, hi)),
        (has_down, remote(1, lat.at[:, :, rows - 1], top, ti, hi + 1)),
        (has_up, remote(2, lat.at[:, :, 0], bot, ti, hi - 1)),
        (has_prev & has_down, remote(3, prev.at[:, :, rows - 1], ptop, ti, hi + 1)),
        (has_prev & has_up, remote(4, prev.at[:, :, 0], pbot, ti, hi - 1)),
        (has_next, remote(5, g_pack.at[inner], g_recv.at[inner], ti + 1, hi)),
        (has_next, remote(6, g_pack.at[outer_low], g_recv.at[outer_low], ti + 1, hi)),
        (has_next, remote(7, g_pack.at[outer_high], g_recv.at[outer_high], ti + 1, hi)),
    )
    senders = (
        (has_prev, ti - 1, hi),
        (has_up, ti, hi - 1),
        (has_down, ti, hi + 1),
        (has_prev & has_up, ti, hi - 1),
        (has_prev & has_down, ti, hi + 1),
        (has_prev, ti - 1, hi),
        (has_prev, ti - 1, hi),
        (has_prev, ti - 1, hi),
    )
    barrier = pltpu.get_barrier_semaphore()
    for there, t, h in senders[:3]:

        @pl.when(there)
        def _():
            pl.semaphore_signal(barrier, inc=1, device_id=(t, h), device_id_type=pl.DeviceIdType.MESH)

    pl.semaphore_wait(barrier, sum(there.astype(jnp.int32) for there, _ in sends[:3]))

    def start(k):
        @pl.when(sends[k][0])
        def _():
            sends[k][1].start()

    for k in (0, 1, 2):
        start(k)

    landing = (prev, top, bot, ptop, pbot, g_recv.at[inner], g_recv.at[outer_low], g_recv.at[outer_high])

    def arrive(k):
        there = senders[k][0]

        @pl.when(there)
        def _():
            sends[k][1].wait_recv()

        @pl.when(jnp.logical_not(there))
        def _():
            landing[k][...] = jnp.zeros(landing[k].shape, BF)

    col_in = lax.broadcasted_iota(jnp.int32, (cols, 1), 0)
    band = hi * rows
    local[0].wait()
    local[1].wait()
    row_limit = [rows_s[v] for v in range(videos)]
    col_limit = [cols_s[v] for v in range(videos)]

    def mask_into(src, at, r, fs, shift):
        for v in range(videos):
            row = band + r - 1
            keep = (col_in < col_limit[v]) & ((row >= 0) & (row < row_limit[v]))
            for f in fs:
                cell = src[v, f] if at is None else src[v, f, at]
                xm[r, v, (f + shift) * cols : (f + shift + 1) * cols] = jnp.where(keep, cell, jnp.zeros_like(cell))

    every = range(frames)
    local[2].wait()
    for r in range(rows):
        mask_into(x, r, r + 1, every, old)

    third = taps // 3

    def own_cells(a, r):
        return [xm[r, v, a * cols : a * cols + seg] for v in range(videos)]

    def product(bs, frame_taps, targets, add=False):
        pieces = [(a, b) for a in frame_taps for b in bs]
        lhs = jnp.concatenate([w1[a, b * third : (b + 1) * third] for a, b in pieces], axis=-1)
        rhs = jnp.concatenate(
            [
                jnp.concatenate([cell for _, at in targets for cell in own_cells(a, at + b // 2)], axis=0)
                for a, b in pieces
            ],
            axis=-1,
        )
        res = nt(lhs, rhs)
        for n, (dst, at) in enumerate(targets):
            val = res[:, n * lanes : (n + 1) * lanes]
            dst[at] = dst[at] + val if add else val

    both, mid = (0, 2), (1,)

    lane = lax.broadcasted_iota(jnp.int32, (1, lanes), 1)
    lane_col = lane % cols
    first_col = lane_col == 0
    last_col = lane_col == cols - 1
    lane_rows, lane_cols = row_limit[0], col_limit[0]
    for v in range(1, videos):
        lane_rows = jnp.where(lane >= v * seg, row_limit[v], lane_rows)
        lane_cols = jnp.where(lane >= v * seg, col_limit[v], lane_cols)
    keep_col = lane_col < lane_cols
    split = old * cols
    early = lane % seg

    def gate(shared, middle, keep):
        s0, s1, s2 = [shared[c * outs : (c + 1) * outs] + middle[c * outs : (c + 1) * outs] for c in range(3)]
        joint = s0 + jnp.where(last_col, 0.0, pltpu.roll(s2, lanes - 1, 1))
        planes = []
        for hidden in (jnp.where(first_col, s2, pltpu.roll(joint, 1, 1)) + s1, joint + s1):
            mean = jnp.sum(hidden * hidden, axis=0, keepdims=True) * (1.0 / outs)
            scale = jnp.where(keep, lax.rsqrt(mean + 1e-06), 0.0)
            normed = hidden * scale * gain_c[...]
            planes.append(normed + normed * jnp.tanh(normed))
        even, odd = planes
        before = jnp.where(first_col, 0.0, pltpu.roll(odd, 1, 1))
        after = jnp.where(last_col, 0.0, pltpu.roll(even, lanes - 1, 1))
        return before, even, odd, after

    def gate_own(i):
        row = band * 2 + i - 1
        keep = keep_col & ((row >= 0) & (row < 2 * lane_rows))
        for at, plane in enumerate(gate(t_own[i // 2], m_own[(i + 1) // 2], keep)):
            g_own[i, at] = plane.astype(BF)
        even, odd = g_own[i, 1], g_own[i, 2]
        g_pack[i] = jnp.where(early < split, pltpu.roll(even, lanes - split, 1), odd)

    def shift_time(i):
        packed = g_recv[i]
        none = jnp.zeros_like(packed)
        before = jnp.where(first_col, none, pltpu.roll(packed, 1, 1))
        after = jnp.where(last_col, none, pltpu.roll(packed, lanes - 1, 1))
        for at, (piece, lies) in enumerate(((before, split), (packed, 0), (packed, split), (after, 0))):
            own = g_own[i, at]
            placed = pltpu.roll(piece, lanes - lies, 1) if lies else piece
            nearer = pltpu.roll(piece, lanes - lies - cols, 1)
            g_time[0, i, at] = jnp.where(early < split, placed, pltpu.roll(own, split, 1))
            g_time[1, i, at] = jnp.where(early < cols, nearer, pltpu.roll(own, cols, 1))

    cells = 2 * lanes
    place = lax.broadcasted_iota(jnp.int32, (cells, cells), 0)
    taken = lax.broadcasted_iota(jnp.int32, (cells, cells), 1)
    perm = (taken == (place % 2) * lanes + place // 2).astype(BF)

    def plane_of(a, i, at):
        return g_own[i, at] if a == 2 else g_time[a, i, at]

    def taps_of(l, frame_taps):
        rhs = jnp.concatenate(
            [
                jnp.concatenate(
                    [plane_of(a, 2 * l + s + b, PLANES[p][c]) for s in range(2) for p in range(2)],
                    axis=1,
                )
                for a in frame_taps
                for b in range(3)
                for c in range(3)
            ],
            axis=0,
        )
        lo, hi_at = frame_taps[0] * taps, (frame_taps[-1] + 1) * taps
        return jnp.dot(w2t[:, lo:hi_at], rhs, preferred_element_type=F32)

    def newest(l):
        totals[l] = taps_of(l, (2,))

    def finish(l):
        total = totals[l] + taps_of(l, (0, 1))
        residual = short[:, l * lanes : (l + 1) * lanes]
        for s in range(2):
            row = 2 * (band + l) + s
            keep = keep_col & (row < 2 * lane_rows)
            pair = jnp.concatenate(
                [
                    jnp.where(keep, total[:, (2 * s + p) * lanes : (2 * s + p + 1) * lanes] + residual, 0.0)
                    for p in range(2)
                ],
                axis=1,
            ).astype(BF)
            mixed = nt(perm, pair).astype(BF)
            out_ref[:, :, 2 * l + s] = mixed.reshape(videos, frames, 2 * cols, outs)

    own_shared = [(t_own, l) for l in range(1, rows)]
    own_middle = [(m_own, r) for r in range(1, rows + 1)]
    local[4].wait()
    local[5].wait()
    product(both, (2,), own_shared)
    product(mid, (2,), own_middle)
    local[3].wait()
    gain_c[...] = jnp.broadcast_to(0.5 * gain_row[...], (lanes, outs)).T
    short[...] = nt(
        ws[...],
        jnp.concatenate([piece for r in range(rows) for piece in own_cells(2, r + 1)], axis=0),
    )
    local[6].wait()
    depth = w2.shape[0]
    step = 3 * 128
    for k in range(0, depth, step):
        size = min(step, depth - k)
        w2t[:, k : k + size] = w2[k : k + size].T
    local[7].wait()

    arrive(0)
    start(3)
    start(4)
    for r in range(rows):
        mask_into(prev, r, r + 1, range(old), 0)
    product(both, (0, 1), own_shared, add=True)
    product(mid, (0, 1), own_middle, add=True)
    center = range(2, 2 * rows)
    for i in center:
        gate_own(i)
    start(5)
    for l in range(1, rows - 1):
        newest(l)

    for k in range(1, 5):
        arrive(k)
    for src, psrc, r in ((top, ptop, 0), (bot, pbot, ext - 1)):
        mask_into(src, None, r, every, old)
        mask_into(psrc, None, r, range(old), 0)
    product(both, range(3), [(t_own, 0), (t_own, rows)])
    product(mid, range(3), [(m_own, 0), (m_own, ext - 1)])
    edges = (0, 1, 2 * rows, 2 * rows + 1)
    for i in edges:
        gate_own(i)
    start(6)
    start(7)

    arrive(5)
    for l in (0, rows - 1):
        newest(l)
    for i in center:
        shift_time(i)
    for l in range(1, rows - 1):
        finish(l)

    arrive(6)
    arrive(7)
    for i in edges:
        shift_time(i)
    for l in (0, rows - 1):
        finish(l)

    for there, copy in sends:

        @pl.when(there)
        def _():
            copy.wait_send()


def shards(tm, height, latents, conv_in, conv_out, shortcut, norm_gain, video_rows, video_cols):
    videos, frames, rows, cols, chans = latents.shape
    outs = conv_in.shape[-1]
    ext = rows + 2
    lanes = videos * frames * cols
    taps = 9 * outs
    depth = 27 * outs
    old = 2
    anywhere = pl.BlockSpec(memory_space=pl.ANY)
    return pl.pallas_call(
        functools.partial(section, tm, height),
        out_shape=jax.ShapeDtypeStruct((videos, frames, 2 * rows, 2 * cols, outs), BF),
        in_specs=[anywhere] * 7,
        out_specs=pl.BlockSpec(memory_space=pltpu.VMEM),
        scratch_shapes=[
            pltpu.VMEM((videos, frames, rows, cols, chans), BF),
            pltpu.VMEM((videos, old, rows, cols, chans), BF),
            pltpu.VMEM((videos, frames, cols, chans), BF),
            pltpu.VMEM((videos, frames, cols, chans), BF),
            pltpu.VMEM((videos, old, cols, chans), BF),
            pltpu.VMEM((videos, old, cols, chans), BF),
            pltpu.VMEM((3, taps, chans), BF),
            pltpu.VMEM((depth, outs), BF),
            pltpu.VMEM((outs, chans), BF),
            pltpu.VMEM((1, outs), F32),
            pltpu.SMEM((videos,), jnp.int32),
            pltpu.SMEM((videos,), jnp.int32),
            pltpu.VMEM((outs, depth), BF),
            pltpu.VMEM((outs, lanes), F32),
            pltpu.VMEM((ext, videos, (frames + old) * cols, chans), BF),
            pltpu.VMEM((ext - 1, 3 * outs, lanes), F32),
            pltpu.VMEM((ext, 3 * outs, lanes), F32),
            pltpu.VMEM((2 * rows + 2, 4, outs, lanes), BF),
            pltpu.VMEM((2 * rows + 2, outs, lanes), BF),
            pltpu.VMEM((2 * rows + 2, outs, lanes), BF),
            pltpu.VMEM((2, 2 * rows + 2, 4, outs, lanes), BF),
            pltpu.VMEM((rows, outs, 4 * lanes), F32),
            pltpu.VMEM((outs, rows * lanes), F32),
            pltpu.SemaphoreType.DMA((8,)),
            pltpu.SemaphoreType.DMA((8,)),
            pltpu.SemaphoreType.DMA((8,)),
        ],
        compiler_params=pltpu.CompilerParams(
            collective_id=0, has_side_effects=True, vmem_limit_bytes=56 << 20
        ),
    )(
        latents,
        jnp.swapaxes(conv_in, 3, 4).reshape(3, taps, chans),
        conv_out.reshape(depth, outs),
        shortcut.T,
        norm_gain.reshape(1, outs),
        video_rows,
        video_cols,
    )


def solution(mesh):
    in_specs = (P(None, "tm", "height", None, None), P(), P(), P(), P(), P(), P())
    out_specs = P(None, "tm", "height", None, None)
    return jax.shard_map(
        functools.partial(shards, mesh.shape["tm"], mesh.shape["height"]),
        mesh=mesh,
        in_specs=in_specs,
        out_specs=out_specs,
        check_vma=False,
    )
```

```python
import functools

import jax
import jax.numpy as jnp
from jax import lax
from jax.experimental import pallas as pl
from jax.experimental.pallas import tpu as pltpu
from jax.sharding import PartitionSpec as P

BF = jnp.bfloat16
F32 = jnp.float32
NT = (((1,), (1,)), ((), ()))
PLANES = ((0, 1, 2), (1, 2, 3))


def nt(lhs, rhs):
    return lax.dot_general(lhs, rhs, NT, preferred_element_type=F32)


def section(
    tm,
    height,
    lat,
    w1_hbm,
    w2_hbm,
    ws_hbm,
    gain_hbm,
    rows_hbm,
    cols_hbm,
    out_ref,
    x,
    prev,
    top,
    bot,
    ptop,
    pbot,
    w1,
    w2,
    ws,
    gain_row,
    rows_s,
    cols_s,
    w2t,
    gain_c,
    xm,
    t_own,
    m_own,
    g_own,
    g_pack,
    g_recv,
    g_time,
    totals,
    short,
    out_v,
    out_sem,
    local_sem,
    send_sem,
    recv_sem,
):
    videos, frames, rows, cols, chans = lat.shape
    outs = ws.shape[0]
    taps = 9 * outs
    ext = rows + 2
    lanes = videos * frames * cols
    seg = frames * cols
    ti = lax.axis_index("tm")
    hi = lax.axis_index("height")
    has_up, has_down = hi > 0, hi < height - 1
    has_prev, has_next = ti > 0, ti < tm - 1

    local = [
        pltpu.make_async_copy(src, dst, local_sem.at[k])
        for k, (src, dst) in enumerate(
            (
                (rows_hbm, rows_s),
                (cols_hbm, cols_s),
                (lat, x),
                (gain_hbm, gain_row),
                (ws_hbm, ws),
                (w1_hbm.at[2], w1.at[2]),
                (w2_hbm, w2),
                (w1_hbm.at[:2], w1.at[:2]),
            )
        )
    ]
    for copy in local:
        copy.start()

    def remote(k, src, dst, t, h):
        return pltpu.make_async_remote_copy(
            src_ref=src,
            dst_ref=dst,
            send_sem=send_sem.at[k],
            recv_sem=recv_sem.at[k],
            device_id=(t, h),
            device_id_type=pl.DeviceIdType.MESH,
        )

    old = prev.shape[1]
    head, tail = pl.ds(2, rows), pl.ds(rows + 2, rows - 2)
    low, high = pl.ds(0, 2), pl.ds(2 * rows, 2)
    sends = (
        (has_next, remote(0, lat.at[:, frames - 1], prev.at[:, old - 1], ti + 1, hi)),
        (has_down, remote(1, lat.at[:, :, rows - 1], top, ti, hi + 1)),
        (has_up, remote(2, lat.at[:, :, 0], bot, ti, hi - 1)),
        (has_prev & has_down, remote(3, prev.at[:, :, rows - 1], ptop, ti, hi + 1)),
        (has_prev & has_up, remote(4, prev.at[:, :, 0], pbot, ti, hi - 1)),
        (has_next, remote(5, g_pack.at[head], g_recv.at[head], ti + 1, hi)),
        (has_next, remote(6, g_pack.at[low], g_recv.at[low], ti + 1, hi)),
        (has_next, remote(7, g_pack.at[high], g_recv.at[high], ti + 1, hi)),
        (has_next, remote(8, g_pack.at[tail], g_recv.at[tail], ti + 1, hi)),
        (has_next, remote(9, lat.at[:, frames - 2], prev.at[:, old - 2], ti + 1, hi)),
    )
    after_me = (has_prev, ti - 1, hi)
    senders = (
        after_me,
        (has_up, ti, hi - 1),
        (has_down, ti, hi + 1),
        (has_prev & has_up, ti, hi - 1),
        (has_prev & has_down, ti, hi + 1),
    ) + (after_me,) * 5
    barrier = pltpu.get_barrier_semaphore()
    for there, t, h in senders[:3]:

        @pl.when(there)
        def _():
            pl.semaphore_signal(barrier, inc=1, device_id=(t, h), device_id_type=pl.DeviceIdType.MESH)

    pl.semaphore_wait(barrier, sum(there.astype(jnp.int32) for there, _ in sends[:3]))

    def start(k):
        @pl.when(sends[k][0])
        def _():
            sends[k][1].start()

    for k in (0, 9, 1, 2):
        start(k)

    landing = (
        prev.at[:, old - 1],
        top,
        bot,
        ptop,
        pbot,
        g_recv.at[head],
        g_recv.at[low],
        g_recv.at[high],
        g_recv.at[tail],
        prev.at[:, old - 2],
    )

    def arrive(k):
        there = senders[k][0]

        @pl.when(there)
        def _():
            sends[k][1].wait_recv()

        @pl.when(jnp.logical_not(there))
        def _():
            landing[k][...] = jnp.zeros(landing[k].shape, BF)

    col_in = lax.broadcasted_iota(jnp.int32, (cols, 1), 0)
    band = hi * rows
    local[0].wait()
    local[1].wait()
    row_limit = [rows_s[v] for v in range(videos)]
    col_limit = [cols_s[v] for v in range(videos)]

    def mask_into(src, at, r, fs, shift):
        for v in range(videos):
            row = band + r - 1
            keep = (col_in < col_limit[v]) & ((row >= 0) & (row < row_limit[v]))
            for f in fs:
                cell = src[v, f] if at is None else src[v, f, at]
                xm[r, v, (f + shift) * cols : (f + shift + 1) * cols] = jnp.where(keep, cell, jnp.zeros_like(cell))

    every = range(frames)
    local[2].wait()
    for r in range(rows):
        mask_into(x, r, r + 1, every, old)

    third = taps // 3

    def own_cells(a, r):
        return [xm[r, v, a * cols : a * cols + seg] for v in range(videos)]

    def product(bs, frame_taps, targets, add=False):
        pieces = [(a, b) for a in frame_taps for b in bs]
        lhs = jnp.concatenate([w1[a, b * third : (b + 1) * third] for a, b in pieces], axis=-1)
        rhs = jnp.concatenate(
            [
                jnp.concatenate([cell for _, at in targets for cell in own_cells(a, at + b // 2)], axis=0)
                for a, b in pieces
            ],
            axis=-1,
        )
        res = nt(lhs, rhs)
        for n, (dst, at) in enumerate(targets):
            val = res[:, n * lanes : (n + 1) * lanes]
            dst[at] = dst[at] + val if add else val

    both, mid = (0, 2), (1,)

    lane = lax.broadcasted_iota(jnp.int32, (1, lanes), 1)
    lane_col = lane % cols
    first_col = lane_col == 0
    last_col = lane_col == cols - 1
    lane_rows, lane_cols = row_limit[0], col_limit[0]
    for v in range(1, videos):
        lane_rows = jnp.where(lane >= v * seg, row_limit[v], lane_rows)
        lane_cols = jnp.where(lane >= v * seg, col_limit[v], lane_cols)
    keep_col = lane_col < lane_cols
    split = old * cols
    early = lane % seg

    def gate(shared, middle, keep):
        s0, s1, s2 = [shared[c * outs : (c + 1) * outs] + middle[c * outs : (c + 1) * outs] for c in range(3)]
        joint = s0 + jnp.where(last_col, 0.0, pltpu.roll(s2, lanes - 1, 1))
        planes = []
        for hidden in (jnp.where(first_col, s2, pltpu.roll(joint, 1, 1)) + s1, joint + s1):
            mean = jnp.sum(hidden * hidden, axis=0, keepdims=True) * (1.0 / outs)
            scale = jnp.where(keep, lax.rsqrt(mean + 1e-06), 0.0)
            normed = hidden * scale * gain_c[...]
            planes.append(normed + normed * jnp.tanh(normed))
        even, odd = planes
        before = jnp.where(first_col, 0.0, pltpu.roll(odd, 1, 1))
        after = jnp.where(last_col, 0.0, pltpu.roll(even, lanes - 1, 1))
        return before, even, odd, after

    def gate_own(i):
        row = band * 2 + i - 1
        keep = keep_col & ((row >= 0) & (row < 2 * lane_rows))
        for at, plane in enumerate(gate(t_own[i // 2], m_own[(i + 1) // 2], keep)):
            g_own[i, at] = plane.astype(BF)
        even, odd = g_own[i, 1], g_own[i, 2]
        g_pack[i] = jnp.where(early < split, pltpu.roll(even, lanes - split, 1), odd)

    def shift_time(i):
        packed = g_recv[i]
        none = jnp.zeros_like(packed)
        before = jnp.where(first_col, none, pltpu.roll(packed, 1, 1))
        after = jnp.where(last_col, none, pltpu.roll(packed, lanes - 1, 1))
        for at, (piece, lies) in enumerate(((before, split), (packed, 0), (packed, split), (after, 0))):
            own = g_own[i, at]
            placed = pltpu.roll(piece, lanes - lies, 1) if lies else piece
            nearer = pltpu.roll(piece, lanes - lies - cols, 1)
            g_time[0, i, at] = jnp.where(early < split, placed, pltpu.roll(own, split, 1))
            g_time[1, i, at] = jnp.where(early < cols, nearer, pltpu.roll(own, cols, 1))

    cells = 2 * lanes
    place = lax.broadcasted_iota(jnp.int32, (cells, cells), 0)
    taken = lax.broadcasted_iota(jnp.int32, (cells, cells), 1)
    perm = (taken == (place % 2) * lanes + place // 2).astype(BF)

    def plane_of(a, i, at):
        return g_own[i, at] if a == 2 else g_time[a, i, at]

    def taps_of(l, frame_taps):
        rhs = jnp.concatenate(
            [
                jnp.concatenate(
                    [plane_of(a, 2 * l + s + b, PLANES[p][c]) for s in range(2) for p in range(2)],
                    axis=1,
                )
                for a in frame_taps
                for b in range(3)
                for c in range(3)
            ],
            axis=0,
        )
        lo, hi_at = frame_taps[0] * taps, (frame_taps[-1] + 1) * taps
        return jnp.dot(w2t[:, lo:hi_at], rhs, preferred_element_type=F32)

    def newest(l):
        totals[l] = taps_of(l, (2,))

    def finish(l):
        total = totals[l] + taps_of(l, (0, 1))
        residual = short[:, l * lanes : (l + 1) * lanes]
        for s in range(2):
            row = 2 * (band + l) + s
            keep = keep_col & (row < 2 * lane_rows)
            pair = jnp.concatenate(
                [
                    jnp.where(keep, total[:, (2 * s + p) * lanes : (2 * s + p + 1) * lanes] + residual, 0.0)
                    for p in range(2)
                ],
                axis=1,
            ).astype(BF)
            mixed = nt(perm, pair).astype(BF)
            out_v[:, :, 2 * l + s] = mixed.reshape(videos, frames, 2 * cols, outs)

    def result(l):
        at = pl.ds(2 * l, 2)
        return pltpu.make_async_copy(out_v.at[:, :, at], out_ref.at[:, :, at], out_sem.at[l])

    def leave(l):
        result(l).start()

    own_shared = [(t_own, l) for l in range(1, rows)]
    own_middle = [(m_own, r) for r in range(1, rows + 1)]
    local[4].wait()
    local[5].wait()
    product(both, (2,), own_shared)
    product(mid, (2,), own_middle)
    local[3].wait()
    gain_c[...] = jnp.broadcast_to(0.5 * gain_row[...], (lanes, outs)).T
    short[...] = nt(
        ws[...],
        jnp.concatenate([piece for r in range(rows) for piece in own_cells(2, r + 1)], axis=0),
    )
    local[6].wait()
    depth = w2.shape[0]
    step = 3 * 128
    for k in range(0, depth, step):
        size = min(step, depth - k)
        w2t[:, k : k + size] = w2[k : k + size].T
    local[7].wait()

    for a, k in ((1, 0), (0, 9)):
        arrive(k)
        for r in range(rows):
            mask_into(prev, r, r + 1, (a,), 0)
        if a == 0:
            start(3)
            start(4)
        product(both, (a,), own_shared, add=True)
        product(mid, (a,), own_middle, add=True)

    for i in range(2, rows + 2):
        gate_own(i)
    start(5)
    for i in range(rows + 2, 2 * rows):
        gate_own(i)
    newest(1)
    start(8)

    arrive(5)
    newest(2)
    for i in range(2, rows + 2):
        shift_time(i)
    finish(1)
    leave(1)

    for k in (1, 2, 3, 4, 8):
        arrive(k)
    for src, psrc, r in ((top, ptop, 0), (bot, pbot, ext - 1)):
        mask_into(src, None, r, every, old)
        mask_into(psrc, None, r, range(old), 0)
    product(both, range(3), [(t_own, 0), (t_own, rows)])
    product(mid, range(3), [(m_own, 0), (m_own, ext - 1)])
    edges = (0, 1, 2 * rows, 2 * rows + 1)
    for i in edges:
        gate_own(i)
    for i in range(rows + 2, 2 * rows):
        shift_time(i)
    finish(2)
    start(6)
    start(7)
    leave(2)

    newest(0)
    arrive(6)
    arrive(7)
    newest(3)
    for i in edges:
        shift_time(i)
    finish(0)
    leave(0)
    finish(3)
    leave(3)
    for l in range(rows):
        result(l).wait()

    for there, copy in sends:

        @pl.when(there)
        def _():
            copy.wait_send()


def shards(tm, height, latents, conv_in, conv_out, shortcut, norm_gain, video_rows, video_cols):
    videos, frames, rows, cols, chans = latents.shape
    outs = conv_in.shape[-1]
    ext = rows + 2
    lanes = videos * frames * cols
    taps = 9 * outs
    depth = 27 * outs
    old = 2
    anywhere = pl.BlockSpec(memory_space=pl.ANY)
    return pl.pallas_call(
        functools.partial(section, tm, height),
        out_shape=jax.ShapeDtypeStruct((videos, frames, 2 * rows, 2 * cols, outs), BF),
        in_specs=[anywhere] * 7,
        out_specs=anywhere,
        scratch_shapes=[
            pltpu.VMEM((videos, frames, rows, cols, chans), BF),
            pltpu.VMEM((videos, old, rows, cols, chans), BF),
            pltpu.VMEM((videos, frames, cols, chans), BF),
            pltpu.VMEM((videos, frames, cols, chans), BF),
            pltpu.VMEM((videos, old, cols, chans), BF),
            pltpu.VMEM((videos, old, cols, chans), BF),
            pltpu.VMEM((3, taps, chans), BF),
            pltpu.VMEM((depth, outs), BF),
            pltpu.VMEM((outs, chans), BF),
            pltpu.VMEM((1, outs), F32),
            pltpu.SMEM((videos,), jnp.int32),
            pltpu.SMEM((videos,), jnp.int32),
            pltpu.VMEM((outs, depth), BF),
            pltpu.VMEM((outs, lanes), F32),
            pltpu.VMEM((ext, videos, (frames + old) * cols, chans), BF),
            pltpu.VMEM((ext - 1, 3 * outs, lanes), F32),
            pltpu.VMEM((ext, 3 * outs, lanes), F32),
            pltpu.VMEM((2 * rows + 2, 4, outs, lanes), BF),
            pltpu.VMEM((2 * rows + 2, outs, lanes), BF),
            pltpu.VMEM((2 * rows + 2, outs, lanes), BF),
            pltpu.VMEM((2, 2 * rows + 2, 4, outs, lanes), BF),
            pltpu.VMEM((rows, outs, 4 * lanes), F32),
            pltpu.VMEM((outs, rows * lanes), F32),
            pltpu.VMEM((videos, frames, 2 * rows, 2 * cols, outs), BF),
            pltpu.SemaphoreType.DMA((rows,)),
            pltpu.SemaphoreType.DMA((8,)),
            pltpu.SemaphoreType.DMA((10,)),
            pltpu.SemaphoreType.DMA((10,)),
        ],
        compiler_params=pltpu.CompilerParams(
            collective_id=0, has_side_effects=True, vmem_limit_bytes=56 << 20
        ),
    )(
        latents,
        jnp.swapaxes(conv_in, 3, 4).reshape(3, taps, chans),
        conv_out.reshape(depth, outs),
        shortcut.T,
        norm_gain.reshape(1, outs),
        video_rows,
        video_cols,
    )


def solution(mesh):
    in_specs = (P(None, "tm", "height", None, None), P(), P(), P(), P(), P(), P())
    out_specs = P(None, "tm", "height", None, None)
    return jax.shard_map(
        functools.partial(shards, mesh.shape["tm"], mesh.shape["height"]),
        mesh=mesh,
        in_specs=in_specs,
        out_specs=out_specs,
        check_vma=False,
    )
```

```python
import functools

import jax
import jax.numpy as jnp
from jax import lax
from jax.experimental import pallas as pl
from jax.experimental.pallas import tpu as pltpu
from jax.sharding import PartitionSpec as P

BF = jnp.bfloat16
F32 = jnp.float32
NT = (((1,), (1,)), ((), ()))
PLANES = ((0, 1, 2), (1, 2, 3))


def nt(lhs, rhs):
    return lax.dot_general(lhs, rhs, NT, preferred_element_type=F32)


def section(
    tm,
    height,
    lat,
    w1_hbm,
    w2_hbm,
    ws_hbm,
    gain_hbm,
    rows_hbm,
    cols_hbm,
    out_ref,
    x,
    prev,
    top,
    bot,
    ptop,
    pbot,
    w1,
    w2,
    ws,
    gain_row,
    rows_s,
    cols_s,
    w2t,
    gain_c,
    xm,
    t_own,
    m_own,
    g_own,
    g_pack,
    g_recv,
    g_old,
    totals,
    short,
    out_v,
    out_sem,
    local_sem,
    send_sem,
    recv_sem,
):
    videos, frames, rows, cols, chans = lat.shape
    outs = ws.shape[0]
    taps = 9 * outs
    ext = rows + 2
    lanes = videos * frames * cols
    seg = frames * cols
    ti = lax.axis_index("tm")
    hi = lax.axis_index("height")
    has_up, has_down = hi > 0, hi < height - 1
    has_prev, has_next = ti > 0, ti < tm - 1

    local = [
        pltpu.make_async_copy(src, dst, local_sem.at[k])
        for k, (src, dst) in enumerate(
            (
                (rows_hbm, rows_s),
                (cols_hbm, cols_s),
                (lat, x),
                (gain_hbm, gain_row),
                (ws_hbm, ws),
                (w1_hbm.at[2], w1.at[2]),
                (w2_hbm, w2),
                (w1_hbm.at[:2], w1.at[:2]),
            )
        )
    ]
    for copy in local:
        copy.start()

    def remote(k, src, dst, t, h):
        return pltpu.make_async_remote_copy(
            src_ref=src,
            dst_ref=dst,
            send_sem=send_sem.at[k],
            recv_sem=recv_sem.at[k],
            device_id=(t, h),
            device_id_type=pl.DeviceIdType.MESH,
        )

    old = prev.shape[1]
    head = pl.ds(2, 2 * rows - 2)
    low, high = pl.ds(0, 2), pl.ds(2 * rows, 2)
    sends = (
        (has_next, remote(0, lat.at[:, frames - 1], prev.at[:, old - 1], ti + 1, hi)),
        (has_down, remote(1, lat.at[:, :, rows - 1], top, ti, hi + 1)),
        (has_up, remote(2, lat.at[:, :, 0], bot, ti, hi - 1)),
        (has_prev & has_down, remote(3, prev.at[:, :, rows - 1], ptop, ti, hi + 1)),
        (has_prev & has_up, remote(4, prev.at[:, :, 0], pbot, ti, hi - 1)),
        (has_next, remote(5, g_pack.at[head], g_recv.at[head], ti + 1, hi)),
        (has_next, remote(6, g_pack.at[low], g_recv.at[low], ti + 1, hi)),
        (has_next, remote(7, g_pack.at[high], g_recv.at[high], ti + 1, hi)),
        (has_next, remote(8, lat.at[:, frames - 2], prev.at[:, old - 2], ti + 1, hi)),
    )
    after_me = (has_prev, ti - 1, hi)
    senders = (
        after_me,
        (has_up, ti, hi - 1),
        (has_down, ti, hi + 1),
        (has_prev & has_up, ti, hi - 1),
        (has_prev & has_down, ti, hi + 1),
    ) + (after_me,) * 4
    barrier = pltpu.get_barrier_semaphore()
    for there, t, h in senders[:3]:

        @pl.when(there)
        def _():
            pl.semaphore_signal(barrier, inc=1, device_id=(t, h), device_id_type=pl.DeviceIdType.MESH)

    pl.semaphore_wait(barrier, sum(there.astype(jnp.int32) for there, _ in sends[:3]))

    def start(k):
        @pl.when(sends[k][0])
        def _():
            sends[k][1].start()

    for k in (0, 8, 1, 2):
        start(k)

    landing = (
        prev.at[:, old - 1],
        top,
        bot,
        ptop,
        pbot,
        g_recv.at[head],
        g_recv.at[low],
        g_recv.at[high],
        prev.at[:, old - 2],
    )

    def arrive(k):
        there = senders[k][0]

        @pl.when(there)
        def _():
            sends[k][1].wait_recv()

        @pl.when(jnp.logical_not(there))
        def _():
            landing[k][...] = jnp.zeros(landing[k].shape, BF)

    col_in = lax.broadcasted_iota(jnp.int32, (cols, 1), 0)
    band = hi * rows
    local[0].wait()
    local[1].wait()
    row_limit = [rows_s[v] for v in range(videos)]
    col_limit = [cols_s[v] for v in range(videos)]

    def mask_into(src, at, r, fs, shift):
        for v in range(videos):
            row = band + r - 1
            keep = (col_in < col_limit[v]) & ((row >= 0) & (row < row_limit[v]))
            for f in fs:
                cell = src[v, f] if at is None else src[v, f, at]
                xm[r, v, (f + shift) * cols : (f + shift + 1) * cols] = jnp.where(keep, cell, jnp.zeros_like(cell))

    every = range(frames)
    local[2].wait()
    for r in range(rows):
        mask_into(x, r, r + 1, every, old)

    third = taps // 3

    def own_cells(a, r):
        return [xm[r, v, a * cols : a * cols + seg] for v in range(videos)]

    def product(bs, frame_taps, targets, add=False):
        pieces = [(a, b) for a in frame_taps for b in bs]
        lhs = jnp.concatenate([w1[a, b * third : (b + 1) * third] for a, b in pieces], axis=-1)
        rhs = jnp.concatenate(
            [
                jnp.concatenate([cell for _, at in targets for cell in own_cells(a, at + b // 2)], axis=0)
                for a, b in pieces
            ],
            axis=-1,
        )
        res = nt(lhs, rhs)
        for n, (dst, at) in enumerate(targets):
            val = res[:, n * lanes : (n + 1) * lanes]
            dst[at] = dst[at] + val if add else val

    both, mid = (0, 2), (1,)

    lane = lax.broadcasted_iota(jnp.int32, (1, lanes), 1)
    lane_col = lane % cols
    first_col = lane_col == 0
    last_col = lane_col == cols - 1
    lane_rows, lane_cols = row_limit[0], col_limit[0]
    for v in range(1, videos):
        lane_rows = jnp.where(lane >= v * seg, row_limit[v], lane_rows)
        lane_cols = jnp.where(lane >= v * seg, col_limit[v], lane_cols)
    keep_col = lane_col < lane_cols
    split = old * cols
    early = lane % seg

    def gate(shared, middle, keep):
        s0, s1, s2 = [shared[c * outs : (c + 1) * outs] + middle[c * outs : (c + 1) * outs] for c in range(3)]
        joint = s0 + jnp.where(last_col, 0.0, pltpu.roll(s2, lanes - 1, 1))
        planes = []
        for hidden in (jnp.where(first_col, s2, pltpu.roll(joint, 1, 1)) + s1, joint + s1):
            mean = jnp.sum(hidden * hidden, axis=0, keepdims=True) * (1.0 / outs)
            scale = jnp.where(keep, lax.rsqrt(mean + 1e-06), 0.0)
            normed = hidden * scale * gain_c[...]
            planes.append(normed + normed * jnp.tanh(normed))
        even, odd = planes
        before = jnp.where(first_col, 0.0, pltpu.roll(odd, 1, 1))
        after = jnp.where(last_col, 0.0, pltpu.roll(even, lanes - 1, 1))
        return before, even, odd, after

    def gate_own(i):
        row = band * 2 + i - 1
        keep = keep_col & ((row >= 0) & (row < 2 * lane_rows))
        for at, plane in enumerate(gate(t_own[i // 2], m_own[(i + 1) // 2], keep)):
            g_own[i, at] = plane.astype(BF)
        even, odd = g_own[i, 1], g_own[i, 2]
        g_pack[i] = jnp.where(early < split, pltpu.roll(even, lanes - split, 1), odd)

    def swap(plane):
        return jnp.where(early < split, pltpu.roll(plane, lanes - split, 1), pltpu.roll(plane, split, 1))

    def old_planes(i):
        packed = g_recv[i]
        none = jnp.zeros_like(packed)
        before = jnp.where(first_col, none, pltpu.roll(packed, 1, 1))
        after = jnp.where(last_col, none, pltpu.roll(packed, lanes - 1, 1))
        g_old[0, i] = swap(jnp.where(early < split, packed, before))
        g_old[1, i] = swap(jnp.where(early < split, after, packed))

    cells = 2 * lanes
    place = lax.broadcasted_iota(jnp.int32, (cells, cells), 0)
    taken = lax.broadcasted_iota(jnp.int32, (cells, cells), 1)
    perm = (taken == (place % 2) * lanes + place // 2).astype(BF)

    def later(plane):
        return jnp.where(early < cols, 0.0, pltpu.roll(plane, cols, 1))

    def own_taps(l):
        rhs = jnp.concatenate(
            [
                jnp.concatenate([g_own[2 * l + s + b, PLANES[p][c]] for s in range(2) for p in range(2)], axis=1)
                for b in range(3)
                for c in range(3)
            ],
            axis=0,
        )
        res = jnp.dot(w2t[...], rhs, preferred_element_type=F32)
        for n in range(4):
            by_tap = [res[a * outs : (a + 1) * outs, n * lanes : (n + 1) * lanes] for a in range(3)]
            totals[l, n] = by_tap[2] + later(by_tap[1] + later(by_tap[0]))

    def old_taps(ls):
        def plane(i, c):
            return g_recv[i] if c == 1 else g_old[c // 2, i]

        rhs = jnp.concatenate(
            [
                jnp.concatenate([plane(2 * l + s + b, c) for l in ls for s in range(2)], axis=1)
                for b in range(3)
                for c in range(3)
            ],
            axis=0,
        )
        res = jnp.dot(w2t[: 2 * outs], rhs, preferred_element_type=F32)
        for n in range(2 * len(ls)):
            oldest, newer = [res[a * outs : (a + 1) * outs, n * lanes : (n + 1) * lanes] for a in range(2)]
            both_taps = oldest + jnp.where(early % split < cols, pltpu.roll(newer, lanes - cols, 1), 0.0)
            for p, part in enumerate((both_taps, pltpu.roll(both_taps, lanes - split, 1))):
                at = 2 * (n % 2) + p
                totals[ls[n // 2], at] = totals[ls[n // 2], at] + jnp.where(early < split, part, 0.0)

    def finish(l):
        residual = short[:, l * lanes : (l + 1) * lanes]
        for s in range(2):
            row = 2 * (band + l) + s
            keep = keep_col & (row < 2 * lane_rows)
            pair = jnp.concatenate(
                [
                    jnp.where(keep, totals[l, 2 * s + p] + residual, 0.0)
                    for p in range(2)
                ],
                axis=1,
            ).astype(BF)
            mixed = nt(perm, pair).astype(BF)
            out_v[:, :, 2 * l + s] = mixed.reshape(videos, frames, 2 * cols, outs)

    def result(l):
        at = pl.ds(2 * l, 2)
        return pltpu.make_async_copy(out_v.at[:, :, at], out_ref.at[:, :, at], out_sem.at[l])

    def leave(l):
        result(l).start()

    own_shared = [(t_own, l) for l in range(1, rows)]
    own_middle = [(m_own, r) for r in range(1, rows + 1)]
    local[4].wait()
    local[5].wait()
    product(both, (2,), own_shared)
    product(mid, (2,), own_middle)
    local[3].wait()
    gain_c[...] = jnp.broadcast_to(0.5 * gain_row[...], (lanes, outs)).T
    short[...] = nt(
        ws[...],
        jnp.concatenate([piece for r in range(rows) for piece in own_cells(2, r + 1)], axis=0),
    )
    local[6].wait()
    step = 3 * 128
    for a in range(3):
        for k in range(0, taps, step):
            size = min(step, taps - k)
            w2t[a * outs : (a + 1) * outs, k : k + size] = w2[a * taps + k : a * taps + k + size].T
    local[7].wait()

    for a, k in ((1, 0), (0, 8)):
        arrive(k)
        for r in range(rows):
            mask_into(prev, r, r + 1, (a,), 0)
        if a == 0:
            start(3)
            start(4)
        product(both, (a,), own_shared, add=True)
        product(mid, (a,), own_middle, add=True)

    center = range(2, 2 * rows)
    for i in center:
        gate_own(i)
    start(5)
    own_taps(1)

    for k in range(1, 5):
        arrive(k)
    for src, psrc, r in ((top, ptop, 0), (bot, pbot, ext - 1)):
        mask_into(src, None, r, every, old)
        mask_into(psrc, None, r, range(old), 0)
    product(both, range(3), [(t_own, 0), (t_own, rows)])
    product(mid, range(3), [(m_own, 0), (m_own, ext - 1)])
    edges = (0, 1, 2 * rows, 2 * rows + 1)
    for i in edges:
        gate_own(i)
    own_taps(2)
    start(6)
    start(7)

    arrive(5)
    own_taps(0)
    for i in center:
        old_planes(i)
    own_taps(3)

    arrive(6)
    arrive(7)
    for i in edges:
        old_planes(i)
    for ls in ((1, 2), (0, 3)):
        old_taps(ls)
        for l in ls:
            finish(l)
            leave(l)
    for l in range(rows):
        result(l).wait()

    for there, copy in sends:

        @pl.when(there)
        def _():
            copy.wait_send()


def shards(tm, height, latents, conv_in, conv_out, shortcut, norm_gain, video_rows, video_cols):
    videos, frames, rows, cols, chans = latents.shape
    outs = conv_in.shape[-1]
    ext = rows + 2
    lanes = videos * frames * cols
    taps = 9 * outs
    depth = 27 * outs
    old = 2
    anywhere = pl.BlockSpec(memory_space=pl.ANY)
    return pl.pallas_call(
        functools.partial(section, tm, height),
        out_shape=jax.ShapeDtypeStruct((videos, frames, 2 * rows, 2 * cols, outs), BF),
        in_specs=[anywhere] * 7,
        out_specs=anywhere,
        scratch_shapes=[
            pltpu.VMEM((videos, frames, rows, cols, chans), BF),
            pltpu.VMEM((videos, old, rows, cols, chans), BF),
            pltpu.VMEM((videos, frames, cols, chans), BF),
            pltpu.VMEM((videos, frames, cols, chans), BF),
            pltpu.VMEM((videos, old, cols, chans), BF),
            pltpu.VMEM((videos, old, cols, chans), BF),
            pltpu.VMEM((3, taps, chans), BF),
            pltpu.VMEM((depth, outs), BF),
            pltpu.VMEM((outs, chans), BF),
            pltpu.VMEM((1, outs), F32),
            pltpu.SMEM((videos,), jnp.int32),
            pltpu.SMEM((videos,), jnp.int32),
            pltpu.VMEM((3 * outs, taps), BF),
            pltpu.VMEM((outs, lanes), F32),
            pltpu.VMEM((ext, videos, (frames + old) * cols, chans), BF),
            pltpu.VMEM((ext - 1, 3 * outs, lanes), F32),
            pltpu.VMEM((ext, 3 * outs, lanes), F32),
            pltpu.VMEM((2 * rows + 2, 4, outs, lanes), BF),
            pltpu.VMEM((2 * rows + 2, outs, lanes), BF),
            pltpu.VMEM((2 * rows + 2, outs, lanes), BF),
            pltpu.VMEM((2, 2 * rows + 2, outs, lanes), BF),
            pltpu.VMEM((rows, 4, outs, lanes), F32),
            pltpu.VMEM((outs, rows * lanes), F32),
            pltpu.VMEM((videos, frames, 2 * rows, 2 * cols, outs), BF),
            pltpu.SemaphoreType.DMA((rows,)),
            pltpu.SemaphoreType.DMA((8,)),
            pltpu.SemaphoreType.DMA((9,)),
            pltpu.SemaphoreType.DMA((9,)),
        ],
        compiler_params=pltpu.CompilerParams(
            collective_id=0, has_side_effects=True, vmem_limit_bytes=56 << 20
        ),
    )(
        latents,
        jnp.swapaxes(conv_in, 3, 4).reshape(3, taps, chans),
        conv_out.reshape(depth, outs),
        shortcut.T,
        norm_gain.reshape(1, outs),
        video_rows,
        video_cols,
    )


def solution(mesh):
    in_specs = (P(None, "tm", "height", None, None), P(), P(), P(), P(), P(), P())
    out_specs = P(None, "tm", "height", None, None)
    return jax.shard_map(
        functools.partial(shards, mesh.shape["tm"], mesh.shape["height"]),
        mesh=mesh,
        in_specs=in_specs,
        out_specs=out_specs,
        check_vma=False,
    )
```

```python
import functools

import jax
import jax.numpy as jnp
from jax import lax
from jax.experimental import pallas as pl
from jax.experimental.pallas import tpu as pltpu
from jax.sharding import PartitionSpec as P

BF = jnp.bfloat16
F32 = jnp.float32
NT = (((1,), (1,)), ((), ()))
PLANES = ((0, 1, 2), (1, 2, 3))


def nt(lhs, rhs):
    return lax.dot_general(lhs, rhs, NT, preferred_element_type=F32)


def section(
    tm,
    height,
    lat,
    w1_hbm,
    w2_hbm,
    ws_hbm,
    gain_hbm,
    rows_hbm,
    cols_hbm,
    out_ref,
    x,
    prev,
    top,
    bot,
    ptop,
    pbot,
    w1,
    w2,
    ws,
    gain_row,
    rows_s,
    cols_s,
    w2t,
    gain_c,
    xm,
    t_own,
    m_own,
    g_own,
    g_pack,
    g_recv,
    g_old,
    totals,
    short,
    out_v,
    out_sem,
    local_sem,
    send_sem,
    recv_sem,
):
    videos, frames, rows, cols, chans = lat.shape
    outs = ws.shape[0]
    taps = 9 * outs
    ext = rows + 2
    lanes = videos * frames * cols
    seg = frames * cols
    ti = lax.axis_index("tm")
    hi = lax.axis_index("height")
    has_up, has_down = hi > 0, hi < height - 1
    has_prev, has_next = ti > 0, ti < tm - 1

    local = [
        pltpu.make_async_copy(src, dst, local_sem.at[k])
        for k, (src, dst) in enumerate(
            (
                (rows_hbm, rows_s),
                (cols_hbm, cols_s),
                (lat, x),
                (gain_hbm, gain_row),
                (ws_hbm, ws),
                (w1_hbm.at[2], w1.at[2]),
                (w2_hbm, w2),
                (w1_hbm.at[:2], w1.at[:2]),
            )
        )
    ]
    for copy in local[:6]:
        copy.start()

    def remote(k, src, dst, t, h):
        return pltpu.make_async_remote_copy(
            src_ref=src,
            dst_ref=dst,
            send_sem=send_sem.at[k],
            recv_sem=recv_sem.at[k],
            device_id=(t, h),
            device_id_type=pl.DeviceIdType.MESH,
        )

    old = prev.shape[1]
    head = pl.ds(2, 2 * rows - 2)
    low, high = pl.ds(0, 2), pl.ds(2 * rows, 2)
    sends = (
        (has_next, remote(0, lat.at[:, frames - 1], prev.at[:, old - 1], ti + 1, hi)),
        (has_down, remote(1, lat.at[:, :, rows - 1], top, ti, hi + 1)),
        (has_up, remote(2, lat.at[:, :, 0], bot, ti, hi - 1)),
        (has_prev & has_down, remote(3, prev.at[:, :, rows - 1], ptop, ti, hi + 1)),
        (has_prev & has_up, remote(4, prev.at[:, :, 0], pbot, ti, hi - 1)),
        (has_next, remote(5, g_pack.at[head], g_recv.at[head], ti + 1, hi)),
        (has_next, remote(6, g_pack.at[low], g_recv.at[low], ti + 1, hi)),
        (has_next, remote(7, g_pack.at[high], g_recv.at[high], ti + 1, hi)),
        (has_next, remote(8, lat.at[:, frames - 2], prev.at[:, old - 2], ti + 1, hi)),
    )
    after_me = (has_prev, ti - 1, hi)
    senders = (
        after_me,
        (has_up, ti, hi - 1),
        (has_down, ti, hi + 1),
        (has_prev & has_up, ti, hi - 1),
        (has_prev & has_down, ti, hi + 1),
    ) + (after_me,) * 4
    barrier = pltpu.get_barrier_semaphore()
    for there, t, h in senders[:3]:

        @pl.when(there)
        def _():
            pl.semaphore_signal(barrier, inc=1, device_id=(t, h), device_id_type=pl.DeviceIdType.MESH)

    pl.semaphore_wait(barrier, sum(there.astype(jnp.int32) for there, _ in sends[:3]))

    def start(k):
        @pl.when(sends[k][0])
        def _():
            sends[k][1].start()

    for k in (0, 8, 1, 2):
        start(k)
    for copy in local[6:]:
        copy.start()

    landing = (
        prev.at[:, old - 1],
        top,
        bot,
        ptop,
        pbot,
        g_recv.at[head],
        g_recv.at[low],
        g_recv.at[high],
        prev.at[:, old - 2],
    )

    def arrive(k):
        there = senders[k][0]

        @pl.when(there)
        def _():
            sends[k][1].wait_recv()

        @pl.when(jnp.logical_not(there))
        def _():
            landing[k][...] = jnp.zeros(landing[k].shape, BF)

    col_in = lax.broadcasted_iota(jnp.int32, (cols, 1), 0)
    band = hi * rows
    local[0].wait()
    local[1].wait()
    row_limit = [rows_s[v] for v in range(videos)]
    col_limit = [cols_s[v] for v in range(videos)]

    def mask_into(src, at, r, fs, shift):
        for v in range(videos):
            row = band + r - 1
            keep = (col_in < col_limit[v]) & ((row >= 0) & (row < row_limit[v]))
            for f in fs:
                cell = src[v, f] if at is None else src[v, f, at]
                xm[r, v, (f + shift) * cols : (f + shift + 1) * cols] = jnp.where(keep, cell, jnp.zeros_like(cell))

    every = range(frames)
    local[2].wait()
    for r in range(rows):
        mask_into(x, r, r + 1, every, old)

    third = taps // 3

    def own_cells(a, r):
        return [xm[r, v, a * cols : a * cols + seg] for v in range(videos)]

    def product(bs, frame_taps, targets, add=False):
        pieces = [(a, b) for a in frame_taps for b in bs]
        lhs = jnp.concatenate([w1[a, b * third : (b + 1) * third] for a, b in pieces], axis=-1)
        rhs = jnp.concatenate(
            [
                jnp.concatenate([cell for _, at in targets for cell in own_cells(a, at + b // 2)], axis=0)
                for a, b in pieces
            ],
            axis=-1,
        )
        res = nt(lhs, rhs)
        for n, (dst, at) in enumerate(targets):
            val = res[:, n * lanes : (n + 1) * lanes]
            dst[at] = dst[at] + val if add else val

    both, mid = (0, 2), (1,)

    lane = lax.broadcasted_iota(jnp.int32, (1, lanes), 1)
    lane_col = lane % cols
    first_col = lane_col == 0
    last_col = lane_col == cols - 1
    lane_rows, lane_cols = row_limit[0], col_limit[0]
    for v in range(1, videos):
        lane_rows = jnp.where(lane >= v * seg, row_limit[v], lane_rows)
        lane_cols = jnp.where(lane >= v * seg, col_limit[v], lane_cols)
    keep_col = lane_col < lane_cols
    split = old * cols
    early = lane % seg

    def gate(shared, middle, keep):
        s0, s1, s2 = [shared[c * outs : (c + 1) * outs] + middle[c * outs : (c + 1) * outs] for c in range(3)]
        joint = s0 + jnp.where(last_col, 0.0, pltpu.roll(s2, lanes - 1, 1))
        planes = []
        for hidden in (jnp.where(first_col, s2, pltpu.roll(joint, 1, 1)) + s1, joint + s1):
            mean = jnp.sum(hidden * hidden, axis=0, keepdims=True) * (1.0 / outs)
            scale = jnp.where(keep, lax.rsqrt(mean + 1e-06), 0.0)
            normed = hidden * scale * gain_c[...]
            planes.append(normed + normed * jnp.tanh(normed))
        even, odd = planes
        before = jnp.where(first_col, 0.0, pltpu.roll(odd, 1, 1))
        after = jnp.where(last_col, 0.0, pltpu.roll(even, lanes - 1, 1))
        return before, even, odd, after

    def gate_own(i):
        row = band * 2 + i - 1
        keep = keep_col & ((row >= 0) & (row < 2 * lane_rows))
        for at, plane in enumerate(gate(t_own[i // 2], m_own[(i + 1) // 2], keep)):
            g_own[i, at] = plane.astype(BF)
        even, odd = g_own[i, 1], g_own[i, 2]
        g_pack[i] = jnp.where(early < split, pltpu.roll(even, lanes - split, 1), odd)

    def swap(plane):
        return jnp.where(early < split, pltpu.roll(plane, lanes - split, 1), pltpu.roll(plane, split, 1))

    def old_planes(i):
        packed = g_recv[i]
        none = jnp.zeros_like(packed)
        before = jnp.where(first_col, none, pltpu.roll(packed, 1, 1))
        after = jnp.where(last_col, none, pltpu.roll(packed, lanes - 1, 1))
        g_old[0, i] = swap(jnp.where(early < split, packed, before))
        g_old[1, i] = swap(jnp.where(early < split, after, packed))

    cells = 2 * lanes
    place = lax.broadcasted_iota(jnp.int32, (cells, cells), 0)
    taken = lax.broadcasted_iota(jnp.int32, (cells, cells), 1)
    perm = (taken == (place % 2) * lanes + place // 2).astype(BF)

    def later(plane):
        return jnp.where(early < cols, 0.0, pltpu.roll(plane, cols, 1))

    def own_taps(l):
        rhs = jnp.concatenate(
            [
                jnp.concatenate([g_own[2 * l + s + b, PLANES[p][c]] for s in range(2) for p in range(2)], axis=1)
                for b in range(3)
                for c in range(3)
            ],
            axis=0,
        )
        res = jnp.dot(w2t[...], rhs, preferred_element_type=F32)
        for n in range(4):
            by_tap = [res[a * outs : (a + 1) * outs, n * lanes : (n + 1) * lanes] for a in range(3)]
            totals[l, n] = by_tap[2] + later(by_tap[1] + later(by_tap[0]))

    def old_taps(ls):
        def plane(i, c):
            return g_recv[i] if c == 1 else g_old[c // 2, i]

        rhs = jnp.concatenate(
            [
                jnp.concatenate([plane(2 * l + s + b, c) for l in ls for s in range(2)], axis=1)
                for b in range(3)
                for c in range(3)
            ],
            axis=0,
        )
        res = jnp.dot(w2t[: 2 * outs], rhs, preferred_element_type=F32)
        added = {}
        for n in range(2 * len(ls)):
            oldest, newer = [res[a * outs : (a + 1) * outs, n * lanes : (n + 1) * lanes] for a in range(2)]
            both_taps = oldest + jnp.where(early % split < cols, pltpu.roll(newer, lanes - cols, 1), 0.0)
            for p, part in enumerate((both_taps, pltpu.roll(both_taps, lanes - split, 1))):
                added[ls[n // 2], 2 * (n % 2) + p] = jnp.where(early < split, part, 0.0)
        return added

    def finish(l, added):
        residual = short[:, l * lanes : (l + 1) * lanes]
        for s in range(2):
            row = 2 * (band + l) + s
            keep = keep_col & (row < 2 * lane_rows)
            pair = jnp.concatenate(
                [
                    jnp.where(keep, totals[l, 2 * s + p] + residual + added[l, 2 * s + p], 0.0)
                    for p in range(2)
                ],
                axis=1,
            ).astype(BF)
            mixed = nt(perm, pair).astype(BF)
            out_v[:, :, 2 * l + s] = mixed.reshape(videos, frames, 2 * cols, outs)

    def result(l):
        at = pl.ds(2 * l, 2)
        return pltpu.make_async_copy(out_v.at[:, :, at], out_ref.at[:, :, at], out_sem.at[l])

    def leave(l):
        result(l).start()

    own_shared = [(t_own, l) for l in range(1, rows)]
    own_middle = [(m_own, r) for r in range(1, rows + 1)]
    local[4].wait()
    local[5].wait()
    product(both, (2,), own_shared)
    product(mid, (2,), own_middle)
    local[3].wait()
    gain_c[...] = jnp.broadcast_to(0.5 * gain_row[...], (lanes, outs)).T
    short[...] = nt(
        ws[...],
        jnp.concatenate([piece for r in range(rows) for piece in own_cells(2, r + 1)], axis=0),
    )
    local[6].wait()
    step = 3 * 128
    for a in range(3):
        for k in range(0, taps, step):
            size = min(step, taps - k)
            w2t[a * outs : (a + 1) * outs, k : k + size] = w2[a * taps + k : a * taps + k + size].T
    local[7].wait()

    for a, k in ((1, 0), (0, 8)):
        arrive(k)
        for r in range(rows):
            mask_into(prev, r, r + 1, (a,), 0)
        if a == 0:
            start(3)
            start(4)
        product(both, (a,), own_shared, add=True)
        product(mid, (a,), own_middle, add=True)

    center = range(2, 2 * rows)
    for i in center:
        gate_own(i)
    start(5)
    own_taps(1)

    for k in range(1, 5):
        arrive(k)
    for src, psrc, r in ((top, ptop, 0), (bot, pbot, ext - 1)):
        mask_into(src, None, r, every, old)
        mask_into(psrc, None, r, range(old), 0)
    product(both, range(3), [(t_own, 0), (t_own, rows)])
    product(mid, range(3), [(m_own, 0), (m_own, ext - 1)])
    edges = (0, 1, 2 * rows, 2 * rows + 1)
    for i in edges:
        gate_own(i)
    own_taps(2)
    start(6)
    start(7)

    arrive(5)
    own_taps(0)
    for i in center:
        old_planes(i)
    own_taps(3)

    arrive(6)
    arrive(7)
    for i in edges:
        old_planes(i)
    added = {**old_taps((1, 2)), **old_taps((0, 3))}
    for l in (1, 2, 0):
        finish(l, added)
    leave(1)
    leave(2)
    leave(0)
    finish(3, added)
    leave(3)
    for l in range(rows):
        result(l).wait()

    for there, copy in sends:

        @pl.when(there)
        def _():
            copy.wait_send()


def shards(tm, height, latents, conv_in, conv_out, shortcut, norm_gain, video_rows, video_cols):
    videos, frames, rows, cols, chans = latents.shape
    outs = conv_in.shape[-1]
    ext = rows + 2
    lanes = videos * frames * cols
    taps = 9 * outs
    depth = 27 * outs
    old = 2
    anywhere = pl.BlockSpec(memory_space=pl.ANY)
    return pl.pallas_call(
        functools.partial(section, tm, height),
        out_shape=jax.ShapeDtypeStruct((videos, frames, 2 * rows, 2 * cols, outs), BF),
        in_specs=[anywhere] * 7,
        out_specs=anywhere,
        scratch_shapes=[
            pltpu.VMEM((videos, frames, rows, cols, chans), BF),
            pltpu.VMEM((videos, old, rows, cols, chans), BF),
            pltpu.VMEM((videos, frames, cols, chans), BF),
            pltpu.VMEM((videos, frames, cols, chans), BF),
            pltpu.VMEM((videos, old, cols, chans), BF),
            pltpu.VMEM((videos, old, cols, chans), BF),
            pltpu.VMEM((3, taps, chans), BF),
            pltpu.VMEM((depth, outs), BF),
            pltpu.VMEM((outs, chans), BF),
            pltpu.VMEM((1, outs), F32),
            pltpu.SMEM((videos,), jnp.int32),
            pltpu.SMEM((videos,), jnp.int32),
            pltpu.VMEM((3 * outs, taps), BF),
            pltpu.VMEM((outs, lanes), F32),
            pltpu.VMEM((ext, videos, (frames + old) * cols, chans), BF),
            pltpu.VMEM((ext - 1, 3 * outs, lanes), F32),
            pltpu.VMEM((ext, 3 * outs, lanes), F32),
            pltpu.VMEM((2 * rows + 2, 4, outs, lanes), BF),
            pltpu.VMEM((2 * rows + 2, outs, lanes), BF),
            pltpu.VMEM((2 * rows + 2, outs, lanes), BF),
            pltpu.VMEM((2, 2 * rows + 2, outs, lanes), BF),
            pltpu.VMEM((rows, 4, outs, lanes), F32),
            pltpu.VMEM((outs, rows * lanes), F32),
            pltpu.VMEM((videos, frames, 2 * rows, 2 * cols, outs), BF),
            pltpu.SemaphoreType.DMA((rows,)),
            pltpu.SemaphoreType.DMA((8,)),
            pltpu.SemaphoreType.DMA((9,)),
            pltpu.SemaphoreType.DMA((9,)),
        ],
        compiler_params=pltpu.CompilerParams(
            collective_id=0, has_side_effects=True, vmem_limit_bytes=56 << 20
        ),
    )(
        latents,
        jnp.swapaxes(conv_in, 3, 4).reshape(3, taps, chans),
        conv_out.reshape(depth, outs),
        shortcut.T,
        norm_gain.reshape(1, outs),
        video_rows,
        video_cols,
    )


def solution(mesh):
    in_specs = (P(None, "tm", "height", None, None), P(), P(), P(), P(), P(), P())
    out_specs = P(None, "tm", "height", None, None)
    return jax.shard_map(
        functools.partial(shards, mesh.shape["tm"], mesh.shape["height"]),
        mesh=mesh,
        in_specs=in_specs,
        out_specs=out_specs,
        check_vma=False,
    )
```

```python
import functools

import jax
import jax.numpy as jnp
from jax import lax
from jax.experimental import pallas as pl
from jax.experimental.pallas import tpu as pltpu
from jax.sharding import PartitionSpec as P

BF = jnp.bfloat16
F32 = jnp.float32
NT = (((1,), (1,)), ((), ()))
PLANES = ((0, 1, 2), (1, 2, 3))


def nt(lhs, rhs):
    return lax.dot_general(lhs, rhs, NT, preferred_element_type=F32)


def section(
    tm,
    height,
    lat,
    w1_hbm,
    w2_hbm,
    ws_hbm,
    gain_hbm,
    rows_hbm,
    cols_hbm,
    out_ref,
    x,
    prev,
    top,
    bot,
    ptop,
    pbot,
    w1,
    w2,
    ws,
    gain_row,
    rows_s,
    cols_s,
    w2t,
    gain_c,
    xm,
    t_own,
    m_own,
    g_own,
    g_pack,
    g_recv,
    g_old,
    totals,
    short,
    out_v,
    out_sem,
    local_sem,
    send_sem,
    recv_sem,
):
    videos, frames, rows, cols, chans = lat.shape
    outs = ws.shape[0]
    taps = 9 * outs
    ext = rows + 2
    lanes = videos * frames * cols
    seg = frames * cols
    ti = lax.axis_index("tm")
    hi = lax.axis_index("height")
    has_up, has_down = hi > 0, hi < height - 1
    has_prev, has_next = ti > 0, ti < tm - 1

    local = [
        pltpu.make_async_copy(src, dst, local_sem.at[k])
        for k, (src, dst) in enumerate(
            (
                (rows_hbm, rows_s),
                (cols_hbm, cols_s),
                (lat, x),
                (gain_hbm, gain_row),
                (ws_hbm, ws),
                (w1_hbm.at[2], w1.at[2]),
                (w2_hbm, w2),
                (w1_hbm.at[:2], w1.at[:2]),
            )
        )
    ]
    def remote(k, src, dst, t, h):
        return pltpu.make_async_remote_copy(
            src_ref=src,
            dst_ref=dst,
            send_sem=send_sem.at[k],
            recv_sem=recv_sem.at[k],
            device_id=(t, h),
            device_id_type=pl.DeviceIdType.MESH,
        )

    old = prev.shape[1]
    head = pl.ds(2, 2 * rows - 2)
    low, high = pl.ds(0, 2), pl.ds(2 * rows, 2)
    sends = (
        (has_next, remote(0, lat.at[:, frames - 1], prev.at[:, old - 1], ti + 1, hi)),
        (has_down, remote(1, lat.at[:, :, rows - 1], top, ti, hi + 1)),
        (has_up, remote(2, lat.at[:, :, 0], bot, ti, hi - 1)),
        (has_prev & has_down, remote(3, prev.at[:, :, rows - 1], ptop, ti, hi + 1)),
        (has_prev & has_up, remote(4, prev.at[:, :, 0], pbot, ti, hi - 1)),
        (has_next, remote(5, g_pack.at[head], g_recv.at[head], ti + 1, hi)),
        (has_next, remote(6, g_pack.at[low], g_recv.at[low], ti + 1, hi)),
        (has_next, remote(7, g_pack.at[high], g_recv.at[high], ti + 1, hi)),
        (has_next, remote(8, lat.at[:, frames - 2], prev.at[:, old - 2], ti + 1, hi)),
    )
    after_me = (has_prev, ti - 1, hi)
    senders = (
        after_me,
        (has_up, ti, hi - 1),
        (has_down, ti, hi + 1),
        (has_prev & has_up, ti, hi - 1),
        (has_prev & has_down, ti, hi + 1),
    ) + (after_me,) * 4
    barrier = pltpu.get_barrier_semaphore()
    for there, t, h in senders[:3]:

        @pl.when(there)
        def _():
            pl.semaphore_signal(barrier, inc=1, device_id=(t, h), device_id_type=pl.DeviceIdType.MESH)

    for copy in local[:6]:
        copy.start()
    pl.semaphore_wait(barrier, sum(there.astype(jnp.int32) for there, _ in sends[:3]))

    def start(k):
        @pl.when(sends[k][0])
        def _():
            sends[k][1].start()

    for k in (0, 8, 1, 2):
        start(k)
    for copy in local[6:]:
        copy.start()

    landing = (
        prev.at[:, old - 1],
        top,
        bot,
        ptop,
        pbot,
        g_recv.at[head],
        g_recv.at[low],
        g_recv.at[high],
        prev.at[:, old - 2],
    )

    def arrive(k):
        there = senders[k][0]

        @pl.when(there)
        def _():
            sends[k][1].wait_recv()

        @pl.when(jnp.logical_not(there))
        def _():
            landing[k][...] = jnp.zeros(landing[k].shape, BF)

    col_in = lax.broadcasted_iota(jnp.int32, (cols, 1), 0)
    band = hi * rows
    local[0].wait()
    local[1].wait()
    row_limit = [rows_s[v] for v in range(videos)]
    col_limit = [cols_s[v] for v in range(videos)]

    def mask_into(src, at, r, fs, shift):
        for v in range(videos):
            row = band + r - 1
            keep = (col_in < col_limit[v]) & ((row >= 0) & (row < row_limit[v]))
            for f in fs:
                cell = src[v, f] if at is None else src[v, f, at]
                xm[r, v, (f + shift) * cols : (f + shift + 1) * cols] = jnp.where(keep, cell, jnp.zeros_like(cell))

    every = range(frames)
    local[2].wait()
    for r in range(rows):
        mask_into(x, r, r + 1, every, old)

    third = taps // 3

    def own_cells(a, r):
        return [xm[r, v, a * cols : a * cols + seg] for v in range(videos)]

    def product(bs, frame_taps, targets, add=False):
        pieces = [(a, b) for a in frame_taps for b in bs]
        lhs = jnp.concatenate([w1[a, b * third : (b + 1) * third] for a, b in pieces], axis=-1)
        rhs = jnp.concatenate(
            [
                jnp.concatenate([cell for _, at in targets for cell in own_cells(a, at + b // 2)], axis=0)
                for a, b in pieces
            ],
            axis=-1,
        )
        res = nt(lhs, rhs)
        for n, (dst, at) in enumerate(targets):
            val = res[:, n * lanes : (n + 1) * lanes]
            dst[at] = dst[at] + val if add else val

    both, mid = (0, 2), (1,)

    lane = lax.broadcasted_iota(jnp.int32, (1, lanes), 1)
    lane_col = lane % cols
    first_col = lane_col == 0
    last_col = lane_col == cols - 1
    lane_rows, lane_cols = row_limit[0], col_limit[0]
    for v in range(1, videos):
        lane_rows = jnp.where(lane >= v * seg, row_limit[v], lane_rows)
        lane_cols = jnp.where(lane >= v * seg, col_limit[v], lane_cols)
    keep_col = lane_col < lane_cols
    split = old * cols
    early = lane % seg

    def gate(shared, middle, keep):
        s0, s1, s2 = [shared[c * outs : (c + 1) * outs] + middle[c * outs : (c + 1) * outs] for c in range(3)]
        joint = s0 + jnp.where(last_col, 0.0, pltpu.roll(s2, lanes - 1, 1))
        planes = []
        for hidden in (jnp.where(first_col, s2, pltpu.roll(joint, 1, 1)) + s1, joint + s1):
            mean = jnp.sum(hidden * hidden, axis=0, keepdims=True) * (1.0 / outs)
            scale = jnp.where(keep, lax.rsqrt(mean + 1e-06), 0.0)
            normed = hidden * scale * gain_c[...]
            planes.append(normed + normed * jnp.tanh(normed))
        even, odd = planes
        before = jnp.where(first_col, 0.0, pltpu.roll(odd, 1, 1))
        after = jnp.where(last_col, 0.0, pltpu.roll(even, lanes - 1, 1))
        return before, even, odd, after

    def gate_own(i):
        row = band * 2 + i - 1
        keep = keep_col & ((row >= 0) & (row < 2 * lane_rows))
        for at, plane in enumerate(gate(t_own[i // 2], m_own[(i + 1) // 2], keep)):
            g_own[i, at] = plane.astype(BF)
        even, odd = g_own[i, 1], g_own[i, 2]
        g_pack[i] = jnp.where(early < split, pltpu.roll(even, lanes - split, 1), odd)

    def swap(plane):
        return jnp.where(early < split, pltpu.roll(plane, lanes - split, 1), pltpu.roll(plane, split, 1))

    def old_planes(i):
        packed = g_recv[i]
        none = jnp.zeros_like(packed)
        before = jnp.where(first_col, none, pltpu.roll(packed, 1, 1))
        after = jnp.where(last_col, none, pltpu.roll(packed, lanes - 1, 1))
        g_old[0, i] = swap(jnp.where(early < split, packed, before))
        g_old[1, i] = swap(jnp.where(early < split, after, packed))

    cells = 2 * lanes
    place = lax.broadcasted_iota(jnp.int32, (cells, cells), 0)
    taken = lax.broadcasted_iota(jnp.int32, (cells, cells), 1)
    perm = (taken == (place % 2) * lanes + place // 2).astype(BF)

    def later(plane):
        return jnp.where(early < cols, 0.0, pltpu.roll(plane, cols, 1))

    def own_taps(l):
        rhs = jnp.concatenate(
            [
                jnp.concatenate([g_own[2 * l + s + b, PLANES[p][c]] for s in range(2) for p in range(2)], axis=1)
                for b in range(3)
                for c in range(3)
            ],
            axis=0,
        )
        res = jnp.dot(w2t[...], rhs, preferred_element_type=F32)
        for n in range(4):
            by_tap = [res[a * outs : (a + 1) * outs, n * lanes : (n + 1) * lanes] for a in range(3)]
            totals[l, n] = by_tap[2] + later(by_tap[1] + later(by_tap[0]))

    def old_taps(ls):
        def plane(i, c):
            return g_recv[i] if c == 1 else g_old[c // 2, i]

        rhs = jnp.concatenate(
            [
                jnp.concatenate([plane(2 * l + s + b, c) for l in ls for s in range(2)], axis=1)
                for b in range(3)
                for c in range(3)
            ],
            axis=0,
        )
        res = jnp.dot(w2t[: 2 * outs], rhs, preferred_element_type=F32)
        added = {}
        for n in range(2 * len(ls)):
            oldest, newer = [res[a * outs : (a + 1) * outs, n * lanes : (n + 1) * lanes] for a in range(2)]
            both_taps = oldest + jnp.where(early % split < cols, pltpu.roll(newer, lanes - cols, 1), 0.0)
            for p, part in enumerate((both_taps, pltpu.roll(both_taps, lanes - split, 1))):
                added[ls[n // 2], 2 * (n % 2) + p] = jnp.where(early < split, part, 0.0)
        return added

    def finish(l, added):
        residual = short[:, l * lanes : (l + 1) * lanes]
        for s in range(2):
            row = 2 * (band + l) + s
            keep = keep_col & (row < 2 * lane_rows)
            pair = jnp.concatenate(
                [
                    jnp.where(keep, totals[l, 2 * s + p] + residual + added[l, 2 * s + p], 0.0)
                    for p in range(2)
                ],
                axis=1,
            ).astype(BF)
            mixed = nt(perm, pair).astype(BF)
            out_v[:, :, 2 * l + s] = mixed.reshape(videos, frames, 2 * cols, outs)

    def result(l):
        at = pl.ds(2 * l, 2)
        return pltpu.make_async_copy(out_v.at[:, :, at], out_ref.at[:, :, at], out_sem.at[l])

    def leave(l):
        result(l).start()

    own_shared = [(t_own, l) for l in range(1, rows)]
    own_middle = [(m_own, r) for r in range(1, rows + 1)]
    local[4].wait()
    local[5].wait()
    product(both, (2,), own_shared)
    product(mid, (2,), own_middle)
    local[3].wait()
    gain_c[...] = jnp.broadcast_to(0.5 * gain_row[...], (lanes, outs)).T
    short[...] = nt(
        ws[...],
        jnp.concatenate([piece for r in range(rows) for piece in own_cells(2, r + 1)], axis=0),
    )
    local[6].wait()
    step = 3 * 128
    for a in range(3):
        for k in range(0, taps, step):
            size = min(step, taps - k)
            w2t[a * outs : (a + 1) * outs, k : k + size] = w2[a * taps + k : a * taps + k + size].T
    local[7].wait()

    for a, k in ((1, 0), (0, 8)):
        arrive(k)
        for r in range(rows):
            mask_into(prev, r, r + 1, (a,), 0)
        if a == 0:
            start(3)
            start(4)
        product(both, (a,), own_shared, add=True)
        product(mid, (a,), own_middle, add=True)

    center = range(2, 2 * rows)
    for i in center[:4]:
        gate_own(i)
    own_taps(1)
    for i in center[4:]:
        gate_own(i)
    start(5)

    for k in range(1, 5):
        arrive(k)
    for src, psrc, r in ((top, ptop, 0), (bot, pbot, ext - 1)):
        mask_into(src, None, r, every, old)
        mask_into(psrc, None, r, range(old), 0)
    product(both, range(3), [(t_own, 0), (t_own, rows)])
    product(mid, range(3), [(m_own, 0), (m_own, ext - 1)])
    edges = (0, 1, 2 * rows, 2 * rows + 1)
    for i in edges:
        gate_own(i)
    own_taps(2)
    start(6)
    start(7)

    arrive(5)
    own_taps(0)
    for i in center:
        old_planes(i)
    own_taps(3)

    arrive(6)
    arrive(7)
    for i in edges:
        old_planes(i)
    added = {**old_taps((1, 2)), **old_taps((0, 3))}
    for l in (1, 2, 0):
        finish(l, added)
    leave(1)
    leave(2)
    leave(0)
    finish(3, added)
    leave(3)
    for l in range(rows):
        result(l).wait()

    for there, copy in sends:

        @pl.when(there)
        def _():
            copy.wait_send()


def shards(tm, height, latents, conv_in, conv_out, shortcut, norm_gain, video_rows, video_cols):
    videos, frames, rows, cols, chans = latents.shape
    outs = conv_in.shape[-1]
    ext = rows + 2
    lanes = videos * frames * cols
    taps = 9 * outs
    depth = 27 * outs
    old = 2
    anywhere = pl.BlockSpec(memory_space=pl.ANY)
    return pl.pallas_call(
        functools.partial(section, tm, height),
        out_shape=jax.ShapeDtypeStruct((videos, frames, 2 * rows, 2 * cols, outs), BF),
        in_specs=[anywhere] * 7,
        out_specs=anywhere,
        scratch_shapes=[
            pltpu.VMEM((videos, frames, rows, cols, chans), BF),
            pltpu.VMEM((videos, old, rows, cols, chans), BF),
            pltpu.VMEM((videos, frames, cols, chans), BF),
            pltpu.VMEM((videos, frames, cols, chans), BF),
            pltpu.VMEM((videos, old, cols, chans), BF),
            pltpu.VMEM((videos, old, cols, chans), BF),
            pltpu.VMEM((3, taps, chans), BF),
            pltpu.VMEM((depth, outs), BF),
            pltpu.VMEM((outs, chans), BF),
            pltpu.VMEM((1, outs), F32),
            pltpu.SMEM((videos,), jnp.int32),
            pltpu.SMEM((videos,), jnp.int32),
            pltpu.VMEM((3 * outs, taps), BF),
            pltpu.VMEM((outs, lanes), F32),
            pltpu.VMEM((ext, videos, (frames + old) * cols, chans), BF),
            pltpu.VMEM((ext - 1, 3 * outs, lanes), F32),
            pltpu.VMEM((ext, 3 * outs, lanes), F32),
            pltpu.VMEM((2 * rows + 2, 4, outs, lanes), BF),
            pltpu.VMEM((2 * rows + 2, outs, lanes), BF),
            pltpu.VMEM((2 * rows + 2, outs, lanes), BF),
            pltpu.VMEM((2, 2 * rows + 2, outs, lanes), BF),
            pltpu.VMEM((rows, 4, outs, lanes), F32),
            pltpu.VMEM((outs, rows * lanes), F32),
            pltpu.VMEM((videos, frames, 2 * rows, 2 * cols, outs), BF),
            pltpu.SemaphoreType.DMA((rows,)),
            pltpu.SemaphoreType.DMA((8,)),
            pltpu.SemaphoreType.DMA((9,)),
            pltpu.SemaphoreType.DMA((9,)),
        ],
        compiler_params=pltpu.CompilerParams(
            collective_id=0, has_side_effects=True, vmem_limit_bytes=56 << 20
        ),
    )(
        latents,
        jnp.swapaxes(conv_in, 3, 4).reshape(3, taps, chans),
        conv_out.reshape(depth, outs),
        shortcut.T,
        norm_gain.reshape(1, outs),
        video_rows,
        video_cols,
    )


def solution(mesh):
    in_specs = (P(None, "tm", "height", None, None), P(), P(), P(), P(), P(), P())
    out_specs = P(None, "tm", "height", None, None)
    return jax.shard_map(
        functools.partial(shards, mesh.shape["tm"], mesh.shape["height"]),
        mesh=mesh,
        in_specs=in_specs,
        out_specs=out_specs,
        check_vma=False,
    )
```

```python
import functools

import jax
import jax.numpy as jnp
from jax import lax
from jax.experimental import pallas as pl
from jax.experimental.pallas import tpu as pltpu
from jax.sharding import PartitionSpec as P

BF = jnp.bfloat16
F32 = jnp.float32
NT = (((1,), (1,)), ((), ()))
PLANES = ((0, 1, 2), (1, 2, 3))


def nt(lhs, rhs):
    return lax.dot_general(lhs, rhs, NT, preferred_element_type=F32)


def section(
    tm,
    height,
    lat,
    w1_hbm,
    w2_hbm,
    ws_hbm,
    gain_hbm,
    rows_hbm,
    cols_hbm,
    out_ref,
    x,
    prev,
    top,
    bot,
    ptop,
    pbot,
    w1,
    w2,
    ws,
    gain_row,
    rows_s,
    cols_s,
    w2t,
    gain_c,
    xm,
    t_own,
    m_own,
    g_own,
    g_pack,
    g_recv,
    g_old,
    totals,
    short,
    out_v,
    out_sem,
    local_sem,
    send_sem,
    recv_sem,
):
    videos, frames, rows, cols, chans = lat.shape
    outs = ws.shape[0]
    taps = 9 * outs
    ext = rows + 2
    lanes = videos * frames * cols
    seg = frames * cols
    ti = lax.axis_index("tm")
    hi = lax.axis_index("height")
    has_up, has_down = hi > 0, hi < height - 1
    has_prev, has_next = ti > 0, ti < tm - 1

    local = [
        pltpu.make_async_copy(src, dst, local_sem.at[k])
        for k, (src, dst) in enumerate(
            (
                (rows_hbm, rows_s),
                (cols_hbm, cols_s),
                (lat, x),
                (gain_hbm, gain_row),
                (ws_hbm, ws),
                (w1_hbm.at[2], w1.at[2]),
                (w2_hbm, w2),
                (w1_hbm.at[:2], w1.at[:2]),
            )
        )
    ]
    def remote(k, src, dst, t, h):
        return pltpu.make_async_remote_copy(
            src_ref=src,
            dst_ref=dst,
            send_sem=send_sem.at[k],
            recv_sem=recv_sem.at[k],
            device_id=(t, h),
            device_id_type=pl.DeviceIdType.MESH,
        )

    old = prev.shape[1]
    head = pl.ds(2, 2 * rows - 2)
    low, high = pl.ds(0, 2), pl.ds(2 * rows, 2)
    sends = (
        (has_next, remote(0, lat.at[:, frames - 1], prev.at[:, old - 1], ti + 1, hi)),
        (has_down, remote(1, lat.at[:, :, rows - 1], top, ti, hi + 1)),
        (has_up, remote(2, lat.at[:, :, 0], bot, ti, hi - 1)),
        (has_prev & has_down, remote(3, prev.at[:, :, rows - 1], ptop, ti, hi + 1)),
        (has_prev & has_up, remote(4, prev.at[:, :, 0], pbot, ti, hi - 1)),
        (has_next, remote(5, g_pack.at[head], g_recv.at[head], ti + 1, hi)),
        (has_next, remote(6, g_pack.at[low], g_recv.at[low], ti + 1, hi)),
        (has_next, remote(7, g_pack.at[high], g_recv.at[high], ti + 1, hi)),
        (has_next, remote(8, lat.at[:, frames - 2], prev.at[:, old - 2], ti + 1, hi)),
    )
    after_me = (has_prev, ti - 1, hi)
    senders = (
        after_me,
        (has_up, ti, hi - 1),
        (has_down, ti, hi + 1),
        (has_prev & has_up, ti, hi - 1),
        (has_prev & has_down, ti, hi + 1),
    ) + (after_me,) * 4
    barrier = pltpu.get_barrier_semaphore()
    for there, t, h in senders[:3]:

        @pl.when(there)
        def _():
            pl.semaphore_signal(barrier, inc=1, device_id=(t, h), device_id_type=pl.DeviceIdType.MESH)

    for copy in local[:6]:
        copy.start()
    pl.semaphore_wait(barrier, sum(there.astype(jnp.int32) for there, _ in sends[:3]))

    def start(k):
        @pl.when(sends[k][0])
        def _():
            sends[k][1].start()

    for k in (0, 8, 1, 2):
        start(k)
    for copy in local[6:]:
        copy.start()

    landing = (
        prev.at[:, old - 1],
        top,
        bot,
        ptop,
        pbot,
        g_recv.at[head],
        g_recv.at[low],
        g_recv.at[high],
        prev.at[:, old - 2],
    )

    def arrive(k):
        there = senders[k][0]

        @pl.when(there)
        def _():
            sends[k][1].wait_recv()

        @pl.when(jnp.logical_not(there))
        def _():
            landing[k][...] = jnp.zeros(landing[k].shape, BF)

    col_in = lax.broadcasted_iota(jnp.int32, (cols, 1), 0)
    band = hi * rows
    local[0].wait()
    local[1].wait()
    row_limit = [rows_s[v] for v in range(videos)]
    col_limit = [cols_s[v] for v in range(videos)]

    def mask_into(src, at, r, fs, shift):
        for v in range(videos):
            row = band + r - 1
            keep = (col_in < col_limit[v]) & ((row >= 0) & (row < row_limit[v]))
            for f in fs:
                cell = src[v, f] if at is None else src[v, f, at]
                xm[r, v, (f + shift) * cols : (f + shift + 1) * cols] = jnp.where(keep, cell, jnp.zeros_like(cell))

    every = range(frames)
    local[2].wait()
    for r in range(rows):
        mask_into(x, r, r + 1, every, old)

    third = taps // 3

    def own_cells(a, r):
        return [xm[r, v, a * cols : a * cols + seg] for v in range(videos)]

    def product(bs, frame_taps, targets, add=False):
        pieces = [(a, b) for a in frame_taps for b in bs]
        lhs = jnp.concatenate([w1[a, b * third : (b + 1) * third] for a, b in pieces], axis=-1)
        rhs = jnp.concatenate(
            [
                jnp.concatenate([cell for _, at in targets for cell in own_cells(a, at + b // 2)], axis=0)
                for a, b in pieces
            ],
            axis=-1,
        )
        res = nt(lhs, rhs)
        for n, (dst, at) in enumerate(targets):
            val = res[:, n * lanes : (n + 1) * lanes]
            dst[at] = dst[at] + val if add else val

    both, mid = (0, 2), (1,)

    lane = lax.broadcasted_iota(jnp.int32, (1, lanes), 1)
    lane_col = lane % cols
    first_col = lane_col == 0
    last_col = lane_col == cols - 1
    lane_rows, lane_cols = row_limit[0], col_limit[0]
    for v in range(1, videos):
        lane_rows = jnp.where(lane >= v * seg, row_limit[v], lane_rows)
        lane_cols = jnp.where(lane >= v * seg, col_limit[v], lane_cols)
    keep_col = lane_col < lane_cols
    split = old * cols
    early = lane % seg

    def gate(shared, middle, keep):
        s0, s1, s2 = [shared[c * outs : (c + 1) * outs] + middle[c * outs : (c + 1) * outs] for c in range(3)]
        joint = s0 + jnp.where(last_col, 0.0, pltpu.roll(s2, lanes - 1, 1))
        planes = []
        for hidden in (jnp.where(first_col, s2, pltpu.roll(joint, 1, 1)) + s1, joint + s1):
            mean = jnp.sum(hidden * hidden, axis=0, keepdims=True) * (1.0 / outs)
            scale = jnp.where(keep, lax.rsqrt(mean + 1e-06), 0.0)
            normed = hidden * scale * gain_c[...]
            planes.append(normed + normed * jnp.tanh(normed))
        even, odd = planes
        before = jnp.where(first_col, 0.0, pltpu.roll(odd, 1, 1))
        after = jnp.where(last_col, 0.0, pltpu.roll(even, lanes - 1, 1))
        return before, even, odd, after

    def gate_own(i):
        row = band * 2 + i - 1
        keep = keep_col & ((row >= 0) & (row < 2 * lane_rows))
        for at, plane in enumerate(gate(t_own[i // 2], m_own[(i + 1) // 2], keep)):
            g_own[i, at] = plane.astype(BF)
        even, odd = g_own[i, 1], g_own[i, 2]
        g_pack[i] = jnp.where(early < split, pltpu.roll(even, lanes - split, 1), odd)

    def swap(plane):
        return jnp.where(early < split, pltpu.roll(plane, lanes - split, 1), pltpu.roll(plane, split, 1))

    def old_planes(i):
        packed = g_recv[i]
        none = jnp.zeros_like(packed)
        before = jnp.where(first_col, none, pltpu.roll(packed, 1, 1))
        after = jnp.where(last_col, none, pltpu.roll(packed, lanes - 1, 1))
        g_old[0, i] = swap(jnp.where(early < split, packed, before))
        g_old[1, i] = swap(jnp.where(early < split, after, packed))

    def later(plane):
        return jnp.where(early < cols, 0.0, pltpu.roll(plane, cols, 1))

    def own_taps(l):
        rhs = jnp.concatenate(
            [
                jnp.concatenate([g_own[2 * l + s + b, PLANES[p][c]] for s in range(2) for p in range(2)], axis=1)
                for b in range(3)
                for c in range(3)
            ],
            axis=0,
        )
        res = jnp.dot(w2t[...], rhs, preferred_element_type=F32)
        for n in range(4):
            by_tap = [res[a * outs : (a + 1) * outs, n * lanes : (n + 1) * lanes] for a in range(3)]
            totals[l, n] = by_tap[2] + later(by_tap[1] + later(by_tap[0]))

    def old_taps(ls):
        def plane(i, c):
            return g_recv[i] if c == 1 else g_old[c // 2, i]

        rhs = jnp.concatenate(
            [
                jnp.concatenate([plane(2 * l + s + b, c) for l in ls for s in range(2)], axis=1)
                for b in range(3)
                for c in range(3)
            ],
            axis=0,
        )
        res = jnp.dot(w2t[: 2 * outs], rhs, preferred_element_type=F32)
        added = {}
        for n in range(2 * len(ls)):
            oldest, newer = [res[a * outs : (a + 1) * outs, n * lanes : (n + 1) * lanes] for a in range(2)]
            both_taps = oldest + jnp.where(early % split < cols, pltpu.roll(newer, lanes - cols, 1), 0.0)
            for p, part in enumerate((both_taps, pltpu.roll(both_taps, lanes - split, 1))):
                added[ls[n // 2], 2 * (n % 2) + p] = jnp.where(early < split, part, 0.0)
        return added

    def finish(l, added):
        residual = short[:, l * lanes : (l + 1) * lanes]
        for s in range(2):
            row = 2 * (band + l) + s
            keep = keep_col & (row < 2 * lane_rows)
            for p in range(2):
                whole = totals[l, 2 * s + p] + residual + added[l, 2 * s + p]
                out_v[2 * l + s, :, p * lanes : (p + 1) * lanes] = jnp.where(keep, whole, 0.0).astype(BF)

    def result(l):
        at = pl.ds(2 * l, 2)
        return pltpu.make_async_copy(out_v.at[at], out_ref.at[at], out_sem.at[l])

    def leave(l):
        result(l).start()

    own_shared = [(t_own, l) for l in range(1, rows)]
    own_middle = [(m_own, r) for r in range(1, rows + 1)]
    local[4].wait()
    local[5].wait()
    product(both, (2,), own_shared)
    product(mid, (2,), own_middle)
    local[3].wait()
    gain_c[...] = jnp.broadcast_to(0.5 * gain_row[...], (lanes, outs)).T
    short[...] = nt(
        ws[...],
        jnp.concatenate([piece for r in range(rows) for piece in own_cells(2, r + 1)], axis=0),
    )
    local[6].wait()
    step = 3 * 128
    for a in range(3):
        for k in range(0, taps, step):
            size = min(step, taps - k)
            w2t[a * outs : (a + 1) * outs, k : k + size] = w2[a * taps + k : a * taps + k + size].T
    local[7].wait()

    for a, k in ((1, 0), (0, 8)):
        arrive(k)
        for r in range(rows):
            mask_into(prev, r, r + 1, (a,), 0)
        if a == 0:
            start(3)
            start(4)
        product(both, (a,), own_shared, add=True)
        product(mid, (a,), own_middle, add=True)

    center = range(2, 2 * rows)
    for i in center[:4]:
        gate_own(i)
    own_taps(1)
    for i in center[4:]:
        gate_own(i)
    start(5)

    for k in range(1, 5):
        arrive(k)
    for src, psrc, r in ((top, ptop, 0), (bot, pbot, ext - 1)):
        mask_into(src, None, r, every, old)
        mask_into(psrc, None, r, range(old), 0)
    product(both, range(3), [(t_own, 0), (t_own, rows)])
    product(mid, range(3), [(m_own, 0), (m_own, ext - 1)])
    edges = (0, 1, 2 * rows, 2 * rows + 1)
    for i in edges:
        gate_own(i)
    own_taps(2)
    start(6)
    start(7)

    arrive(5)
    own_taps(0)
    for i in center:
        old_planes(i)
    own_taps(3)

    arrive(6)
    arrive(7)
    for i in edges:
        old_planes(i)
    added = {**old_taps((1, 2)), **old_taps((0, 3))}
    for l in (1, 2, 0):
        finish(l, added)
    leave(1)
    leave(2)
    leave(0)
    finish(3, added)
    leave(3)
    for l in range(rows):
        result(l).wait()

    for there, copy in sends:

        @pl.when(there)
        def _():
            copy.wait_send()


def arrange(sums_ref, out_ref, sums, out_v, in_sem, out_sem):
    videos, frames, high, wide, outs = out_ref.shape
    cells = sums.shape[-1]
    steps = high // 2

    def fetch(l):
        at = pl.ds(2 * l, 2)
        return pltpu.make_async_copy(sums_ref.at[at], sums.at[at], in_sem.at[l])

    def result(l):
        at = pl.ds(2 * l, 2)
        return pltpu.make_async_copy(out_v.at[:, :, at], out_ref.at[:, :, at], out_sem.at[l])

    for l in range(steps):
        fetch(l).start()
    place = lax.broadcasted_iota(jnp.int32, (cells, cells), 0)
    taken = lax.broadcasted_iota(jnp.int32, (cells, cells), 1)
    perm = (taken == (place % 2) * (cells // 2) + place // 2).astype(BF)
    for l in range(steps):
        fetch(l).wait()
        for row in range(2 * l, 2 * l + 2):
            out_v[:, :, row] = nt(perm, sums[row]).astype(BF).reshape(videos, frames, wide, outs)
        result(l).start()
    for l in range(steps):
        result(l).wait()


def shards(tm, height, latents, conv_in, conv_out, shortcut, norm_gain, video_rows, video_cols):
    videos, frames, rows, cols, chans = latents.shape
    outs = conv_in.shape[-1]
    ext = rows + 2
    lanes = videos * frames * cols
    taps = 9 * outs
    depth = 27 * outs
    old = 2
    anywhere = pl.BlockSpec(memory_space=pl.ANY)
    sums = pl.pallas_call(
        functools.partial(section, tm, height),
        out_shape=jax.ShapeDtypeStruct((2 * rows, outs, 2 * lanes), BF),
        in_specs=[anywhere] * 7,
        out_specs=anywhere,
        scratch_shapes=[
            pltpu.VMEM((videos, frames, rows, cols, chans), BF),
            pltpu.VMEM((videos, old, rows, cols, chans), BF),
            pltpu.VMEM((videos, frames, cols, chans), BF),
            pltpu.VMEM((videos, frames, cols, chans), BF),
            pltpu.VMEM((videos, old, cols, chans), BF),
            pltpu.VMEM((videos, old, cols, chans), BF),
            pltpu.VMEM((3, taps, chans), BF),
            pltpu.VMEM((depth, outs), BF),
            pltpu.VMEM((outs, chans), BF),
            pltpu.VMEM((1, outs), F32),
            pltpu.SMEM((videos,), jnp.int32),
            pltpu.SMEM((videos,), jnp.int32),
            pltpu.VMEM((3 * outs, taps), BF),
            pltpu.VMEM((outs, lanes), F32),
            pltpu.VMEM((ext, videos, (frames + old) * cols, chans), BF),
            pltpu.VMEM((ext - 1, 3 * outs, lanes), F32),
            pltpu.VMEM((ext, 3 * outs, lanes), F32),
            pltpu.VMEM((2 * rows + 2, 4, outs, lanes), BF),
            pltpu.VMEM((2 * rows + 2, outs, lanes), BF),
            pltpu.VMEM((2 * rows + 2, outs, lanes), BF),
            pltpu.VMEM((2, 2 * rows + 2, outs, lanes), BF),
            pltpu.VMEM((rows, 4, outs, lanes), F32),
            pltpu.VMEM((outs, rows * lanes), F32),
            pltpu.VMEM((2 * rows, outs, 2 * lanes), BF),
            pltpu.SemaphoreType.DMA((rows,)),
            pltpu.SemaphoreType.DMA((8,)),
            pltpu.SemaphoreType.DMA((9,)),
            pltpu.SemaphoreType.DMA((9,)),
        ],
        compiler_params=pltpu.CompilerParams(
            collective_id=0, has_side_effects=True, vmem_limit_bytes=56 << 20
        ),
    )(
        latents,
        jnp.swapaxes(conv_in, 3, 4).reshape(3, taps, chans),
        conv_out.reshape(depth, outs),
        shortcut.T,
        norm_gain.reshape(1, outs),
        video_rows,
        video_cols,
    )
    shape = (videos, frames, 2 * rows, 2 * cols, outs)
    return pl.pallas_call(
        arrange,
        out_shape=jax.ShapeDtypeStruct(shape, BF),
        in_specs=[anywhere],
        out_specs=anywhere,
        scratch_shapes=[
            pltpu.VMEM((2 * rows, outs, 2 * lanes), BF),
            pltpu.VMEM(shape, BF),
            pltpu.SemaphoreType.DMA((rows,)),
            pltpu.SemaphoreType.DMA((rows,)),
        ],
        compiler_params=pltpu.CompilerParams(vmem_limit_bytes=56 << 20),
    )(sums)


def solution(mesh):
    in_specs = (P(None, "tm", "height", None, None), P(), P(), P(), P(), P(), P())
    out_specs = P(None, "tm", "height", None, None)
    return jax.shard_map(
        functools.partial(shards, mesh.shape["tm"], mesh.shape["height"]),
        mesh=mesh,
        in_specs=in_specs,
        out_specs=out_specs,
        check_vma=False,
    )
```

```python
import functools

import jax
import jax.numpy as jnp
from jax import lax
from jax.experimental import pallas as pl
from jax.experimental.pallas import tpu as pltpu
from jax.sharding import PartitionSpec as P

BF = jnp.bfloat16
F32 = jnp.float32
NT = (((1,), (1,)), ((), ()))
PLANES = ((0, 1, 2), (1, 2, 3))


def nt(lhs, rhs):
    return lax.dot_general(lhs, rhs, NT, preferred_element_type=F32)


def section(
    tm,
    height,
    lat,
    w1_hbm,
    w2_hbm,
    ws_hbm,
    gain_hbm,
    rows_hbm,
    cols_hbm,
    out_ref,
    x,
    prev,
    top,
    bot,
    ptop,
    pbot,
    w1,
    w2,
    ws,
    gain_row,
    rows_s,
    cols_s,
    w2t,
    gain_c,
    xm,
    t_own,
    m_own,
    g_own,
    g_pack,
    g_recv,
    g_old,
    totals,
    short,
    out_v,
    out_sem,
    local_sem,
    send_sem,
    recv_sem,
):
    videos, frames, rows, cols, chans = lat.shape
    outs = ws.shape[0]
    taps = 9 * outs
    ext = rows + 2
    lanes = videos * frames * cols
    seg = frames * cols
    ti = lax.axis_index("tm")
    hi = lax.axis_index("height")
    has_up, has_down = hi > 0, hi < height - 1
    has_prev, has_next = ti > 0, ti < tm - 1

    local = [
        pltpu.make_async_copy(src, dst, local_sem.at[k])
        for k, (src, dst) in enumerate(
            (
                (rows_hbm, rows_s),
                (cols_hbm, cols_s),
                (lat, x),
                (gain_hbm, gain_row),
                (ws_hbm, ws),
                (w1_hbm.at[2], w1.at[2]),
                (w2_hbm, w2),
                (w1_hbm.at[:2], w1.at[:2]),
            )
        )
    ]
    def remote(k, src, dst, t, h):
        return pltpu.make_async_remote_copy(
            src_ref=src,
            dst_ref=dst,
            send_sem=send_sem.at[k],
            recv_sem=recv_sem.at[k],
            device_id=(t, h),
            device_id_type=pl.DeviceIdType.MESH,
        )

    old = prev.shape[1]
    head = pl.ds(2, 2 * rows - 2)
    low, high = pl.ds(0, 2), pl.ds(2 * rows, 2)
    sends = (
        (has_next, remote(0, lat.at[:, frames - 1], prev.at[:, old - 1], ti + 1, hi)),
        (has_down, remote(1, lat.at[:, :, rows - 1], top, ti, hi + 1)),
        (has_up, remote(2, lat.at[:, :, 0], bot, ti, hi - 1)),
        (has_prev & has_down, remote(3, prev.at[:, :, rows - 1], ptop, ti, hi + 1)),
        (has_prev & has_up, remote(4, prev.at[:, :, 0], pbot, ti, hi - 1)),
        (has_next, remote(5, g_pack.at[head], g_recv.at[head], ti + 1, hi)),
        (has_next, remote(6, g_pack.at[low], g_recv.at[low], ti + 1, hi)),
        (has_next, remote(7, g_pack.at[high], g_recv.at[high], ti + 1, hi)),
        (has_next, remote(8, lat.at[:, frames - 2], prev.at[:, old - 2], ti + 1, hi)),
    )
    after_me = (has_prev, ti - 1, hi)
    senders = (
        after_me,
        (has_up, ti, hi - 1),
        (has_down, ti, hi + 1),
        (has_prev & has_up, ti, hi - 1),
        (has_prev & has_down, ti, hi + 1),
    ) + (after_me,) * 4
    barrier = pltpu.get_barrier_semaphore()
    for there, t, h in senders[:3]:

        @pl.when(there)
        def _():
            pl.semaphore_signal(barrier, inc=1, device_id=(t, h), device_id_type=pl.DeviceIdType.MESH)

    for copy in local[:6]:
        copy.start()
    pl.semaphore_wait(barrier, sum(there.astype(jnp.int32) for there, _ in sends[:3]))

    def start(k):
        @pl.when(sends[k][0])
        def _():
            sends[k][1].start()

    for k in (0, 8, 1, 2):
        start(k)
    for copy in local[6:]:
        copy.start()

    landing = (
        prev.at[:, old - 1],
        top,
        bot,
        ptop,
        pbot,
        g_recv.at[head],
        g_recv.at[low],
        g_recv.at[high],
        prev.at[:, old - 2],
    )

    def arrive(k):
        there = senders[k][0]

        @pl.when(there)
        def _():
            sends[k][1].wait_recv()

        @pl.when(jnp.logical_not(there))
        def _():
            landing[k][...] = jnp.zeros(landing[k].shape, BF)

    col_in = lax.broadcasted_iota(jnp.int32, (cols, 1), 0)
    band = hi * rows
    local[0].wait()
    local[1].wait()
    row_limit = [rows_s[v] for v in range(videos)]
    col_limit = [cols_s[v] for v in range(videos)]

    def mask_into(src, at, r, fs, shift):
        for v in range(videos):
            row = band + r - 1
            keep = (col_in < col_limit[v]) & ((row >= 0) & (row < row_limit[v]))
            for f in fs:
                cell = src[v, f] if at is None else src[v, f, at]
                xm[r, v, (f + shift) * cols : (f + shift + 1) * cols] = jnp.where(keep, cell, jnp.zeros_like(cell))

    every = range(frames)
    local[2].wait()
    for r in range(rows):
        mask_into(x, r, r + 1, every, old)

    third = taps // 3

    def own_cells(a, r):
        return [xm[r, v, a * cols : a * cols + seg] for v in range(videos)]

    def product(bs, frame_taps, targets, add=False):
        pieces = [(a, b) for a in frame_taps for b in bs]
        lhs = jnp.concatenate([w1[a, b * third : (b + 1) * third] for a, b in pieces], axis=-1)
        rhs = jnp.concatenate(
            [
                jnp.concatenate([cell for _, at in targets for cell in own_cells(a, at + b // 2)], axis=0)
                for a, b in pieces
            ],
            axis=-1,
        )
        res = nt(lhs, rhs)
        for n, (dst, at) in enumerate(targets):
            val = res[:, n * lanes : (n + 1) * lanes]
            dst[at] = dst[at] + val if add else val

    both, mid = (0, 2), (1,)

    lane = lax.broadcasted_iota(jnp.int32, (1, lanes), 1)
    lane_col = lane % cols
    first_col = lane_col == 0
    last_col = lane_col == cols - 1
    lane_rows, lane_cols = row_limit[0], col_limit[0]
    for v in range(1, videos):
        lane_rows = jnp.where(lane >= v * seg, row_limit[v], lane_rows)
        lane_cols = jnp.where(lane >= v * seg, col_limit[v], lane_cols)
    keep_col = lane_col < lane_cols
    split = old * cols
    early = lane % seg

    def gate(shared, middle, keep):
        s0, s1, s2 = [shared[c * outs : (c + 1) * outs] + middle[c * outs : (c + 1) * outs] for c in range(3)]
        joint = s0 + jnp.where(last_col, 0.0, pltpu.roll(s2, lanes - 1, 1))
        planes = []
        for hidden in (jnp.where(first_col, s2, pltpu.roll(joint, 1, 1)) + s1, joint + s1):
            mean = jnp.sum(hidden * hidden, axis=0, keepdims=True) * (1.0 / outs)
            scale = jnp.where(keep, lax.rsqrt(mean + 1e-06), 0.0)
            normed = hidden * scale * gain_c[...]
            planes.append(normed + normed * jnp.tanh(normed))
        even, odd = planes
        before = jnp.where(first_col, 0.0, pltpu.roll(odd, 1, 1))
        after = jnp.where(last_col, 0.0, pltpu.roll(even, lanes - 1, 1))
        return before, even, odd, after

    def gate_own(i):
        row = band * 2 + i - 1
        keep = keep_col & ((row >= 0) & (row < 2 * lane_rows))
        for at, plane in enumerate(gate(t_own[i // 2], m_own[(i + 1) // 2], keep)):
            g_own[i, at] = plane.astype(BF)
        even, odd = g_own[i, 1], g_own[i, 2]
        g_pack[i] = jnp.where(early < split, pltpu.roll(even, lanes - split, 1), odd)

    def swap(plane):
        return jnp.where(early < split, pltpu.roll(plane, lanes - split, 1), pltpu.roll(plane, split, 1))

    def old_planes(i):
        packed = g_recv[i]
        none = jnp.zeros_like(packed)
        before = jnp.where(first_col, none, pltpu.roll(packed, 1, 1))
        after = jnp.where(last_col, none, pltpu.roll(packed, lanes - 1, 1))
        g_old[0, i] = swap(jnp.where(early < split, packed, before))
        g_old[1, i] = swap(jnp.where(early < split, after, packed))

    def later(plane):
        return jnp.where(early < cols, 0.0, pltpu.roll(plane, cols, 1))

    def own_taps(l):
        rhs = jnp.concatenate(
            [
                jnp.concatenate([g_own[2 * l + s + b, PLANES[p][c]] for s in range(2) for p in range(2)], axis=1)
                for b in range(3)
                for c in range(3)
            ],
            axis=0,
        )
        res = jnp.dot(w2t[...], rhs, preferred_element_type=F32)
        for n in range(4):
            by_tap = [res[a * outs : (a + 1) * outs, n * lanes : (n + 1) * lanes] for a in range(3)]
            totals[l, n] = by_tap[2] + later(by_tap[1] + later(by_tap[0]))

    def old_taps(ls):
        def plane(i, c):
            return g_recv[i] if c == 1 else g_old[c // 2, i]

        rhs = jnp.concatenate(
            [
                jnp.concatenate([plane(2 * l + s + b, c) for l in ls for s in range(2)], axis=1)
                for b in range(3)
                for c in range(3)
            ],
            axis=0,
        )
        res = jnp.dot(w2t[: 2 * outs], rhs, preferred_element_type=F32)
        added = {}
        for n in range(2 * len(ls)):
            oldest, newer = [res[a * outs : (a + 1) * outs, n * lanes : (n + 1) * lanes] for a in range(2)]
            both_taps = oldest + jnp.where(early % split < cols, pltpu.roll(newer, lanes - cols, 1), 0.0)
            for p, part in enumerate((both_taps, pltpu.roll(both_taps, lanes - split, 1))):
                added[ls[n // 2], 2 * (n % 2) + p] = jnp.where(early < split, part, 0.0)
        return added

    def finish(l, added):
        residual = short[:, l * lanes : (l + 1) * lanes]
        for s in range(2):
            row = 2 * (band + l) + s
            keep = keep_col & (row < 2 * lane_rows)
            for p in range(2):
                whole = totals[l, 2 * s + p] + residual + added[l, 2 * s + p]
                out_v[2 * l + s, :, p * lanes : (p + 1) * lanes] = jnp.where(keep, whole, 0.0).astype(BF)

    def result(l):
        at = pl.ds(2 * l, 2)
        return pltpu.make_async_copy(out_v.at[at], out_ref.at[at], out_sem.at[l])

    def leave(l):
        result(l).start()

    own_shared = [(t_own, l) for l in range(1, rows)]
    own_middle = [(m_own, r) for r in range(1, rows + 1)]
    local[4].wait()
    local[5].wait()
    product(both, (2,), own_shared)
    product(mid, (2,), own_middle)
    local[3].wait()
    gain_c[...] = jnp.broadcast_to(0.5 * gain_row[...], (lanes, outs)).T
    short[...] = nt(
        ws[...],
        jnp.concatenate([piece for r in range(rows) for piece in own_cells(2, r + 1)], axis=0),
    )
    local[6].wait()
    step = 3 * 128
    for a in range(3):
        for k in range(0, taps, step):
            size = min(step, taps - k)
            w2t[a * outs : (a + 1) * outs, k : k + size] = w2[a * taps + k : a * taps + k + size].T
    local[7].wait()

    for a, k in ((1, 0), (0, 8)):
        arrive(k)
        for r in range(rows):
            mask_into(prev, r, r + 1, (a,), 0)
        if a == 0:
            start(3)
            start(4)
        product(both, (a,), own_shared, add=True)
        product(mid, (a,), own_middle, add=True)

    center = range(2, 2 * rows)
    for i in center[:4]:
        gate_own(i)
    own_taps(1)
    for i in center[4:]:
        gate_own(i)
    start(5)

    edge_shared, edge_middle = [(t_own, 0), (t_own, rows)], [(m_own, 0), (m_own, ext - 1)]
    arrive(1)
    arrive(2)
    for src, r in ((top, 0), (bot, ext - 1)):
        mask_into(src, None, r, every, old)
    product(both, (2,), edge_shared)
    product(mid, (2,), edge_middle)
    arrive(3)
    arrive(4)
    for psrc, r in ((ptop, 0), (pbot, ext - 1)):
        mask_into(psrc, None, r, range(old), 0)
    product(both, (0, 1), edge_shared, add=True)
    product(mid, (0, 1), edge_middle, add=True)
    edges = (0, 1, 2 * rows, 2 * rows + 1)
    for i in edges:
        gate_own(i)
    own_taps(2)
    start(6)
    start(7)

    arrive(5)
    own_taps(0)
    for i in center:
        old_planes(i)
    own_taps(3)

    arrive(6)
    arrive(7)
    for i in edges:
        old_planes(i)
    added = {**old_taps((1, 2)), **old_taps((0, 3))}
    for l in (1, 2, 0):
        finish(l, added)
    leave(1)
    leave(2)
    leave(0)
    finish(3, added)
    leave(3)
    for l in range(rows):
        result(l).wait()

    for there, copy in sends:

        @pl.when(there)
        def _():
            copy.wait_send()


def arrange(sums_ref, out_ref, sums, out_v, in_sem, out_sem):
    videos, frames, high, wide, outs = out_ref.shape
    cells = sums.shape[-1]

    def fetch(l):
        at = pl.ds(2 * l, 2)
        return pltpu.make_async_copy(sums_ref.at[at], sums.at[at], in_sem.at[l])

    def result(row):
        return pltpu.make_async_copy(out_v.at[:, :, row], out_ref.at[:, :, row], out_sem.at[row])

    for l in range(high // 2):
        fetch(l).start()
    place = lax.broadcasted_iota(jnp.int32, (cells, cells), 0)
    taken = lax.broadcasted_iota(jnp.int32, (cells, cells), 1)
    perm = (taken == (place % 2) * (cells // 2) + place // 2).astype(BF)
    for row in range(high):
        if row % 2 == 0:
            fetch(row // 2).wait()
        out_v[:, :, row] = nt(perm, sums[row]).astype(BF).reshape(videos, frames, wide, outs)
        result(row).start()
    for row in range(high):
        result(row).wait()


def shards(tm, height, latents, conv_in, conv_out, shortcut, norm_gain, video_rows, video_cols):
    videos, frames, rows, cols, chans = latents.shape
    outs = conv_in.shape[-1]
    ext = rows + 2
    lanes = videos * frames * cols
    taps = 9 * outs
    depth = 27 * outs
    old = 2
    anywhere = pl.BlockSpec(memory_space=pl.ANY)
    sums = pl.pallas_call(
        functools.partial(section, tm, height),
        out_shape=jax.ShapeDtypeStruct((2 * rows, outs, 2 * lanes), BF),
        in_specs=[anywhere] * 7,
        out_specs=anywhere,
        scratch_shapes=[
            pltpu.VMEM((videos, frames, rows, cols, chans), BF),
            pltpu.VMEM((videos, old, rows, cols, chans), BF),
            pltpu.VMEM((videos, frames, cols, chans), BF),
            pltpu.VMEM((videos, frames, cols, chans), BF),
            pltpu.VMEM((videos, old, cols, chans), BF),
            pltpu.VMEM((videos, old, cols, chans), BF),
            pltpu.VMEM((3, taps, chans), BF),
            pltpu.VMEM((depth, outs), BF),
            pltpu.VMEM((outs, chans), BF),
            pltpu.VMEM((1, outs), F32),
            pltpu.SMEM((videos,), jnp.int32),
            pltpu.SMEM((videos,), jnp.int32),
            pltpu.VMEM((3 * outs, taps), BF),
            pltpu.VMEM((outs, lanes), F32),
            pltpu.VMEM((ext, videos, (frames + old) * cols, chans), BF),
            pltpu.VMEM((ext - 1, 3 * outs, lanes), F32),
            pltpu.VMEM((ext, 3 * outs, lanes), F32),
            pltpu.VMEM((2 * rows + 2, 4, outs, lanes), BF),
            pltpu.VMEM((2 * rows + 2, outs, lanes), BF),
            pltpu.VMEM((2 * rows + 2, outs, lanes), BF),
            pltpu.VMEM((2, 2 * rows + 2, outs, lanes), BF),
            pltpu.VMEM((rows, 4, outs, lanes), F32),
            pltpu.VMEM((outs, rows * lanes), F32),
            pltpu.VMEM((2 * rows, outs, 2 * lanes), BF),
            pltpu.SemaphoreType.DMA((rows,)),
            pltpu.SemaphoreType.DMA((8,)),
            pltpu.SemaphoreType.DMA((9,)),
            pltpu.SemaphoreType.DMA((9,)),
        ],
        compiler_params=pltpu.CompilerParams(
            collective_id=0, has_side_effects=True, vmem_limit_bytes=56 << 20
        ),
    )(
        latents,
        jnp.swapaxes(conv_in, 3, 4).reshape(3, taps, chans),
        conv_out.reshape(depth, outs),
        shortcut.T,
        norm_gain.reshape(1, outs),
        video_rows,
        video_cols,
    )
    shape = (videos, frames, 2 * rows, 2 * cols, outs)
    return pl.pallas_call(
        arrange,
        out_shape=jax.ShapeDtypeStruct(shape, BF),
        in_specs=[anywhere],
        out_specs=anywhere,
        scratch_shapes=[
            pltpu.VMEM((2 * rows, outs, 2 * lanes), BF),
            pltpu.VMEM(shape, BF),
            pltpu.SemaphoreType.DMA((rows,)),
            pltpu.SemaphoreType.DMA((2 * rows,)),
        ],
        compiler_params=pltpu.CompilerParams(vmem_limit_bytes=56 << 20),
    )(sums)


def solution(mesh):
    in_specs = (P(None, "tm", "height", None, None), P(), P(), P(), P(), P(), P())
    out_specs = P(None, "tm", "height", None, None)
    return jax.shard_map(
        functools.partial(shards, mesh.shape["tm"], mesh.shape["height"]),
        mesh=mesh,
        in_specs=in_specs,
        out_specs=out_specs,
        check_vma=False,
    )
```

```python
import functools

import jax
import jax.numpy as jnp
from jax import lax
from jax.experimental import pallas as pl
from jax.experimental.pallas import tpu as pltpu
from jax.sharding import PartitionSpec as P

BF = jnp.bfloat16
F32 = jnp.float32
NT = (((1,), (1,)), ((), ()))
PLANES = ((0, 1, 2), (1, 2, 3))


def nt(lhs, rhs):
    return lax.dot_general(lhs, rhs, NT, preferred_element_type=F32)


def section(
    tm,
    height,
    lat,
    w1_hbm,
    w2_hbm,
    ws_hbm,
    gain_hbm,
    rows_hbm,
    cols_hbm,
    out_ref,
    x,
    prev,
    top,
    bot,
    ptop,
    pbot,
    w1,
    w2,
    ws,
    gain_row,
    rows_s,
    cols_s,
    w2t,
    gain_c,
    xm,
    t_own,
    m_own,
    g_own,
    g_pack,
    g_recv,
    g_old,
    totals,
    short,
    out_v,
    out_sem,
    local_sem,
    send_sem,
    recv_sem,
):
    videos, frames, rows, cols, chans = lat.shape
    outs = ws.shape[0]
    taps = 9 * outs
    ext = rows + 2
    lanes = videos * frames * cols
    seg = frames * cols
    ti = lax.axis_index("tm")
    hi = lax.axis_index("height")
    has_up, has_down = hi > 0, hi < height - 1
    has_prev, has_next = ti > 0, ti < tm - 1

    local = [
        pltpu.make_async_copy(src, dst, local_sem.at[k])
        for k, (src, dst) in enumerate(
            (
                (rows_hbm, rows_s),
                (cols_hbm, cols_s),
                (lat, x),
                (gain_hbm, gain_row),
                (ws_hbm, ws),
                (w1_hbm.at[2], w1.at[2]),
                (w2_hbm, w2),
                (w1_hbm.at[:2], w1.at[:2]),
            )
        )
    ]
    def remote(k, src, dst, t, h):
        return pltpu.make_async_remote_copy(
            src_ref=src,
            dst_ref=dst,
            send_sem=send_sem.at[k],
            recv_sem=recv_sem.at[k],
            device_id=(t, h),
            device_id_type=pl.DeviceIdType.MESH,
        )

    old = prev.shape[1]
    head = pl.ds(2, 2 * rows - 2)
    low, high = pl.ds(0, 2), pl.ds(2 * rows, 2)
    sends = (
        (has_next, remote(0, lat.at[:, frames - 1], prev.at[:, old - 1], ti + 1, hi)),
        (has_down, remote(1, lat.at[:, :, rows - 1], top, ti, hi + 1)),
        (has_up, remote(2, lat.at[:, :, 0], bot, ti, hi - 1)),
        (has_prev & has_down, remote(3, prev.at[:, :, rows - 1], ptop, ti, hi + 1)),
        (has_prev & has_up, remote(4, prev.at[:, :, 0], pbot, ti, hi - 1)),
        (has_next, remote(5, g_pack.at[head], g_recv.at[head], ti + 1, hi)),
        (has_next, remote(6, g_pack.at[low], g_recv.at[low], ti + 1, hi)),
        (has_next, remote(7, g_pack.at[high], g_recv.at[high], ti + 1, hi)),
        (has_next, remote(8, lat.at[:, frames - 2], prev.at[:, old - 2], ti + 1, hi)),
    )
    after_me = (has_prev, ti - 1, hi)
    senders = (
        after_me,
        (has_up, ti, hi - 1),
        (has_down, ti, hi + 1),
        (has_prev & has_up, ti, hi - 1),
        (has_prev & has_down, ti, hi + 1),
    ) + (after_me,) * 4
    barrier = pltpu.get_barrier_semaphore()
    for there, t, h in senders[:3]:

        @pl.when(there)
        def _():
            pl.semaphore_signal(barrier, inc=1, device_id=(t, h), device_id_type=pl.DeviceIdType.MESH)

    for copy in local[:6]:
        copy.start()
    pl.semaphore_wait(barrier, sum(there.astype(jnp.int32) for there, _ in sends[:3]))

    def start(k):
        @pl.when(sends[k][0])
        def _():
            sends[k][1].start()

    for k in (0, 8, 1, 2):
        start(k)
    for copy in local[6:]:
        copy.start()

    landing = (
        prev.at[:, old - 1],
        top,
        bot,
        ptop,
        pbot,
        g_recv.at[head],
        g_recv.at[low],
        g_recv.at[high],
        prev.at[:, old - 2],
    )

    def arrive(k):
        there = senders[k][0]

        @pl.when(there)
        def _():
            sends[k][1].wait_recv()

        @pl.when(jnp.logical_not(there))
        def _():
            landing[k][...] = jnp.zeros(landing[k].shape, BF)

    col_in = lax.broadcasted_iota(jnp.int32, (cols, 1), 0)
    band = hi * rows
    local[0].wait()
    local[1].wait()
    row_limit = [rows_s[v] for v in range(videos)]
    col_limit = [cols_s[v] for v in range(videos)]

    def mask_into(src, at, r, fs, shift):
        for v in range(videos):
            row = band + r - 1
            keep = (col_in < col_limit[v]) & ((row >= 0) & (row < row_limit[v]))
            for f in fs:
                cell = src[v, f] if at is None else src[v, f, at]
                xm[r, v, (f + shift) * cols : (f + shift + 1) * cols] = jnp.where(keep, cell, jnp.zeros_like(cell))

    every = range(frames)
    local[2].wait()
    for r in range(rows):
        mask_into(x, r, r + 1, every, old)

    third = taps // 3

    def own_cells(a, r):
        return [xm[r, v, a * cols : a * cols + seg] for v in range(videos)]

    def product(bs, frame_taps, targets, add=False):
        pieces = [(a, b) for a in frame_taps for b in bs]
        lhs = jnp.concatenate([w1[a, b * third : (b + 1) * third] for a, b in pieces], axis=-1)
        rhs = jnp.concatenate(
            [
                jnp.concatenate([cell for _, at in targets for cell in own_cells(a, at + b // 2)], axis=0)
                for a, b in pieces
            ],
            axis=-1,
        )
        res = nt(lhs, rhs)
        for n, (dst, at) in enumerate(targets):
            val = res[:, n * lanes : (n + 1) * lanes]
            dst[at] = dst[at] + val if add else val

    both, mid = (0, 2), (1,)

    lane = lax.broadcasted_iota(jnp.int32, (1, lanes), 1)
    lane_col = lane % cols
    first_col = lane_col == 0
    last_col = lane_col == cols - 1
    lane_rows, lane_cols = row_limit[0], col_limit[0]
    for v in range(1, videos):
        lane_rows = jnp.where(lane >= v * seg, row_limit[v], lane_rows)
        lane_cols = jnp.where(lane >= v * seg, col_limit[v], lane_cols)
    keep_col = lane_col < lane_cols
    split = old * cols
    early = lane % seg

    def gate(shared, middle, keep):
        s0, s1, s2 = [shared[c * outs : (c + 1) * outs] + middle[c * outs : (c + 1) * outs] for c in range(3)]
        joint = s0 + jnp.where(last_col, 0.0, pltpu.roll(s2, lanes - 1, 1))
        planes = []
        for hidden in (jnp.where(first_col, s2, pltpu.roll(joint, 1, 1)) + s1, joint + s1):
            mean = jnp.sum(hidden * hidden, axis=0, keepdims=True) * (1.0 / outs)
            scale = jnp.where(keep, lax.rsqrt(mean + 1e-06), 0.0)
            normed = hidden * scale * gain_c[...]
            planes.append(normed + normed * jnp.tanh(normed))
        even, odd = planes
        before = jnp.where(first_col, 0.0, pltpu.roll(odd, 1, 1))
        after = jnp.where(last_col, 0.0, pltpu.roll(even, lanes - 1, 1))
        return before, even, odd, after

    def gate_own(i):
        row = band * 2 + i - 1
        keep = keep_col & ((row >= 0) & (row < 2 * lane_rows))
        for at, plane in enumerate(gate(t_own[i // 2], m_own[(i + 1) // 2], keep)):
            g_own[i, at] = plane.astype(BF)
        even, odd = g_own[i, 1], g_own[i, 2]
        g_pack[i] = jnp.where(early < split, pltpu.roll(even, lanes - split, 1), odd)

    def swap(plane):
        return jnp.where(early < split, pltpu.roll(plane, lanes - split, 1), pltpu.roll(plane, split, 1))

    def old_planes(i):
        packed = g_recv[i]
        none = jnp.zeros_like(packed)
        before = jnp.where(first_col, none, pltpu.roll(packed, 1, 1))
        after = jnp.where(last_col, none, pltpu.roll(packed, lanes - 1, 1))
        g_old[0, i] = swap(jnp.where(early < split, packed, before))
        g_old[1, i] = swap(jnp.where(early < split, after, packed))

    cells = 2 * lanes
    place = lax.broadcasted_iota(jnp.int32, (cells, cells), 0)
    taken = lax.broadcasted_iota(jnp.int32, (cells, cells), 1)
    perm = (taken == (place % 2) * lanes + place // 2).astype(BF)

    def later(plane):
        return jnp.where(early < cols, 0.0, pltpu.roll(plane, cols, 1))

    def own_taps(l):
        rhs = jnp.concatenate(
            [
                jnp.concatenate([g_own[2 * l + s + b, PLANES[p][c]] for s in range(2) for p in range(2)], axis=1)
                for b in range(3)
                for c in range(3)
            ],
            axis=0,
        )
        res = jnp.dot(w2t[...], rhs, preferred_element_type=F32)
        for n in range(4):
            by_tap = [res[a * outs : (a + 1) * outs, n * lanes : (n + 1) * lanes] for a in range(3)]
            totals[l, n] = by_tap[2] + later(by_tap[1] + later(by_tap[0]))

    def old_taps(ls):
        def plane(i, c):
            return g_recv[i] if c == 1 else g_old[c // 2, i]

        rhs = jnp.concatenate(
            [
                jnp.concatenate([plane(2 * l + s + b, c) for l in ls for s in range(2)], axis=1)
                for b in range(3)
                for c in range(3)
            ],
            axis=0,
        )
        res = jnp.dot(w2t[: 2 * outs], rhs, preferred_element_type=F32)
        added = {}
        for n in range(2 * len(ls)):
            oldest, newer = [res[a * outs : (a + 1) * outs, n * lanes : (n + 1) * lanes] for a in range(2)]
            both_taps = oldest + jnp.where(early % split < cols, pltpu.roll(newer, lanes - cols, 1), 0.0)
            for p, part in enumerate((both_taps, pltpu.roll(both_taps, lanes - split, 1))):
                added[ls[n // 2], 2 * (n % 2) + p] = jnp.where(early < split, part, 0.0)
        return added

    def finish(l, added):
        residual = short[:, l * lanes : (l + 1) * lanes]
        for s in range(2):
            row = 2 * (band + l) + s
            keep = keep_col & (row < 2 * lane_rows)
            pair = jnp.concatenate(
                [
                    jnp.where(keep, totals[l, 2 * s + p] + residual + added[l, 2 * s + p], 0.0)
                    for p in range(2)
                ],
                axis=1,
            ).astype(BF)
            mixed = nt(perm, pair).astype(BF)
            out_v[:, :, 2 * l + s] = mixed.reshape(videos, frames, 2 * cols, outs)

    def result(l):
        at = pl.ds(2 * l, 2)
        return pltpu.make_async_copy(out_v.at[:, :, at], out_ref.at[:, :, at], out_sem.at[l])

    def leave(l):
        result(l).start()

    own_shared = [(t_own, l) for l in range(1, rows)]
    own_middle = [(m_own, r) for r in range(1, rows + 1)]
    local[4].wait()
    local[5].wait()
    product(both, (2,), own_shared)
    product(mid, (2,), own_middle)
    local[3].wait()
    gain_c[...] = jnp.broadcast_to(0.5 * gain_row[...], (lanes, outs)).T
    short[...] = nt(
        ws[...],
        jnp.concatenate([piece for r in range(rows) for piece in own_cells(2, r + 1)], axis=0),
    )
    local[6].wait()
    step = 3 * 128
    for a in range(3):
        for k in range(0, taps, step):
            size = min(step, taps - k)
            w2t[a * outs : (a + 1) * outs, k : k + size] = w2[a * taps + k : a * taps + k + size].T
    local[7].wait()

    for a, k in ((1, 0), (0, 8)):
        arrive(k)
        for r in range(rows):
            mask_into(prev, r, r + 1, (a,), 0)
        if a == 0:
            start(3)
            start(4)
        product(both, (a,), own_shared, add=True)
        product(mid, (a,), own_middle, add=True)

    center = range(2, 2 * rows)
    for i in center[:4]:
        gate_own(i)
    own_taps(1)
    for i in center[4:]:
        gate_own(i)
    start(5)

    edge_shared, edge_middle = [(t_own, 0), (t_own, rows)], [(m_own, 0), (m_own, ext - 1)]
    arrive(1)
    arrive(2)
    for src, r in ((top, 0), (bot, ext - 1)):
        mask_into(src, None, r, every, old)
    product(both, (2,), edge_shared)
    product(mid, (2,), edge_middle)
    arrive(3)
    arrive(4)
    for psrc, r in ((ptop, 0), (pbot, ext - 1)):
        mask_into(psrc, None, r, range(old), 0)
    product(both, (0, 1), edge_shared, add=True)
    product(mid, (0, 1), edge_middle, add=True)
    edges = (0, 1, 2 * rows, 2 * rows + 1)
    for i in edges:
        gate_own(i)
    own_taps(2)
    start(6)
    start(7)

    arrive(5)
    own_taps(0)
    for i in center:
        old_planes(i)
    own_taps(3)

    arrive(6)
    arrive(7)
    for i in edges:
        old_planes(i)
    added = {**old_taps((1, 2)), **old_taps((0, 3))}
    for l in (1, 2, 0):
        finish(l, added)
    leave(1)
    leave(2)
    leave(0)
    finish(3, added)
    leave(3)
    for l in range(rows):
        result(l).wait()

    for there, copy in sends:

        @pl.when(there)
        def _():
            copy.wait_send()


def shards(tm, height, latents, conv_in, conv_out, shortcut, norm_gain, video_rows, video_cols):
    videos, frames, rows, cols, chans = latents.shape
    outs = conv_in.shape[-1]
    ext = rows + 2
    lanes = videos * frames * cols
    taps = 9 * outs
    depth = 27 * outs
    old = 2
    anywhere = pl.BlockSpec(memory_space=pl.ANY)
    return pl.pallas_call(
        functools.partial(section, tm, height),
        out_shape=jax.ShapeDtypeStruct((videos, frames, 2 * rows, 2 * cols, outs), BF),
        in_specs=[anywhere] * 7,
        out_specs=anywhere,
        scratch_shapes=[
            pltpu.VMEM((videos, frames, rows, cols, chans), BF),
            pltpu.VMEM((videos, old, rows, cols, chans), BF),
            pltpu.VMEM((videos, frames, cols, chans), BF),
            pltpu.VMEM((videos, frames, cols, chans), BF),
            pltpu.VMEM((videos, old, cols, chans), BF),
            pltpu.VMEM((videos, old, cols, chans), BF),
            pltpu.VMEM((3, taps, chans), BF),
            pltpu.VMEM((depth, outs), BF),
            pltpu.VMEM((outs, chans), BF),
            pltpu.VMEM((1, outs), F32),
            pltpu.SMEM((videos,), jnp.int32),
            pltpu.SMEM((videos,), jnp.int32),
            pltpu.VMEM((3 * outs, taps), BF),
            pltpu.VMEM((outs, lanes), F32),
            pltpu.VMEM((ext, videos, (frames + old) * cols, chans), BF),
            pltpu.VMEM((ext - 1, 3 * outs, lanes), F32),
            pltpu.VMEM((ext, 3 * outs, lanes), F32),
            pltpu.VMEM((2 * rows + 2, 4, outs, lanes), BF),
            pltpu.VMEM((2 * rows + 2, outs, lanes), BF),
            pltpu.VMEM((2 * rows + 2, outs, lanes), BF),
            pltpu.VMEM((2, 2 * rows + 2, outs, lanes), BF),
            pltpu.VMEM((rows, 4, outs, lanes), F32),
            pltpu.VMEM((outs, rows * lanes), F32),
            pltpu.VMEM((videos, frames, 2 * rows, 2 * cols, outs), BF),
            pltpu.SemaphoreType.DMA((rows,)),
            pltpu.SemaphoreType.DMA((8,)),
            pltpu.SemaphoreType.DMA((9,)),
            pltpu.SemaphoreType.DMA((9,)),
        ],
        compiler_params=pltpu.CompilerParams(
            collective_id=0, has_side_effects=True, vmem_limit_bytes=56 << 20
        ),
    )(
        latents,
        jnp.swapaxes(conv_in, 3, 4).reshape(3, taps, chans),
        conv_out.reshape(depth, outs),
        shortcut.T,
        norm_gain.reshape(1, outs),
        video_rows,
        video_cols,
    )


def solution(mesh):
    in_specs = (P(None, "tm", "height", None, None), P(), P(), P(), P(), P(), P())
    out_specs = P(None, "tm", "height", None, None)
    return jax.shard_map(
        functools.partial(shards, mesh.shape["tm"], mesh.shape["height"]),
        mesh=mesh,
        in_specs=in_specs,
        out_specs=out_specs,
        check_vma=False,
    )
```
